256 devices in a mesh: req: 32 (over z, x), mdl: 8 (over y, core).
Axes of the slice: x: 4, y: 4, z: 8, core: 2. Of those that a mesh axis runs over, the one named last changes fastest.
Arguments:
- query: bfloat16 [256, 3584], P('req', 'mdl'), may hold values from -16 to 16
- new_key: bfloat16 [256, 3584], P('req', 'mdl'), may hold values from -16 to 16
- new_value: bfloat16 [256, 3584], P('req', 'mdl'), may hold values from -6 to 6
- page_keys: bfloat16 [512, 16, 3584], P('req', None, 'mdl'), may hold values from -6 to 6
- page_values: bfloat16 [512, 16, 3584], P('req', None, 'mdl'), may hold values from -6 to 6
- long_keys: bfloat16 [16384, 3584], P('req', 'mdl'), may hold values from -16 to 16
- long_values: bfloat16 [16384, 3584], P('req', 'mdl'), may hold values from -10 to 10
- cache_lengths: int32 [256], replicated, may hold values from 1 to 16384, as said below
- block_table: int32 [256, 2], P('req'), may hold values from 0 to 511, as said below
- out_weight: bfloat16 [3584, 3584], P('mdl'), may hold values from -0.09375 to 0.09375
- residual: bfloat16 [256, 3584], P('req', 'mdl'), may hold values from -6 to 6
- norm_gain: bfloat16 [3584], replicated, may hold values from 0.25 to 1.75
- x_weight: bfloat16 [3584, 3584], P(None, 'mdl'), may hold values from -0.09375 to 0.09375
- bc_weight: bfloat16 [3584, 128], replicated, may hold values from -0.09375 to 0.09375
- dt_weight: bfloat16 [3584, 56], P(None, 'mdl'), may hold values from -0.09375 to 0.09375
- z_weight: bfloat16 [3584, 3584], P(None, 'mdl'), may hold values from -0.09375 to 0.09375
- dt_bias: float32 [56], P('mdl'), may hold values from -3 to 1
- a_log: float32 [56], P('mdl'), may hold values from 0 to 2.5
- skip_gain: float32 [56], P('mdl'), may hold values from 0.5 to 1.5
- conv_x_weight: bfloat16 [4, 3584], P(None, 'mdl'), may hold values from -3 to 3
- conv_bc_weight: bfloat16 [4, 128], replicated, may hold values from -3 to 3
- conv_x_state: bfloat16 [256, 3, 3584], P('req', None, 'mdl'), may hold values from -6 to 6
- conv_bc_state: bfloat16 [256, 3, 128], P('req'), may hold values from -6 to 6
- ssm_state: float32 [256, 56, 4096], P('req', 'mdl'), may hold values from -6 to 6
- out_gain: bfloat16 [3584], P('mdl'), may hold values from 0.25 to 1.75
Outputs:
- hidden: bfloat16 [256, 3584], P('req', 'mdl')
- mixed: bfloat16 [256, 3584], P('req', 'mdl')
The draws below stay inside these ranges and needn't reach their ends.
Inputs may be any that keep to these rules, and one draw needn't show every extreme that they name: `cache_lengths`: exactly one request has 16384 cached tokens; every other has at most 32, and some request has exactly 32. `block_table`: row r names pages of the block of 16 pages that starts at (r // 8) * 8 * 2; each page is named once in all.
All inputs are finite; a program needn't handle non-finite values.
Results may differ from the reference program's by a relative error of at most 0.023.
Values may be sent and summed in bfloat16 or wider, within the bound.
A program may use at most 64 MiB of HBM per device.

```python
import math
import jax
import jax.numpy as jnp
from jax import lax

MODEL_WIDTH = 3584
ATT_HEADS = 16
HEAD_DIM = 224
MHEADS = 56
MHEAD_DIM = 64
STATE_DIM = 64
KERNEL = 4
PAGE_SIZE = 16
SHORT_MAX = 32
REQ_DEV = 8
LONG_DEV = 512
PAGES_REQ = 2
REQUESTS = 256
LONG_LEN = 16384
PAGES = 512


def draw_cache_lengths(key, part):
    key_base, key_len, key_long, key_full = jax.random.split(key, 4)
    base = jax.random.randint(key_base, (REQUESTS,), 0, 6)
    upper = jnp.minimum(jnp.power(2, base), SHORT_MAX).astype(jnp.int32)
    short = 1 + jax.random.randint(key_len, (REQUESTS,), 0, upper)
    long_row = jax.random.randint(key_long, (), 0, REQUESTS)
    full_row = (long_row + 1 + jax.random.randint(key_full, (), 0, REQUESTS - 1)) % REQUESTS
    rows = jnp.arange(REQUESTS)
    short = jnp.where(rows == full_row, SHORT_MAX, short)
    return jnp.where(rows == long_row, LONG_LEN, short).astype(jnp.int32)


def long_row_of(key):
    key_long = jax.random.fold_in(key, 2)
    return jax.random.randint(key_long, (), 0, REQUESTS)


def draw_block_table(key, part):
    groups = REQUESTS // REQ_DEV
    per_group = REQ_DEV * PAGES_REQ
    scores = jax.random.randint(key, (groups, per_group), 0, 1 << 20) * per_group + jnp.arange(per_group)[None, :]
    order = jnp.argsort(scores, axis=1)
    pages = order + (jnp.arange(groups) * per_group)[:, None]
    return pages.reshape(REQUESTS, PAGES_REQ).astype(jnp.int32)


def query_and_key(key):
    long_row = long_row_of(key)
    key_query, key_key, key_pick, key_strength = jax.random.split(jax.random.fold_in(key, 7), 4)
    columns = ATT_HEADS * HEAD_DIM
    query = jnp.clip(jax.random.normal(key_query, (REQUESTS, columns), jnp.float32), -6.0, 6.0)
    new_key = jnp.clip(jax.random.normal(key_key, (REQUESTS, columns), jnp.float32), -6.0, 6.0)
    rows = jnp.arange(REQUESTS)[:, None]
    chosen = (jax.random.randint(key_pick, (REQUESTS, 1), 0, 4) == 0) & (rows != long_row)
    strength = jnp.where(jax.random.randint(key_strength, (REQUESTS, 1), 0, 2) == 0, 0.5, 0.75)
    level = min(16.0, (400.0 / HEAD_DIM ** 0.5) ** 0.5)
    strong_key = jnp.where(new_key >= 0.0, level, -level)
    new_key = jnp.where(chosen, strong_key, new_key)
    query = jnp.where(chosen, strength * strong_key, query)
    return (query, new_key)


def draw_query(key, part):
    return query_and_key(key)[0].astype(jnp.bfloat16)


def draw_new_key(key, part):
    return query_and_key(key)[1].astype(jnp.bfloat16)


def signs_of(key, shape):
    return 2.0 * jax.random.randint(key, shape, 0, 2).astype(jnp.float32) - 1.0


def long_cache(key):
    long_row = long_row_of(key)
    groups = LONG_LEN // LONG_DEV
    far_block = (long_row // REQ_DEV + groups // 2) % groups
    key_token, key_direction, key_offset, key_knoise, key_vnoise = jax.random.split(jax.random.fold_in(key, 11), 5)
    columns = ATT_HEADS * HEAD_DIM
    token_sign = signs_of(key_token, (LONG_LEN, 1))
    direction = signs_of(key_direction, (1, columns))
    offset = signs_of(key_offset, (1, columns))
    blocks = (jnp.arange(LONG_LEN) // LONG_DEV)[:, None]
    ramp = blocks.astype(jnp.float32) / max(groups - 1, 1)
    key_noise = jnp.clip(jax.random.normal(key_knoise, (LONG_LEN, columns), jnp.float32), -6.0, 6.0)
    value_noise = jnp.clip(jax.random.normal(key_vnoise, (LONG_LEN, columns), jnp.float32), -6.0, 6.0)
    level = 1.0 + 2.0 * ramp
    align = jnp.where(blocks == far_block, 4.0, 2.0)
    keys = 2.0 * key_noise + align * token_sign * direction
    values = value_noise + level * offset + 0.5 * token_sign * offset
    return (keys, values)


def draw_long_keys(key, part):
    return long_cache(key)[0].astype(jnp.bfloat16)


def draw_long_values(key, part):
    return long_cache(key)[1].astype(jnp.bfloat16)


def block_levels(rng, shape, pieces, smallest, largest):
    loudness, own = 1.0, jax.random.fold_in(rng, 6)
    for axis_at, parts in pieces:
        draws = jnp.exp(jax.random.uniform(jax.random.fold_in(own, axis_at), (parts,), jnp.float32, smallest / len(pieces), largest / len(pieces)))
        loudness = loudness * jnp.repeat(draws, shape[axis_at] // parts).reshape([-1 if axis == axis_at else 1 for axis in range(len(shape))])
    return loudness


def noise(rng, shape, spread, reach, cuts=(), held_as=jnp.bfloat16):
    values = jax.random.normal(rng, shape, jnp.float32) * spread
    if len(cuts) > 0:
        values = block_levels(rng, shape, cuts, -0.22, 0.18) * values
    return jnp.clip(values, min=-reach, max=reach).astype(held_as)


def setup_inputs(seed: int = 0) -> dict:
    key_list = jax.random.split(jax.random.key(seed), 26)
    return {
        "query": draw_query(jax.random.fold_in(key_list[25], 71), 0),
        "new_key": draw_new_key(jax.random.fold_in(key_list[25], 71), 0),
        "new_value": noise(key_list[2], (REQUESTS, ATT_HEADS * HEAD_DIM), 1.0, 6.0, ((0, 32), (1, 8))),
        "page_keys": noise(key_list[3], (PAGES, PAGE_SIZE, ATT_HEADS * HEAD_DIM), 1.0, 6.0, ((0, 32), (2, 8))),
        "page_values": noise(key_list[4], (PAGES, PAGE_SIZE, ATT_HEADS * HEAD_DIM), 1.0, 6.0, ((0, 32), (2, 8))),
        "long_keys": draw_long_keys(jax.random.fold_in(key_list[25], 71), 0),
        "long_values": draw_long_values(jax.random.fold_in(key_list[25], 71), 0),
        "cache_lengths": draw_cache_lengths(jax.random.fold_in(key_list[25], 71), 0),
        "block_table": draw_block_table(jax.random.fold_in(key_list[25], 71), 0),
        "out_weight": noise(key_list[9], (ATT_HEADS * HEAD_DIM, MODEL_WIDTH), (ATT_HEADS * HEAD_DIM) ** -0.5, 0.09375, ((0, 8),)),
        "residual": noise(key_list[10], (REQUESTS, MODEL_WIDTH), 1.0, 6.0, ((0, 32), (1, 8))),
        "norm_gain": jnp.clip(1.0 + 0.15 * jax.random.normal(key_list[11], (MODEL_WIDTH,), jnp.float32), 0.25, 1.75).astype(jnp.bfloat16),
        "x_weight": noise(key_list[12], (MODEL_WIDTH, MHEADS * MHEAD_DIM), MODEL_WIDTH ** -0.5, 0.09375, ((1, 8),)),
        "bc_weight": noise(key_list[13], (MODEL_WIDTH, 2 * STATE_DIM), MODEL_WIDTH ** -0.5, 0.09375),
        "dt_weight": noise(key_list[14], (MODEL_WIDTH, MHEADS), MODEL_WIDTH ** -0.5, 0.09375, ((1, 8),)),
        "z_weight": noise(key_list[15], (MODEL_WIDTH, MHEADS * MHEAD_DIM), MODEL_WIDTH ** -0.5, 0.09375, ((1, 8),)),
        "dt_bias": jnp.clip(-3.0 + 4.0 * jax.random.uniform(key_list[16], (MHEADS,), jnp.float32) ** block_levels(key_list[16], (MHEADS,), ((0, 8),), -0.2, 0.2), -3.0, 1.0),
        "a_log": jnp.clip(2.5 * jax.random.uniform(key_list[17], (MHEADS,), jnp.float32) ** block_levels(key_list[17], (MHEADS,), ((0, 8),), -0.2, 0.2), 0.0, 2.5),
        "skip_gain": jnp.clip(0.5 + 1.0 * jax.random.uniform(key_list[18], (MHEADS,), jnp.float32) ** block_levels(key_list[18], (MHEADS,), ((0, 8),), -0.2, 0.2), 0.5, 1.5),
        "conv_x_weight": noise(key_list[19], (KERNEL, MHEADS * MHEAD_DIM), 0.5, 3.0, ((1, 8),)),
        "conv_bc_weight": noise(key_list[20], (KERNEL, 2 * STATE_DIM), 0.5, 3.0),
        "conv_x_state": noise(key_list[21], (REQUESTS, KERNEL - 1, MHEADS * MHEAD_DIM), 1.0, 6.0, ((0, 32), (2, 8))),
        "conv_bc_state": noise(key_list[22], (REQUESTS, KERNEL - 1, 2 * STATE_DIM), 1.0, 6.0, ((0, 32),)),
        "ssm_state": noise(key_list[23], (REQUESTS, MHEADS, MHEAD_DIM * STATE_DIM), 1.0, 6.0, ((0, 32), (1, 8)), jnp.float32),
        "out_gain": jnp.clip(1.0 + 0.15 * jax.random.normal(key_list[24], (MHEADS * MHEAD_DIM,), jnp.float32), 0.25, 1.75).astype(jnp.bfloat16),
    }


def rounded(values):
    return lax.optimization_barrier(values.astype(jnp.bfloat16)).astype(jnp.float32)

def reference(query, new_key, new_value, page_keys, page_values, long_keys, long_values, cache_lengths, block_table, out_weight, residual, norm_gain, x_weight, bc_weight, dt_weight, z_weight, dt_bias, a_log, skip_gain, conv_x_weight, conv_bc_weight, conv_x_state, conv_bc_state, ssm_state, out_gain):
    scale = 1.0 / math.sqrt(HEAD_DIM)
    shape_heads = (REQUESTS, ATT_HEADS, HEAD_DIM)
    heads_q = query.astype(jnp.float32).reshape(shape_heads)
    heads_k = new_key.astype(jnp.float32).reshape(shape_heads)
    heads_v = new_value.astype(jnp.float32).reshape(shape_heads)
    cached_k = page_keys[block_table].astype(jnp.float32).reshape(REQUESTS, SHORT_MAX, ATT_HEADS, HEAD_DIM)
    cached_v = page_values[block_table].astype(jnp.float32).reshape(REQUESTS, SHORT_MAX, ATT_HEADS, HEAD_DIM)
    places = jnp.arange(SHORT_MAX, dtype=jnp.int32)
    usable = (places[None, :] < cache_lengths[:, None]) & (cache_lengths[:, None] <= SHORT_MAX)
    short_scores = jnp.einsum('rhd,rthd->rht', heads_q, cached_k) * scale
    short_scores = jnp.where(usable[:, None, :], short_scores, -jnp.inf)
    own_scores = lax.optimization_barrier(jnp.sum(heads_q * heads_k, axis=-1)) * scale
    row_max = jnp.maximum(lax.optimization_barrier(jnp.max(short_scores, axis=-1)), own_scores)
    long_row = jnp.argmax(cache_lengths).astype(jnp.int32)
    long_query = heads_q[long_row]
    long_k = long_keys.astype(jnp.float32).reshape(LONG_LEN, ATT_HEADS, HEAD_DIM)
    long_v = long_values.astype(jnp.float32).reshape(LONG_LEN, ATT_HEADS, HEAD_DIM)
    long_scores = jnp.einsum('hd,thd->ht', long_query, long_k) * scale
    rows = jnp.arange(REQUESTS, dtype=jnp.int32)
    is_long = (rows == long_row)[:, None]
    row_max = jnp.where(is_long, jnp.maximum(row_max, lax.optimization_barrier(jnp.max(long_scores, axis=-1))[None, :]), row_max)
    short_w = jnp.exp(short_scores - row_max[:, :, None])
    own_w = jnp.exp(own_scores - row_max)
    long_w = jnp.exp(long_scores - row_max[long_row][:, None])
    total = lax.optimization_barrier(jnp.sum(short_w, axis=-1)) + own_w
    total = total + jnp.where(is_long, lax.optimization_barrier(jnp.sum(long_w, axis=-1))[None, :], 0.0)
    numer = jnp.einsum('rht,rthd->rhd', rounded(short_w), cached_v) + rounded(own_w)[..., None] * heads_v
    long_numer = jnp.einsum('ht,thd->hd', rounded(long_w), long_v)
    numer = numer + jnp.where(is_long[:, :, None], long_numer[None], 0.0)
    attended = (numer / total[..., None]).astype(jnp.bfloat16).reshape(REQUESTS, ATT_HEADS * HEAD_DIM)
    projected = jnp.dot(attended, out_weight, preferred_element_type=jnp.float32)
    hidden = (residual.astype(jnp.float32) + projected).astype(jnp.bfloat16)
    hidden_f = hidden.astype(jnp.float32)
    inverse = lax.rsqrt(lax.optimization_barrier(jnp.mean(hidden_f * hidden_f, axis=-1, keepdims=True)) + 1e-05)
    normed = (hidden_f * inverse * norm_gain.astype(jnp.float32)).astype(jnp.bfloat16)
    x_in = jnp.dot(normed, x_weight, preferred_element_type=jnp.float32)
    bc_in = jnp.dot(normed, bc_weight, preferred_element_type=jnp.float32)
    dt_in = jnp.dot(normed, dt_weight, preferred_element_type=jnp.float32)
    z_in = jnp.dot(normed, z_weight, preferred_element_type=jnp.float32)
    window_x = jnp.concatenate([conv_x_state.astype(jnp.float32), x_in[:, None, :]], axis=1)
    x_conv = jax.nn.silu(lax.optimization_barrier(jnp.sum(window_x * conv_x_weight.astype(jnp.float32)[None], axis=1)))
    window_bc = jnp.concatenate([conv_bc_state.astype(jnp.float32), bc_in[:, None, :]], axis=1)
    bc_conv = jax.nn.silu(lax.optimization_barrier(jnp.sum(window_bc * conv_bc_weight.astype(jnp.float32)[None], axis=1)))
    b_part = bc_conv[:, :STATE_DIM]
    c_part = bc_conv[:, STATE_DIM:]
    step = jax.nn.softplus(dt_in + dt_bias[None, :])
    decay = jnp.exp(-jnp.exp(a_log)[None, :] * step)
    x_heads = x_conv.reshape(REQUESTS, MHEADS, MHEAD_DIM)
    state = ssm_state.reshape(REQUESTS, MHEADS, MHEAD_DIM, STATE_DIM)
    state_new = decay[:, :, None, None] * state + (step[:, :, None] * x_heads)[..., None] * b_part[:, None, None, :]
    y_heads = lax.optimization_barrier(jnp.sum(state_new * c_part[:, None, None, :], axis=-1)) + skip_gain[None, :, None] * x_heads
    y_flat = y_heads.reshape(REQUESTS, MHEADS * MHEAD_DIM)
    gated = y_flat * jax.nn.silu(z_in)
    y_inverse = lax.rsqrt(lax.optimization_barrier(jnp.mean(gated * gated, axis=-1, keepdims=True)) + 1e-05)
    mixed = (gated * y_inverse * out_gain.astype(jnp.float32)).astype(jnp.bfloat16)
    return (hidden, mixed)
```

```python
import functools
import math

import jax
import jax.numpy as jnp
from jax import lax
from jax.experimental import pallas as pl
from jax.experimental.pallas import tpu as pltpu
from jax.sharding import PartitionSpec as P

MODEL_WIDTH = 3584
HEAD_DIM = 224
MHEADS = 56
MHEAD_DIM = 64
STATE_DIM = 64
SHORT_MAX = 32
PAGE_SIZE = 16

MESH_ID = pl.DeviceIdType.MESH


def exchange_kernel(n, axis, rows, x_ref, out_ref, land, send_sems, recv_sems):
    me = lax.axis_index(axis)
    barrier = pltpu.get_barrier_semaphore()
    for j in range(1, n):
        peer = lax.rem(me + j, n)
        pl.semaphore_signal(barrier, inc=1, device_id={axis: peer}, device_id_type=MESH_ID)
    pl.semaphore_wait(barrier, n - 1)
    if rows:
        slot = land.at[pl.ds(me, 1)]
    else:
        slot = land.at[me]
    copies = []
    for j in range(1, n):
        peer = lax.rem(me + j, n)
        copy = pltpu.make_async_remote_copy(
            src_ref=x_ref,
            dst_ref=slot,
            send_sem=send_sems.at[j - 1],
            recv_sem=recv_sems.at[j - 1],
            device_id={axis: peer},
            device_id_type=MESH_ID,
        )
        copy.start()
        copies.append(copy)
    for copy in copies:
        copy.wait()
    if rows:
        land[pl.ds(me, 1), :] = x_ref[...]
    else:
        land[me] = x_ref[...]
    out_ref[...] = land[...]


def exchange(x, axis, n, cid):
    rows = x.ndim == 2 and x.shape[0] == 1
    land_shape = (n, x.shape[1]) if rows else (n,) + x.shape
    return pl.pallas_call(
        functools.partial(exchange_kernel, n, axis, rows),
        out_shape=jax.ShapeDtypeStruct(land_shape, x.dtype),
        in_specs=[pl.BlockSpec(memory_space=pltpu.VMEM)],
        out_specs=pl.BlockSpec(memory_space=pltpu.VMEM),
        scratch_shapes=[
            pltpu.VMEM(land_shape, x.dtype),
            pltpu.SemaphoreType.DMA((n - 1,)),
            pltpu.SemaphoreType.DMA((n - 1,)),
        ],
        compiler_params=pltpu.CompilerParams(collective_id=cid, has_side_effects=True),
    )(x)


def shards(
    n_req,
    n_mdl,
    query,
    new_key,
    new_value,
    page_keys,
    page_values,
    long_keys,
    long_values,
    cache_lengths,
    block_table,
    out_weight,
    residual,
    norm_gain,
    x_weight,
    bc_weight,
    dt_weight,
    z_weight,
    dt_bias,
    a_log,
    skip_gain,
    conv_x_weight,
    conv_bc_weight,
    conv_x_state,
    conv_bc_state,
    ssm_state,
    out_gain,
):
    req_count = query.shape[0]
    local_cols = query.shape[1]
    heads_here = local_cols // HEAD_DIM
    scale = 1.0 / math.sqrt(HEAD_DIM)
    device = lax.axis_index("req")
    pages_here = page_keys.shape[0]
    long_row = jnp.argmax(cache_lengths)
    owner = long_row // req_count
    long_local = long_row % req_count

    own_query = lax.dynamic_slice_in_dim(query, long_local, 1, 0).astype(jnp.float32)
    queries = exchange(own_query, "req", n_req, 0)
    long_query = lax.dynamic_index_in_dim(queries, owner, 0, keepdims=False)
    long_query = long_query.astype(jnp.bfloat16).reshape(heads_here, HEAD_DIM)

    long_k = long_keys.reshape(long_keys.shape[0], heads_here, HEAD_DIM)
    long_v = long_values.reshape(long_values.shape[0], heads_here, HEAD_DIM)
    long_scores = (
        jnp.einsum("hd,thd->ht", long_query, long_k, preferred_element_type=jnp.float32) * scale
    )
    long_max = jnp.max(long_scores, axis=-1)
    long_w = jnp.exp(long_scores - long_max[:, None])
    long_total = jnp.sum(long_w, axis=-1)
    long_sums = jnp.einsum(
        "ht,thd->hd", long_w.astype(jnp.bfloat16), long_v, preferred_element_type=jnp.float32
    )
    part_width = heads_here * HEAD_DIM + 2 * heads_here
    part_pad = (-part_width) % 128
    packed = jnp.concatenate(
        [long_sums.reshape(-1), long_max, long_total, jnp.zeros((part_pad,), jnp.float32)]
    )[None, :]

    my_lengths = lax.dynamic_slice_in_dim(cache_lengths, device * req_count, req_count)
    local_pages = block_table - device * pages_here
    heads_q = query.reshape(req_count, heads_here, HEAD_DIM)
    heads_k = new_key.reshape(req_count, heads_here, HEAD_DIM)
    heads_v = new_value.reshape(req_count, heads_here, HEAD_DIM)
    tokens_here = pages_here * PAGE_SIZE
    all_k = page_keys.reshape(tokens_here, heads_here, HEAD_DIM)
    all_v = page_values.reshape(tokens_here, heads_here, HEAD_DIM)
    token_page = jnp.arange(tokens_here, dtype=jnp.int32) // PAGE_SIZE
    token_slot = jnp.arange(tokens_here, dtype=jnp.int32) % PAGE_SIZE
    place = jnp.full((req_count, tokens_here), SHORT_MAX, jnp.int32)
    for i in range(local_pages.shape[1]):
        hit = local_pages[:, i : i + 1] == token_page[None, :]
        place = jnp.where(hit, i * PAGE_SIZE + token_slot[None, :], place)
    usable = (place < my_lengths[:, None]) & (my_lengths[:, None] <= SHORT_MAX)
    short_scores = (
        jnp.einsum("rhd,thd->rht", heads_q, all_k, preferred_element_type=jnp.float32) * scale
    )
    short_scores = jnp.where(usable[:, None, :], short_scores, -jnp.inf)
    own_scores = (
        jnp.einsum("rhd,rhd->rh", heads_q, heads_k, preferred_element_type=jnp.float32) * scale
    )
    local_max = jnp.maximum(jnp.max(short_scores, axis=-1), own_scores)
    short_w = jnp.exp(short_scores - local_max[:, :, None])
    own_w = jnp.exp(own_scores - local_max)
    totals = jnp.sum(short_w, axis=-1) + own_w
    numer = jnp.einsum(
        "rht,thd->rhd", short_w.astype(jnp.bfloat16), all_v, preferred_element_type=jnp.float32
    )
    numer = numer + own_w.astype(jnp.bfloat16).astype(jnp.float32)[..., None] * heads_v.astype(
        jnp.float32
    )

    parts = exchange(packed, "req", n_req, 1)
    sums_all = parts[:, : heads_here * HEAD_DIM].reshape(n_req, heads_here, HEAD_DIM)
    max_all = parts[:, heads_here * HEAD_DIM : heads_here * HEAD_DIM + heads_here]
    total_all = parts[:, heads_here * HEAD_DIM + heads_here : part_width]
    whole_max = jnp.max(max_all, axis=0)
    keep = jnp.exp(max_all - whole_max[None, :])
    whole_total = jnp.sum(total_all * keep, axis=0)
    whole_sums = jnp.sum(sums_all * keep[:, :, None], axis=0)

    chosen = (jnp.arange(req_count, dtype=jnp.int32) == long_local) & (device == owner)
    top = jnp.where(chosen[:, None], jnp.maximum(local_max, whole_max[None, :]), local_max)
    keep_local = jnp.exp(local_max - top)
    keep_long = jnp.exp(jnp.where(chosen[:, None], whole_max[None, :] - top, -jnp.inf))
    totals = totals * keep_local + keep_long * whole_total[None, :]
    numer = numer * keep_local[..., None] + keep_long[..., None] * whole_sums[None]
    attended = (numer / totals[..., None]).astype(jnp.bfloat16).reshape(req_count, local_cols)

    projected = jnp.dot(attended, out_weight, preferred_element_type=jnp.float32)
    feature_cols = residual.shape[1]
    feature_start = lax.axis_index("mdl") * feature_cols
    residual_all = lax.all_gather(residual, "mdl", axis=1, tiled=True)
    partials = exchange(projected.astype(jnp.bfloat16), "mdl", n_mdl, 2)
    summed = jnp.sum(partials.astype(jnp.float32), axis=0)
    hidden_all = (residual_all.astype(jnp.float32) + summed).astype(jnp.bfloat16)
    hidden = lax.dynamic_slice_in_dim(hidden_all, feature_start, feature_cols, 1)
    hidden_f = hidden_all.astype(jnp.float32)
    squares = jnp.sum(hidden_f * hidden_f, axis=-1)
    inverse = lax.rsqrt(squares / MODEL_WIDTH + 1e-05)
    normed = (hidden_f * inverse[:, None] * norm_gain.astype(jnp.float32)[None, :]).astype(
        jnp.bfloat16
    )

    x_in = jnp.dot(normed, x_weight, preferred_element_type=jnp.float32)
    bc_in = jnp.dot(normed, bc_weight, preferred_element_type=jnp.float32)
    dt_in = jnp.dot(normed, dt_weight, preferred_element_type=jnp.float32)
    z_in = jnp.dot(normed, z_weight, preferred_element_type=jnp.float32)
    window_x = jnp.concatenate([conv_x_state.astype(jnp.float32), x_in[:, None, :]], axis=1)
    x_conv = jax.nn.silu(jnp.sum(window_x * conv_x_weight.astype(jnp.float32)[None], axis=1))
    window_bc = jnp.concatenate([conv_bc_state.astype(jnp.float32), bc_in[:, None, :]], axis=1)
    bc_conv = jax.nn.silu(jnp.sum(window_bc * conv_bc_weight.astype(jnp.float32)[None], axis=1))
    b_part = bc_conv[:, :STATE_DIM]
    c_part = bc_conv[:, STATE_DIM:]
    mamba_heads = dt_bias.shape[0]
    step = jax.nn.softplus(dt_in + dt_bias[None, :])
    decay = jnp.exp(-jnp.exp(a_log)[None, :] * step)
    x_heads = x_conv.reshape(req_count, mamba_heads, MHEAD_DIM)
    state = ssm_state.reshape(req_count, mamba_heads, MHEAD_DIM, STATE_DIM)
    state_new = (
        decay[:, :, None, None] * state
        + (step[:, :, None] * x_heads)[..., None] * b_part[:, None, None, :]
    )
    y_heads = (
        jnp.sum(state_new * c_part[:, None, None, :], axis=-1) + skip_gain[None, :, None] * x_heads
    )
    y_flat = y_heads.reshape(req_count, mamba_heads * MHEAD_DIM)
    gated = y_flat * jax.nn.silu(z_in)
    y_part = jnp.sum(gated * gated, axis=-1)
    y_pad = (-req_count) % 128
    y_msg = jnp.concatenate([y_part, jnp.zeros((y_pad,), jnp.float32)])[None, :]
    y_all = exchange(y_msg, "mdl", n_mdl, 3)
    y_squares = jnp.sum(y_all[:, :req_count], axis=0)
    y_inverse = lax.rsqrt(y_squares / (MHEADS * MHEAD_DIM) + 1e-05)
    mixed = (gated * y_inverse[:, None] * out_gain.astype(jnp.float32)[None, :]).astype(
        jnp.bfloat16
    )
    return (hidden, mixed)


def solution(mesh):
    return jax.shard_map(
        functools.partial(shards, mesh.shape["req"], mesh.shape["mdl"]),
        mesh=mesh,
        in_specs=(
            P("req", "mdl"),
            P("req", "mdl"),
            P("req", "mdl"),
            P("req", None, "mdl"),
            P("req", None, "mdl"),
            P("req", "mdl"),
            P("req", "mdl"),
            P(),
            P("req", None),
            P("mdl", None),
            P("req", "mdl"),
            P(),
            P(None, "mdl"),
            P(),
            P(None, "mdl"),
            P(None, "mdl"),
            P("mdl"),
            P("mdl"),
            P("mdl"),
            P(None, "mdl"),
            P(),
            P("req", None, "mdl"),
            P("req", None, None),
            P("req", "mdl", None),
            P("mdl"),
        ),
        out_specs=(P("req", "mdl"), P("req", "mdl")),
        check_vma=False,
    )
```

```python
import functools
import math

import jax
import jax.numpy as jnp
from jax import lax
from jax.experimental import pallas as pl
from jax.experimental.pallas import tpu as pltpu
from jax.sharding import PartitionSpec as P

MODEL_WIDTH = 3584
HEAD_DIM = 224
MHEADS = 56
MHEAD_DIM = 64
STATE_DIM = 64
SHORT_MAX = 32
PAGE_SIZE = 16

MESH_ID = pl.DeviceIdType.MESH


def exchange_kernel(n, axis, count, *refs):
    x_refs = refs[:count]
    out_refs = refs[count : 2 * count]
    lands = refs[2 * count : 3 * count]
    send_sems, recv_sems = refs[3 * count :]
    me = lax.axis_index(axis)
    barrier = pltpu.get_barrier_semaphore()
    for j in range(1, n):
        peer = lax.rem(me + j, n)
        pl.semaphore_signal(barrier, inc=1, device_id={axis: peer}, device_id_type=MESH_ID)
    pl.semaphore_wait(barrier, n - 1)
    copies = []
    for k in range(count):
        rows = len(x_refs[k].shape) == 2 and x_refs[k].shape[0] == 1
        slot = lands[k].at[pl.ds(me, 1)] if rows else lands[k].at[me]
        for j in range(1, n):
            peer = lax.rem(me + j, n)
            copy = pltpu.make_async_remote_copy(
                src_ref=x_refs[k],
                dst_ref=slot,
                send_sem=send_sems.at[k, j - 1],
                recv_sem=recv_sems.at[k, j - 1],
                device_id={axis: peer},
                device_id_type=MESH_ID,
            )
            copy.start()
            copies.append(copy)
    for copy in copies:
        copy.wait()
    for k in range(count):
        rows = len(x_refs[k].shape) == 2 and x_refs[k].shape[0] == 1
        if rows:
            lands[k][pl.ds(me, 1), :] = x_refs[k][...]
        else:
            lands[k][me] = x_refs[k][...]
        out_refs[k][...] = lands[k][...]


def exchange(xs, axis, n, cid):
    shapes = []
    for x in xs:
        rows = x.ndim == 2 and x.shape[0] == 1
        shapes.append(jax.ShapeDtypeStruct((n, x.shape[1]) if rows else (n,) + x.shape, x.dtype))
    count = len(xs)
    return pl.pallas_call(
        functools.partial(exchange_kernel, n, axis, count),
        out_shape=tuple(shapes),
        in_specs=[pl.BlockSpec(memory_space=pltpu.VMEM)] * count,
        out_specs=tuple([pl.BlockSpec(memory_space=pltpu.VMEM)] * count),
        scratch_shapes=[pltpu.VMEM(s.shape, s.dtype) for s in shapes]
        + [pltpu.SemaphoreType.DMA((count, n - 1)), pltpu.SemaphoreType.DMA((count, n - 1))],
        compiler_params=pltpu.CompilerParams(collective_id=cid, has_side_effects=True),
    )(*xs)


def by_head(values, head_mask):
    out = jnp.zeros(values.shape[:-1] + (head_mask.shape[1],), values.dtype)
    for h in range(head_mask.shape[0]):
        out = jnp.where(head_mask[h], values[..., h : h + 1], out)
    return out


def pick_head(values, head_mask):
    out = values[..., 0, :]
    for h in range(1, head_mask.shape[0]):
        out = jnp.where(head_mask[h], values[..., h, :], out)
    return out


def shards(
    n_req,
    n_mdl,
    query,
    new_key,
    new_value,
    page_keys,
    page_values,
    long_keys,
    long_values,
    cache_lengths,
    block_table,
    out_weight,
    residual,
    norm_gain,
    x_weight,
    bc_weight,
    dt_weight,
    z_weight,
    dt_bias,
    a_log,
    skip_gain,
    conv_x_weight,
    conv_bc_weight,
    conv_x_state,
    conv_bc_state,
    ssm_state,
    out_gain,
):
    req_count = query.shape[0]
    local_cols = query.shape[1]
    heads_here = local_cols // HEAD_DIM
    scale = 1.0 / math.sqrt(HEAD_DIM)
    device = lax.axis_index("req")
    pages_here = page_keys.shape[0]
    long_row = jnp.argmax(cache_lengths)
    owner = long_row // req_count
    long_local = long_row % req_count

    head_of_col = jnp.arange(local_cols, dtype=jnp.int32) // HEAD_DIM
    head_mask = head_of_col[None, :] == jnp.arange(heads_here, dtype=jnp.int32)[:, None]

    own_query = lax.dynamic_slice_in_dim(query, long_local, 1, 0).astype(jnp.float32)
    (queries,) = exchange([own_query], "req", n_req, 0)
    long_query = lax.dynamic_index_in_dim(queries, owner, 0, keepdims=True).astype(jnp.bfloat16)
    long_masked = jnp.where(head_mask, long_query, jnp.zeros_like(long_query))
    long_scores = (
        lax.dot_general(
            long_masked, long_keys, (((1,), (1,)), ((), ())), preferred_element_type=jnp.float32
        )
        * scale
    )
    long_max = jnp.max(long_scores, axis=-1)
    long_w = jnp.exp(long_scores - long_max[:, None])
    long_total = jnp.sum(long_w, axis=-1)
    long_sums = pick_head(
        jnp.dot(long_w.astype(jnp.bfloat16), long_values, preferred_element_type=jnp.float32),
        head_mask,
    )
    part_width = local_cols + 2 * heads_here
    part_pad = (-part_width) % 128
    packed = jnp.concatenate(
        [long_sums, long_max, long_total, jnp.zeros((part_pad,), jnp.float32)]
    )[None, :]

    my_lengths = lax.dynamic_slice_in_dim(cache_lengths, device * req_count, req_count)
    local_pages = block_table - device * pages_here
    tokens_here = pages_here * PAGE_SIZE
    all_k = page_keys.reshape(tokens_here, local_cols)
    all_v = page_values.reshape(tokens_here, local_cols)
    token_page = jnp.arange(tokens_here, dtype=jnp.int32) // PAGE_SIZE
    token_slot = jnp.arange(tokens_here, dtype=jnp.int32) % PAGE_SIZE
    place = jnp.full((req_count, tokens_here), SHORT_MAX, jnp.int32)
    for i in range(local_pages.shape[1]):
        hit = local_pages[:, i : i + 1] == token_page[None, :]
        place = jnp.where(hit, i * PAGE_SIZE + token_slot[None, :], place)
    usable = (place < my_lengths[:, None]) & (my_lengths[:, None] <= SHORT_MAX)
    masked_q = jnp.where(head_mask[None], query[:, None, :], jnp.zeros_like(query)[:, None, :])
    short_scores = (
        lax.dot_general(
            masked_q.reshape(req_count * heads_here, local_cols),
            all_k,
            (((1,), (1,)), ((), ())),
            preferred_element_type=jnp.float32,
        ).reshape(req_count, heads_here, tokens_here)
        * scale
    )
    short_scores = jnp.where(usable[:, None, :], short_scores, -jnp.inf)
    own_scores = (
        jnp.sum(
            jnp.where(
                head_mask[None],
                (query.astype(jnp.float32) * new_key.astype(jnp.float32))[:, None, :],
                0.0,
            ),
            axis=-1,
        )
        * scale
    )
    local_max = jnp.maximum(jnp.max(short_scores, axis=-1), own_scores)
    short_w = jnp.exp(short_scores - local_max[:, :, None])
    own_w = jnp.exp(own_scores - local_max)
    totals = jnp.sum(short_w, axis=-1) + own_w
    numer = pick_head(
        jnp.dot(
            short_w.astype(jnp.bfloat16).reshape(req_count * heads_here, tokens_here),
            all_v,
            preferred_element_type=jnp.float32,
        ).reshape(req_count, heads_here, local_cols),
        head_mask,
    )
    own_cols = by_head(own_w.astype(jnp.bfloat16).astype(jnp.float32), head_mask)
    numer = numer + own_cols * new_value.astype(jnp.float32)

    (parts,) = exchange([packed], "req", n_req, 1)
    sums_all = parts[:, :local_cols]
    max_all = parts[:, local_cols : local_cols + heads_here]
    total_all = parts[:, local_cols + heads_here : part_width]
    whole_max = jnp.max(max_all, axis=0)
    keep = jnp.exp(max_all - whole_max[None, :])
    whole_total = jnp.sum(total_all * keep, axis=0)
    whole_sums = jnp.sum(sums_all * by_head(keep, head_mask), axis=0)

    chosen = (jnp.arange(req_count, dtype=jnp.int32) == long_local) & (device == owner)
    top = jnp.where(chosen[:, None], jnp.maximum(local_max, whole_max[None, :]), local_max)
    keep_local = jnp.exp(local_max - top)
    keep_long = jnp.exp(jnp.where(chosen[:, None], whole_max[None, :] - top, -jnp.inf))
    totals = totals * keep_local + keep_long * whole_total[None, :]
    numer = numer * by_head(keep_local, head_mask) + by_head(keep_long, head_mask) * whole_sums[None]
    attended = (numer / by_head(totals, head_mask)).astype(jnp.bfloat16)

    projected = jnp.dot(attended, out_weight, preferred_element_type=jnp.float32)
    feature_cols = residual.shape[1]
    feature_start = lax.axis_index("mdl") * feature_cols
    partials, residuals = exchange([projected.astype(jnp.bfloat16), residual], "mdl", n_mdl, 2)
    residual_all = jnp.transpose(residuals, (1, 0, 2)).reshape(req_count, n_mdl * feature_cols)
    summed = jnp.sum(partials.astype(jnp.float32), axis=0)
    hidden_all = (residual_all.astype(jnp.float32) + summed).astype(jnp.bfloat16)
    hidden = lax.dynamic_slice_in_dim(hidden_all, feature_start, feature_cols, 1)
    hidden_f = hidden_all.astype(jnp.float32)
    squares = jnp.sum(hidden_f * hidden_f, axis=-1)
    inverse = lax.rsqrt(squares / MODEL_WIDTH + 1e-05)
    normed = (hidden_f * inverse[:, None] * norm_gain.astype(jnp.float32)[None, :]).astype(
        jnp.bfloat16
    )

    x_in = jnp.dot(normed, x_weight, preferred_element_type=jnp.float32)
    bc_in = jnp.dot(normed, bc_weight, preferred_element_type=jnp.float32)
    dt_in = jnp.dot(normed, dt_weight, preferred_element_type=jnp.float32)
    z_in = jnp.dot(normed, z_weight, preferred_element_type=jnp.float32)
    window_x = jnp.concatenate([conv_x_state.astype(jnp.float32), x_in[:, None, :]], axis=1)
    x_conv = jax.nn.silu(jnp.sum(window_x * conv_x_weight.astype(jnp.float32)[None], axis=1))
    window_bc = jnp.concatenate([conv_bc_state.astype(jnp.float32), bc_in[:, None, :]], axis=1)
    bc_conv = jax.nn.silu(jnp.sum(window_bc * conv_bc_weight.astype(jnp.float32)[None], axis=1))
    b_part = bc_conv[:, :STATE_DIM]
    c_part = bc_conv[:, STATE_DIM:]
    mamba_heads = dt_bias.shape[0]
    step = jax.nn.softplus(dt_in + dt_bias[None, :])
    decay = jnp.exp(-jnp.exp(a_log)[None, :] * step)
    x_heads = x_conv.reshape(req_count, mamba_heads, MHEAD_DIM)
    state = ssm_state.reshape(req_count, mamba_heads, MHEAD_DIM, STATE_DIM)
    state_new = (
        decay[:, :, None, None] * state
        + (step[:, :, None] * x_heads)[..., None] * b_part[:, None, None, :]
    )
    y_heads = (
        jnp.sum(state_new * c_part[:, None, None, :], axis=-1) + skip_gain[None, :, None] * x_heads
    )
    y_flat = y_heads.reshape(req_count, mamba_heads * MHEAD_DIM)
    gated = y_flat * jax.nn.silu(z_in)
    y_part = jnp.sum(gated * gated, axis=-1)
    y_pad = (-req_count) % 128
    y_msg = jnp.concatenate([y_part, jnp.zeros((y_pad,), jnp.float32)])[None, :]
    (y_all,) = exchange([y_msg], "mdl", n_mdl, 3)
    y_squares = jnp.sum(y_all[:, :req_count], axis=0)
    y_inverse = lax.rsqrt(y_squares / (MHEADS * MHEAD_DIM) + 1e-05)
    mixed = (gated * y_inverse[:, None] * out_gain.astype(jnp.float32)[None, :]).astype(
        jnp.bfloat16
    )
    return (hidden, mixed)


def solution(mesh):
    return jax.shard_map(
        functools.partial(shards, mesh.shape["req"], mesh.shape["mdl"]),
        mesh=mesh,
        in_specs=(
            P("req", "mdl"),
            P("req", "mdl"),
            P("req", "mdl"),
            P("req", None, "mdl"),
            P("req", None, "mdl"),
            P("req", "mdl"),
            P("req", "mdl"),
            P(),
            P("req", None),
            P("mdl", None),
            P("req", "mdl"),
            P(),
            P(None, "mdl"),
            P(),
            P(None, "mdl"),
            P(None, "mdl"),
            P("mdl"),
            P("mdl"),
            P("mdl"),
            P(None, "mdl"),
            P(),
            P("req", None, "mdl"),
            P("req", None, None),
            P("req", "mdl", None),
            P("mdl"),
        ),
        out_specs=(P("req", "mdl"), P("req", "mdl")),
        check_vma=False,
    )
```

```python
import functools
import math

import jax
import jax.numpy as jnp
from jax import lax
from jax.experimental import pallas as pl
from jax.experimental.pallas import tpu as pltpu
from jax.sharding import PartitionSpec as P

MODEL_WIDTH = 3584
HEAD_DIM = 224
MHEADS = 56
MHEAD_DIM = 64
STATE_DIM = 64
SHORT_MAX = 32
PAGE_SIZE = 16

MESH_ID = pl.DeviceIdType.MESH


def exchange_kernel(n, axis, count, *refs):
    x_refs = refs[:count]
    out_refs = refs[count : 2 * count]
    lands = refs[2 * count : 3 * count]
    send_sems, recv_sems = refs[3 * count :]
    me = lax.axis_index(axis)
    barrier = pltpu.get_barrier_semaphore()
    for j in range(1, n):
        peer = lax.rem(me + j, n)
        pl.semaphore_signal(barrier, inc=1, device_id={axis: peer}, device_id_type=MESH_ID)
    pl.semaphore_wait(barrier, n - 1)
    copies = []
    for k in range(count):
        rows = len(x_refs[k].shape) == 2 and x_refs[k].shape[0] == 1
        slot = lands[k].at[pl.ds(me, 1)] if rows else lands[k].at[me]
        for j in range(1, n):
            peer = lax.rem(me + j, n)
            copy = pltpu.make_async_remote_copy(
                src_ref=x_refs[k],
                dst_ref=slot,
                send_sem=send_sems.at[k, j - 1],
                recv_sem=recv_sems.at[k, j - 1],
                device_id={axis: peer},
                device_id_type=MESH_ID,
            )
            copy.start()
            copies.append(copy)
    for copy in copies:
        copy.wait()
    for k in range(count):
        rows = len(x_refs[k].shape) == 2 and x_refs[k].shape[0] == 1
        if rows:
            lands[k][pl.ds(me, 1), :] = x_refs[k][...]
        else:
            lands[k][me] = x_refs[k][...]
        out_refs[k][...] = lands[k][...]


def exchange(xs, axis, n, cid):
    shapes = []
    for x in xs:
        rows = x.ndim == 2 and x.shape[0] == 1
        shapes.append(jax.ShapeDtypeStruct((n, x.shape[1]) if rows else (n,) + x.shape, x.dtype))
    count = len(xs)
    return pl.pallas_call(
        functools.partial(exchange_kernel, n, axis, count),
        out_shape=tuple(shapes),
        in_specs=[pl.BlockSpec(memory_space=pltpu.VMEM)] * count,
        out_specs=tuple([pl.BlockSpec(memory_space=pltpu.VMEM)] * count),
        scratch_shapes=[pltpu.VMEM(s.shape, s.dtype) for s in shapes]
        + [pltpu.SemaphoreType.DMA((count, n - 1)), pltpu.SemaphoreType.DMA((count, n - 1))],
        compiler_params=pltpu.CompilerParams(collective_id=cid, has_side_effects=True),
    )(*xs)


def by_head(values, head_mask):
    out = jnp.zeros(values.shape[:-1] + (head_mask.shape[1],), values.dtype)
    for h in range(head_mask.shape[0]):
        out = jnp.where(head_mask[h], values[..., h : h + 1], out)
    return out


def pick_head(values, head_mask):
    out = values[..., 0, :]
    for h in range(1, head_mask.shape[0]):
        out = jnp.where(head_mask[h], values[..., h, :], out)
    return out


def attention_kernel(n, scale, info_ref, q_ref, k_ref, v_ref, pk_ref, pv_ref, lk_ref, lv_ref,
                     out_ref, qsend, qland, psend, pland, send_sems, recv_sems):
    me = lax.axis_index("req")
    rows, cols = q_ref.shape
    tokens = pk_ref.shape[0]
    long_tokens = lk_ref.shape[0]
    barrier = pltpu.get_barrier_semaphore()
    for j in range(1, n):
        pl.semaphore_signal(barrier, inc=1, device_id={"req": lax.rem(me + j, n)}, device_id_type=MESH_ID)

    owner = info_ref[0]
    long_local = info_ref[1]
    lane = lax.broadcasted_iota(jnp.int32, (1, cols), 1)
    hm0 = lane < HEAD_DIM
    row_id = lax.broadcasted_iota(jnp.int32, (rows, 1), 0)
    q = q_ref[...]
    q32 = q.astype(jnp.float32)
    qsend[...] = jnp.sum(jnp.where(row_id == long_local, q32, 0.0), axis=0, keepdims=True)
    pl.semaphore_wait(barrier, n - 1)

    copies = []
    for j in range(1, n):
        copy = pltpu.make_async_remote_copy(
            src_ref=qsend, dst_ref=qland.at[pl.ds(me, 1)], send_sem=send_sems.at[0, j - 1],
            recv_sem=recv_sems.at[0, j - 1], device_id={"req": lax.rem(me + j, n)}, device_id_type=MESH_ID)
        copy.start()
        copies.append(copy)

    zero_q = jnp.zeros_like(q)
    qm = jnp.concatenate([jnp.where(hm0, q, zero_q), jnp.where(hm0, zero_q, q)], axis=0)
    nt = (((1,), (1,)), ((), ()))
    s = lax.dot_general(qm, pk_ref[...], nt, preferred_element_type=jnp.float32) * scale
    length = jnp.zeros((rows, 1), jnp.int32)
    page0 = jnp.zeros((rows, 1), jnp.int32)
    page1 = jnp.zeros((rows, 1), jnp.int32)
    for r in range(rows):
        length = jnp.where(row_id == r, info_ref[2 + r], length)
        page0 = jnp.where(row_id == r, info_ref[2 + rows + 2 * r], page0)
        page1 = jnp.where(row_id == r, info_ref[3 + rows + 2 * r], page1)
    tok = lax.broadcasted_iota(jnp.int32, (1, tokens), 1)
    tpage = tok // PAGE_SIZE
    tslot = tok % PAGE_SIZE
    usable = ((tpage == page0) & (tslot < length)) | ((tpage == page1) & (tslot + PAGE_SIZE < length))
    usable = usable & (length <= SHORT_MAX)
    usable2 = jnp.concatenate([usable, usable], axis=0)
    s = jnp.where(usable2, s, -jnp.inf)
    prod = q32 * k_ref[...].astype(jnp.float32)
    own0 = jnp.sum(jnp.where(hm0, prod, 0.0), axis=1, keepdims=True)
    own1 = jnp.sum(jnp.where(hm0, 0.0, prod), axis=1, keepdims=True)
    own = jnp.concatenate([own0, own1], axis=0) * scale
    m_s = jnp.maximum(jnp.max(s, axis=1, keepdims=True), own)
    w = jnp.exp(s - m_s)
    ow = jnp.exp(own - m_s)
    tot_s = jnp.sum(w, axis=1, keepdims=True) + ow
    nm = jnp.dot(w.astype(jnp.bfloat16), pv_ref[...], preferred_element_type=jnp.float32)
    owb = ow.astype(jnp.bfloat16).astype(jnp.float32)
    numer = jnp.where(hm0, nm[:rows], nm[rows:]) + jnp.where(
        hm0, owb[:rows], owb[rows:]) * v_ref[...].astype(jnp.float32)

    for copy in copies:
        copy.wait()
    qland[pl.ds(me, 1), :] = qsend[...]
    src_id = lax.broadcasted_iota(jnp.int32, (n, 1), 0)
    lq = jnp.sum(jnp.where(src_id == owner, qland[...], 0.0), axis=0, keepdims=True)
    lq = lq.astype(jnp.bfloat16)
    zero_l = jnp.zeros_like(lq)
    lqm = jnp.concatenate([jnp.where(hm0, lq, zero_l), jnp.where(hm0, zero_l, lq)], axis=0)
    ls = lax.dot_general(lqm, lk_ref[...], nt, preferred_element_type=jnp.float32) * scale
    m_l = jnp.max(ls, axis=1, keepdims=True)
    lw = jnp.exp(ls - m_l)
    l_l = jnp.sum(lw, axis=1, keepdims=True)
    acc = jnp.dot(lw.astype(jnp.bfloat16), lv_ref[...], preferred_element_type=jnp.float32)
    acc_row = jnp.where(hm0, acc[0:1], acc[1:2])
    width = psend.shape[1]
    psend[...] = jnp.zeros((1, width), jnp.float32)
    psend[:, 0:cols] = acc_row
    t = lax.broadcasted_iota(jnp.int32, (1, 128), 1)
    tail = jnp.where(t == 0, m_l[0:1], jnp.where(t == 1, m_l[1:2], jnp.where(
        t == 2, l_l[0:1], jnp.where(t == 3, l_l[1:2], 0.0))))
    psend[:, width - 128 : width] = tail

    copies = []
    for j in range(1, n):
        copy = pltpu.make_async_remote_copy(
            src_ref=psend, dst_ref=pland.at[pl.ds(me, 1)], send_sem=send_sems.at[1, j - 1],
            recv_sem=recv_sems.at[1, j - 1], device_id={"req": lax.rem(me + j, n)}, device_id_type=MESH_ID)
        copy.start()
        copies.append(copy)
    for copy in copies:
        copy.wait()
    pland[pl.ds(me, 1), :] = psend[...]

    parts = pland[...]
    base = width - 128
    sums_all = parts[:, 0:cols]
    whole = []
    for h in range(2):
        mh = parts[:, base + h : base + h + 1]
        lh = parts[:, base + 2 + h : base + 3 + h]
        wm = jnp.max(mh, axis=0, keepdims=True)
        keep = jnp.exp(mh - wm)
        wt = jnp.sum(lh * keep, axis=0, keepdims=True)
        ws = jnp.sum(sums_all * keep, axis=0, keepdims=True)
        whole.append((wm, wt, ws))
    whole_sums = jnp.where(hm0, whole[0][2], whole[1][2])
    chosen = (row_id == long_local) & (me == owner)
    kl, kg, tt = [], [], []
    for h in range(2):
        mh = m_s[h * rows : (h + 1) * rows]
        top = jnp.where(chosen, jnp.maximum(mh, whole[h][0]), mh)
        klh = jnp.exp(mh - top)
        kgh = jnp.where(chosen, jnp.exp(whole[h][0] - top), 0.0)
        kl.append(klh)
        kg.append(kgh)
        tt.append(tot_s[h * rows : (h + 1) * rows] * klh + kgh * whole[h][1])
    numer = numer * jnp.where(hm0, kl[0], kl[1]) + jnp.where(hm0, kg[0], kg[1]) * whole_sums
    out_ref[...] = (numer / jnp.where(hm0, tt[0], tt[1])).astype(out_ref.dtype)


def attention(n, info, query, new_key, new_value, page_k, page_v, long_keys, long_values):
    scale = 1.0 / math.sqrt(HEAD_DIM)
    cols = query.shape[1]
    width = -(-cols // 128) * 128 + 128
    vmem = pl.BlockSpec(memory_space=pltpu.VMEM)
    return pl.pallas_call(
        functools.partial(attention_kernel, n, scale),
        out_shape=jax.ShapeDtypeStruct(query.shape, jnp.bfloat16),
        in_specs=[pl.BlockSpec(memory_space=pltpu.SMEM)] + [vmem] * 7,
        out_specs=vmem,
        scratch_shapes=[
            pltpu.VMEM((1, cols), jnp.float32),
            pltpu.VMEM((n, cols), jnp.float32),
            pltpu.VMEM((1, width), jnp.float32),
            pltpu.VMEM((n, width), jnp.float32),
            pltpu.SemaphoreType.DMA((2, n - 1)),
            pltpu.SemaphoreType.DMA((2, n - 1)),
        ],
        compiler_params=pltpu.CompilerParams(collective_id=0, has_side_effects=True),
    )(info, query, new_key, new_value, page_k, page_v, long_keys, long_values)


def shards(
    n_req,
    n_mdl,
    query,
    new_key,
    new_value,
    page_keys,
    page_values,
    long_keys,
    long_values,
    cache_lengths,
    block_table,
    out_weight,
    residual,
    norm_gain,
    x_weight,
    bc_weight,
    dt_weight,
    z_weight,
    dt_bias,
    a_log,
    skip_gain,
    conv_x_weight,
    conv_bc_weight,
    conv_x_state,
    conv_bc_state,
    ssm_state,
    out_gain,
):
    req_count = query.shape[0]
    local_cols = query.shape[1]
    heads_here = local_cols // HEAD_DIM
    scale = 1.0 / math.sqrt(HEAD_DIM)
    device = lax.axis_index("req")
    pages_here = page_keys.shape[0]
    long_row = jnp.argmax(cache_lengths)
    owner = long_row // req_count
    long_local = long_row % req_count

    assert heads_here == 2
    my_lengths = lax.dynamic_slice_in_dim(cache_lengths, device * req_count, req_count)
    local_pages = block_table - device * pages_here
    info = jnp.concatenate(
        [jnp.stack([owner, long_local]).astype(jnp.int32), my_lengths, local_pages.reshape(-1)]
    )
    tokens_here = pages_here * PAGE_SIZE
    attended = attention(
        n_req,
        info,
        query,
        new_key,
        new_value,
        page_keys.reshape(tokens_here, local_cols),
        page_values.reshape(tokens_here, local_cols),
        long_keys,
        long_values,
    )

    projected = jnp.dot(attended, out_weight, preferred_element_type=jnp.float32)
    feature_cols = residual.shape[1]
    feature_start = lax.axis_index("mdl") * feature_cols
    partials, residuals = exchange([projected.astype(jnp.bfloat16), residual], "mdl", n_mdl, 2)
    residual_all = jnp.transpose(residuals, (1, 0, 2)).reshape(req_count, n_mdl * feature_cols)
    summed = jnp.sum(partials.astype(jnp.float32), axis=0)
    hidden_all = (residual_all.astype(jnp.float32) + summed).astype(jnp.bfloat16)
    hidden = lax.dynamic_slice_in_dim(hidden_all, feature_start, feature_cols, 1)
    hidden_f = hidden_all.astype(jnp.float32)
    squares = jnp.sum(hidden_f * hidden_f, axis=-1)
    inverse = lax.rsqrt(squares / MODEL_WIDTH + 1e-05)
    normed = (hidden_f * inverse[:, None] * norm_gain.astype(jnp.float32)[None, :]).astype(
        jnp.bfloat16
    )

    x_in = jnp.dot(normed, x_weight, preferred_element_type=jnp.float32)
    bc_in = jnp.dot(normed, bc_weight, preferred_element_type=jnp.float32)
    dt_in = jnp.dot(normed, dt_weight, preferred_element_type=jnp.float32)
    z_in = jnp.dot(normed, z_weight, preferred_element_type=jnp.float32)
    window_x = jnp.concatenate([conv_x_state.astype(jnp.float32), x_in[:, None, :]], axis=1)
    x_conv = jax.nn.silu(jnp.sum(window_x * conv_x_weight.astype(jnp.float32)[None], axis=1))
    window_bc = jnp.concatenate([conv_bc_state.astype(jnp.float32), bc_in[:, None, :]], axis=1)
    bc_conv = jax.nn.silu(jnp.sum(window_bc * conv_bc_weight.astype(jnp.float32)[None], axis=1))
    b_part = bc_conv[:, :STATE_DIM]
    c_part = bc_conv[:, STATE_DIM:]
    mamba_heads = dt_bias.shape[0]
    step = jax.nn.softplus(dt_in + dt_bias[None, :])
    decay = jnp.exp(-jnp.exp(a_log)[None, :] * step)
    x_heads = x_conv.reshape(req_count, mamba_heads, MHEAD_DIM)
    state = ssm_state.reshape(req_count, mamba_heads, MHEAD_DIM, STATE_DIM)
    state_new = (
        decay[:, :, None, None] * state
        + (step[:, :, None] * x_heads)[..., None] * b_part[:, None, None, :]
    )
    y_heads = (
        jnp.sum(state_new * c_part[:, None, None, :], axis=-1) + skip_gain[None, :, None] * x_heads
    )
    y_flat = y_heads.reshape(req_count, mamba_heads * MHEAD_DIM)
    gated = y_flat * jax.nn.silu(z_in)
    y_part = jnp.sum(gated * gated, axis=-1)
    y_pad = (-req_count) % 128
    y_msg = jnp.concatenate([y_part, jnp.zeros((y_pad,), jnp.float32)])[None, :]
    (y_all,) = exchange([y_msg], "mdl", n_mdl, 3)
    y_squares = jnp.sum(y_all[:, :req_count], axis=0)
    y_inverse = lax.rsqrt(y_squares / (MHEADS * MHEAD_DIM) + 1e-05)
    mixed = (gated * y_inverse[:, None] * out_gain.astype(jnp.float32)[None, :]).astype(
        jnp.bfloat16
    )
    return (hidden, mixed)


def solution(mesh):
    return jax.shard_map(
        functools.partial(shards, mesh.shape["req"], mesh.shape["mdl"]),
        mesh=mesh,
        in_specs=(
            P("req", "mdl"),
            P("req", "mdl"),
            P("req", "mdl"),
            P("req", None, "mdl"),
            P("req", None, "mdl"),
            P("req", "mdl"),
            P("req", "mdl"),
            P(),
            P("req", None),
            P("mdl", None),
            P("req", "mdl"),
            P(),
            P(None, "mdl"),
            P(),
            P(None, "mdl"),
            P(None, "mdl"),
            P("mdl"),
            P("mdl"),
            P("mdl"),
            P(None, "mdl"),
            P(),
            P("req", None, "mdl"),
            P("req", None, None),
            P("req", "mdl", None),
            P("mdl"),
        ),
        out_specs=(P("req", "mdl"), P("req", "mdl")),
        check_vma=False,
    )
```

```python
import functools
import math

import jax
import jax.numpy as jnp
from jax import lax
from jax.experimental import pallas as pl
from jax.experimental.pallas import tpu as pltpu
from jax.sharding import PartitionSpec as P

MODEL_WIDTH = 3584
HEAD_DIM = 224
MHEADS = 56
MHEAD_DIM = 64
STATE_DIM = 64
SHORT_MAX = 32
PAGE_SIZE = 16

MESH_ID = pl.DeviceIdType.MESH


def exchange_kernel(n, axis, count, *refs):
    x_refs = refs[:count]
    out_refs = refs[count : 2 * count]
    lands = refs[2 * count : 3 * count]
    send_sems, recv_sems = refs[3 * count :]
    me = lax.axis_index(axis)
    barrier = pltpu.get_barrier_semaphore()
    for j in range(1, n):
        peer = lax.rem(me + j, n)
        pl.semaphore_signal(barrier, inc=1, device_id={axis: peer}, device_id_type=MESH_ID)
    pl.semaphore_wait(barrier, n - 1)
    copies = []
    for k in range(count):
        rows = len(x_refs[k].shape) == 2 and x_refs[k].shape[0] == 1
        slot = lands[k].at[pl.ds(me, 1)] if rows else lands[k].at[me]
        for j in range(1, n):
            peer = lax.rem(me + j, n)
            copy = pltpu.make_async_remote_copy(
                src_ref=x_refs[k],
                dst_ref=slot,
                send_sem=send_sems.at[k, j - 1],
                recv_sem=recv_sems.at[k, j - 1],
                device_id={axis: peer},
                device_id_type=MESH_ID,
            )
            copy.start()
            copies.append(copy)
    for copy in copies:
        copy.wait()
    for k in range(count):
        rows = len(x_refs[k].shape) == 2 and x_refs[k].shape[0] == 1
        if rows:
            lands[k][pl.ds(me, 1), :] = x_refs[k][...]
        else:
            lands[k][me] = x_refs[k][...]
        out_refs[k][...] = lands[k][...]


def exchange(xs, axis, n, cid):
    shapes = []
    for x in xs:
        rows = x.ndim == 2 and x.shape[0] == 1
        shapes.append(jax.ShapeDtypeStruct((n, x.shape[1]) if rows else (n,) + x.shape, x.dtype))
    count = len(xs)
    return pl.pallas_call(
        functools.partial(exchange_kernel, n, axis, count),
        out_shape=tuple(shapes),
        in_specs=[pl.BlockSpec(memory_space=pltpu.VMEM)] * count,
        out_specs=tuple([pl.BlockSpec(memory_space=pltpu.VMEM)] * count),
        scratch_shapes=[pltpu.VMEM(s.shape, s.dtype) for s in shapes]
        + [pltpu.SemaphoreType.DMA((count, n - 1)), pltpu.SemaphoreType.DMA((count, n - 1))],
        compiler_params=pltpu.CompilerParams(collective_id=cid, has_side_effects=True),
    )(*xs)


def by_head(values, head_mask):
    out = jnp.zeros(values.shape[:-1] + (head_mask.shape[1],), values.dtype)
    for h in range(head_mask.shape[0]):
        out = jnp.where(head_mask[h], values[..., h : h + 1], out)
    return out


def pick_head(values, head_mask):
    out = values[..., 0, :]
    for h in range(1, head_mask.shape[0]):
        out = jnp.where(head_mask[h], values[..., h, :], out)
    return out


def attention_kernel(n, scale, cl_ref, lens_ref, bt_ref, q_ref, k_ref, v_ref, pk_hbm, pv_hbm,
                     lk_hbm, lv_hbm, out_ref, pk_ref, pv_ref, lk_ref, lv_ref, qsend, qland, psend,
                     pland, load_sems, send_sems, recv_sems):
    me = lax.axis_index("req")
    rows, cols = q_ref.shape
    tokens = pk_ref.shape[0]
    loads = []
    for i, (src, dst) in enumerate(((pk_hbm, pk_ref), (pv_hbm, pv_ref), (lk_hbm, lk_ref), (lv_hbm, lv_ref))):
        load = pltpu.make_async_copy(src, dst, load_sems.at[i])
        load.start()
        loads.append(load)
    barrier = pltpu.get_barrier_semaphore()
    for j in range(1, n):
        pl.semaphore_signal(barrier, inc=1, device_id={"req": lax.rem(me + j, n)}, device_id_type=MESH_ID)

    cl = cl_ref[...]
    longest = jnp.max(cl, axis=1, keepdims=True)
    where_long = jnp.where(cl == longest, lax.broadcasted_iota(jnp.int32, cl.shape, 1), cl.shape[1])
    long_row = jnp.min(where_long, axis=1, keepdims=True)
    owner = long_row // rows
    long_local = long_row - owner * rows
    lane = lax.broadcasted_iota(jnp.int32, (1, cols), 1)
    hm0 = lane < HEAD_DIM
    row_id = lax.broadcasted_iota(jnp.int32, (rows, 1), 0)
    q = q_ref[...]
    q32 = q.astype(jnp.float32)
    qsend[...] = jnp.sum(jnp.where(row_id == long_local, q32, 0.0), axis=0, keepdims=True)
    pl.semaphore_wait(barrier, n - 1)

    copies = []
    for j in range(1, n):
        copy = pltpu.make_async_remote_copy(
            src_ref=qsend, dst_ref=qland.at[pl.ds(me, 1)], send_sem=send_sems.at[0, j - 1],
            recv_sem=recv_sems.at[0, j - 1], device_id={"req": lax.rem(me + j, n)}, device_id_type=MESH_ID)
        copy.start()
        copies.append(copy)

    zero_q = jnp.zeros_like(q)
    qm = jnp.concatenate([jnp.where(hm0, q, zero_q), jnp.where(hm0, zero_q, q)], axis=0)
    nt = (((1,), (1,)), ((), ()))
    loads[0].wait()
    loads[1].wait()
    s = lax.dot_general(qm, pk_ref[...], nt, preferred_element_type=jnp.float32) * scale
    length = jnp.zeros((rows, 1), jnp.int32)
    page0 = jnp.zeros((rows, 1), jnp.int32)
    page1 = jnp.zeros((rows, 1), jnp.int32)
    for r in range(rows):
        length = jnp.where(row_id == r, lens_ref[me * rows + r], length)
        page0 = jnp.where(row_id == r, bt_ref[r, 0] - me * tokens // PAGE_SIZE, page0)
        page1 = jnp.where(row_id == r, bt_ref[r, 1] - me * tokens // PAGE_SIZE, page1)
    tok = lax.broadcasted_iota(jnp.int32, (1, tokens), 1)
    tpage = tok // PAGE_SIZE
    tslot = tok % PAGE_SIZE
    usable = ((tpage == page0) & (tslot < length)) | ((tpage == page1) & (tslot + PAGE_SIZE < length))
    usable = usable & (length <= SHORT_MAX)
    usable2 = jnp.concatenate([usable, usable], axis=0)
    s = jnp.where(usable2, s, -jnp.inf)
    prod = q32 * k_ref[...].astype(jnp.float32)
    own0 = jnp.sum(jnp.where(hm0, prod, 0.0), axis=1, keepdims=True)
    own1 = jnp.sum(jnp.where(hm0, 0.0, prod), axis=1, keepdims=True)
    own = jnp.concatenate([own0, own1], axis=0) * scale
    m_s = jnp.maximum(jnp.max(s, axis=1, keepdims=True), own)
    w = jnp.exp(s - m_s)
    ow = jnp.exp(own - m_s)
    tot_s = jnp.sum(w, axis=1, keepdims=True) + ow
    nm = jnp.dot(w.astype(jnp.bfloat16), pv_ref[...], preferred_element_type=jnp.float32)
    owb = ow.astype(jnp.bfloat16).astype(jnp.float32)
    numer = jnp.where(hm0, nm[:rows], nm[rows:]) + jnp.where(
        hm0, owb[:rows], owb[rows:]) * v_ref[...].astype(jnp.float32)

    for copy in copies:
        copy.wait()
    qland[pl.ds(me, 1), :] = qsend[...]
    src_id = lax.broadcasted_iota(jnp.int32, (n, 1), 0)
    lq = jnp.sum(jnp.where(src_id == owner, qland[...], 0.0), axis=0, keepdims=True)
    lq = lq.astype(jnp.bfloat16)
    zero_l = jnp.zeros_like(lq)
    lqm = jnp.concatenate([jnp.where(hm0, lq, zero_l), jnp.where(hm0, zero_l, lq)], axis=0)
    loads[2].wait()
    loads[3].wait()
    ls = lax.dot_general(lqm, lk_ref[...], nt, preferred_element_type=jnp.float32) * scale
    m_l = jnp.max(ls, axis=1, keepdims=True)
    lw = jnp.exp(ls - m_l)
    l_l = jnp.sum(lw, axis=1, keepdims=True)
    acc = jnp.dot(lw.astype(jnp.bfloat16), lv_ref[...], preferred_element_type=jnp.float32)
    acc_row = jnp.where(hm0, acc[0:1], acc[1:2])
    width = psend.shape[1]
    psend[...] = jnp.zeros((1, width), jnp.float32)
    psend[:, 0:cols] = acc_row
    t = lax.broadcasted_iota(jnp.int32, (1, 128), 1)
    tail = jnp.where(t == 0, m_l[0:1], jnp.where(t == 1, m_l[1:2], jnp.where(
        t == 2, l_l[0:1], jnp.where(t == 3, l_l[1:2], 0.0))))
    psend[:, width - 128 : width] = tail

    copies = []
    for j in range(1, n):
        copy = pltpu.make_async_remote_copy(
            src_ref=psend, dst_ref=pland.at[pl.ds(me, 1)], send_sem=send_sems.at[1, j - 1],
            recv_sem=recv_sems.at[1, j - 1], device_id={"req": lax.rem(me + j, n)}, device_id_type=MESH_ID)
        copy.start()
        copies.append(copy)
    for copy in copies:
        copy.wait()
    pland[pl.ds(me, 1), :] = psend[...]

    parts = pland[...]
    base = width - 128
    sums_all = parts[:, 0:cols]
    whole = []
    for h in range(2):
        mh = parts[:, base + h : base + h + 1]
        lh = parts[:, base + 2 + h : base + 3 + h]
        wm = jnp.max(mh, axis=0, keepdims=True)
        keep = jnp.exp(mh - wm)
        wt = jnp.sum(lh * keep, axis=0, keepdims=True)
        ws = jnp.sum(sums_all * keep, axis=0, keepdims=True)
        whole.append((wm, wt, ws))
    whole_sums = jnp.where(hm0, whole[0][2], whole[1][2])
    chosen = (row_id == long_local) & (me == owner)
    kl, kg, tt = [], [], []
    for h in range(2):
        mh = m_s[h * rows : (h + 1) * rows]
        top = jnp.where(chosen, jnp.maximum(mh, whole[h][0]), mh)
        klh = jnp.exp(mh - top)
        kgh = jnp.where(chosen, jnp.exp(whole[h][0] - top), 0.0)
        kl.append(klh)
        kg.append(kgh)
        tt.append(tot_s[h * rows : (h + 1) * rows] * klh + kgh * whole[h][1])
    numer = numer * jnp.where(hm0, kl[0], kl[1]) + jnp.where(hm0, kg[0], kg[1]) * whole_sums
    out_ref[...] = (numer / jnp.where(hm0, tt[0], tt[1])).astype(out_ref.dtype)


def attention(n, cache_lengths, block_table, query, new_key, new_value, page_k, page_v, long_keys,
              long_values):
    scale = 1.0 / math.sqrt(HEAD_DIM)
    cols = query.shape[1]
    width = -(-cols // 128) * 128 + 128
    vmem = pl.BlockSpec(memory_space=pltpu.VMEM)
    smem = pl.BlockSpec(memory_space=pltpu.SMEM)
    anywhere = pl.BlockSpec(memory_space=pl.ANY)
    return pl.pallas_call(
        functools.partial(attention_kernel, n, scale),
        out_shape=jax.ShapeDtypeStruct(query.shape, jnp.bfloat16),
        in_specs=[vmem, smem, smem, vmem, vmem, vmem] + [anywhere] * 4,
        out_specs=vmem,
        scratch_shapes=[
            pltpu.VMEM(page_k.shape, page_k.dtype),
            pltpu.VMEM(page_v.shape, page_v.dtype),
            pltpu.VMEM(long_keys.shape, long_keys.dtype),
            pltpu.VMEM(long_values.shape, long_values.dtype),
            pltpu.VMEM((1, cols), jnp.float32),
            pltpu.VMEM((n, cols), jnp.float32),
            pltpu.VMEM((1, width), jnp.float32),
            pltpu.VMEM((n, width), jnp.float32),
            pltpu.SemaphoreType.DMA((4,)),
            pltpu.SemaphoreType.DMA((2, n - 1)),
            pltpu.SemaphoreType.DMA((2, n - 1)),
        ],
        compiler_params=pltpu.CompilerParams(collective_id=0, has_side_effects=True),
    )(
        cache_lengths.reshape(1, -1),
        cache_lengths,
        block_table,
        query,
        new_key,
        new_value,
        page_k,
        page_v,
        long_keys,
        long_values,
    )


def shards(
    n_req,
    n_mdl,
    query,
    new_key,
    new_value,
    page_keys,
    page_values,
    long_keys,
    long_values,
    cache_lengths,
    block_table,
    out_weight,
    residual,
    norm_gain,
    x_weight,
    bc_weight,
    dt_weight,
    z_weight,
    dt_bias,
    a_log,
    skip_gain,
    conv_x_weight,
    conv_bc_weight,
    conv_x_state,
    conv_bc_state,
    ssm_state,
    out_gain,
):
    req_count = query.shape[0]
    local_cols = query.shape[1]
    heads_here = local_cols // HEAD_DIM
    scale = 1.0 / math.sqrt(HEAD_DIM)
    device = lax.axis_index("req")
    pages_here = page_keys.shape[0]
    long_row = jnp.argmax(cache_lengths)
    owner = long_row // req_count
    long_local = long_row % req_count

    assert heads_here == 2
    tokens_here = pages_here * PAGE_SIZE
    attended = attention(
        n_req,
        cache_lengths,
        block_table,
        query,
        new_key,
        new_value,
        page_keys.reshape(tokens_here, local_cols),
        page_values.reshape(tokens_here, local_cols),
        long_keys,
        long_values,
    )

    projected = jnp.dot(attended, out_weight, preferred_element_type=jnp.float32)
    feature_cols = residual.shape[1]
    feature_start = lax.axis_index("mdl") * feature_cols
    partials, residuals = exchange([projected.astype(jnp.bfloat16), residual], "mdl", n_mdl, 2)
    residual_all = jnp.transpose(residuals, (1, 0, 2)).reshape(req_count, n_mdl * feature_cols)
    summed = jnp.sum(partials.astype(jnp.float32), axis=0)
    hidden_all = (residual_all.astype(jnp.float32) + summed).astype(jnp.bfloat16)
    hidden = lax.dynamic_slice_in_dim(hidden_all, feature_start, feature_cols, 1)
    hidden_f = hidden_all.astype(jnp.float32)
    squares = jnp.sum(hidden_f * hidden_f, axis=-1)
    inverse = lax.rsqrt(squares / MODEL_WIDTH + 1e-05)
    normed = (hidden_f * inverse[:, None] * norm_gain.astype(jnp.float32)[None, :]).astype(
        jnp.bfloat16
    )

    x_in = jnp.dot(normed, x_weight, preferred_element_type=jnp.float32)
    bc_in = jnp.dot(normed, bc_weight, preferred_element_type=jnp.float32)
    dt_in = jnp.dot(normed, dt_weight, preferred_element_type=jnp.float32)
    z_in = jnp.dot(normed, z_weight, preferred_element_type=jnp.float32)
    window_x = jnp.concatenate([conv_x_state.astype(jnp.float32), x_in[:, None, :]], axis=1)
    x_conv = jax.nn.silu(jnp.sum(window_x * conv_x_weight.astype(jnp.float32)[None], axis=1))
    window_bc = jnp.concatenate([conv_bc_state.astype(jnp.float32), bc_in[:, None, :]], axis=1)
    bc_conv = jax.nn.silu(jnp.sum(window_bc * conv_bc_weight.astype(jnp.float32)[None], axis=1))
    b_part = bc_conv[:, :STATE_DIM]
    c_part = bc_conv[:, STATE_DIM:]
    mamba_heads = dt_bias.shape[0]
    step = jax.nn.softplus(dt_in + dt_bias[None, :])
    decay = jnp.exp(-jnp.exp(a_log)[None, :] * step)
    x_heads = x_conv.reshape(req_count, mamba_heads, MHEAD_DIM)
    state = ssm_state.reshape(req_count, mamba_heads, MHEAD_DIM, STATE_DIM)
    state_new = (
        decay[:, :, None, None] * state
        + (step[:, :, None] * x_heads)[..., None] * b_part[:, None, None, :]
    )
    y_heads = (
        jnp.sum(state_new * c_part[:, None, None, :], axis=-1) + skip_gain[None, :, None] * x_heads
    )
    y_flat = y_heads.reshape(req_count, mamba_heads * MHEAD_DIM)
    gated = y_flat * jax.nn.silu(z_in)
    y_part = jnp.sum(gated * gated, axis=-1)
    y_pad = (-req_count) % 128
    y_msg = jnp.concatenate([y_part, jnp.zeros((y_pad,), jnp.float32)])[None, :]
    (y_all,) = exchange([y_msg], "mdl", n_mdl, 3)
    y_squares = jnp.sum(y_all[:, :req_count], axis=0)
    y_inverse = lax.rsqrt(y_squares / (MHEADS * MHEAD_DIM) + 1e-05)
    mixed = (gated * y_inverse[:, None] * out_gain.astype(jnp.float32)[None, :]).astype(
        jnp.bfloat16
    )
    return (hidden, mixed)


def solution(mesh):
    return jax.shard_map(
        functools.partial(shards, mesh.shape["req"], mesh.shape["mdl"]),
        mesh=mesh,
        in_specs=(
            P("req", "mdl"),
            P("req", "mdl"),
            P("req", "mdl"),
            P("req", None, "mdl"),
            P("req", None, "mdl"),
            P("req", "mdl"),
            P("req", "mdl"),
            P(),
            P("req", None),
            P("mdl", None),
            P("req", "mdl"),
            P(),
            P(None, "mdl"),
            P(),
            P(None, "mdl"),
            P(None, "mdl"),
            P("mdl"),
            P("mdl"),
            P("mdl"),
            P(None, "mdl"),
            P(),
            P("req", None, "mdl"),
            P("req", None, None),
            P("req", "mdl", None),
            P("mdl"),
        ),
        out_specs=(P("req", "mdl"), P("req", "mdl")),
        check_vma=False,
    )
```

```python
import functools
import math

import jax
import jax.numpy as jnp
from jax import lax
from jax.experimental import pallas as pl
from jax.experimental.pallas import tpu as pltpu
from jax.sharding import PartitionSpec as P

MODEL_WIDTH = 3584
HEAD_DIM = 224
MHEADS = 56
MHEAD_DIM = 64
STATE_DIM = 64
SHORT_MAX = 32
PAGE_SIZE = 16

MESH_ID = pl.DeviceIdType.MESH


def exchange_kernel(n, axis, count, *refs):
    x_refs = refs[:count]
    out_refs = refs[count : 2 * count]
    lands = refs[2 * count : 3 * count]
    send_sems, recv_sems = refs[3 * count :]
    me = lax.axis_index(axis)
    barrier = pltpu.get_barrier_semaphore()
    for j in range(1, n):
        peer = lax.rem(me + j, n)
        pl.semaphore_signal(barrier, inc=1, device_id={axis: peer}, device_id_type=MESH_ID)
    pl.semaphore_wait(barrier, n - 1)
    copies = []
    for k in range(count):
        rows = len(x_refs[k].shape) == 2 and x_refs[k].shape[0] == 1
        slot = lands[k].at[pl.ds(me, 1)] if rows else lands[k].at[me]
        for j in range(1, n):
            peer = lax.rem(me + j, n)
            copy = pltpu.make_async_remote_copy(
                src_ref=x_refs[k],
                dst_ref=slot,
                send_sem=send_sems.at[k, j - 1],
                recv_sem=recv_sems.at[k, j - 1],
                device_id={axis: peer},
                device_id_type=MESH_ID,
            )
            copy.start()
            copies.append(copy)
    for copy in copies:
        copy.wait()
    for k in range(count):
        rows = len(x_refs[k].shape) == 2 and x_refs[k].shape[0] == 1
        if rows:
            lands[k][pl.ds(me, 1), :] = x_refs[k][...]
        else:
            lands[k][me] = x_refs[k][...]
        out_refs[k][...] = lands[k][...]


def exchange(xs, axis, n, cid):
    shapes = []
    for x in xs:
        rows = x.ndim == 2 and x.shape[0] == 1
        shapes.append(jax.ShapeDtypeStruct((n, x.shape[1]) if rows else (n,) + x.shape, x.dtype))
    count = len(xs)
    return pl.pallas_call(
        functools.partial(exchange_kernel, n, axis, count),
        out_shape=tuple(shapes),
        in_specs=[pl.BlockSpec(memory_space=pltpu.VMEM)] * count,
        out_specs=tuple([pl.BlockSpec(memory_space=pltpu.VMEM)] * count),
        scratch_shapes=[pltpu.VMEM(s.shape, s.dtype) for s in shapes]
        + [pltpu.SemaphoreType.DMA((count, n - 1)), pltpu.SemaphoreType.DMA((count, n - 1))],
        compiler_params=pltpu.CompilerParams(collective_id=cid, has_side_effects=True),
    )(*xs)


def by_head(values, head_mask):
    out = jnp.zeros(values.shape[:-1] + (head_mask.shape[1],), values.dtype)
    for h in range(head_mask.shape[0]):
        out = jnp.where(head_mask[h], values[..., h : h + 1], out)
    return out


def pick_head(values, head_mask):
    out = values[..., 0, :]
    for h in range(1, head_mask.shape[0]):
        out = jnp.where(head_mask[h], values[..., h, :], out)
    return out


def attention_kernel(n, scale, cl_ref, lens_ref, bt_ref, q_ref, k_ref, v_ref, pk_hbm, pv_hbm,
                     lk_hbm, lv_hbm, out_ref, pk_ref, pv_ref, lk_ref, lv_ref, qsend, qland, psend,
                     pland, load_sems, send_sems, recv_sems):
    me = lax.axis_index("req")
    rows, cols = q_ref.shape
    tokens = pk_ref.shape[0]
    loads = []
    for i, (src, dst) in enumerate(((pk_hbm, pk_ref), (pv_hbm, pv_ref), (lk_hbm, lk_ref), (lv_hbm, lv_ref))):
        load = pltpu.make_async_copy(src, dst, load_sems.at[i])
        load.start()
        loads.append(load)
    barrier = pltpu.get_barrier_semaphore()
    for j in range(1, n):
        pl.semaphore_signal(barrier, inc=1, device_id={"req": lax.rem(me + j, n)}, device_id_type=MESH_ID)

    cl = cl_ref[...]
    longest = jnp.max(cl, axis=1, keepdims=True)
    where_long = jnp.where(cl == longest, lax.broadcasted_iota(jnp.int32, cl.shape, 1), cl.shape[1])
    long_row = jnp.min(where_long, axis=1, keepdims=True)
    owner = long_row // rows
    long_local = long_row - owner * rows
    lane = lax.broadcasted_iota(jnp.int32, (1, cols), 1)
    hm0 = lane < HEAD_DIM
    row_id = lax.broadcasted_iota(jnp.int32, (rows, 1), 0)
    q = q_ref[...]
    q32 = q.astype(jnp.float32)
    qsend[...] = jnp.sum(jnp.where(row_id == long_local, q32, 0.0), axis=0, keepdims=True)
    pl.semaphore_wait(barrier, n - 1)

    copies = []
    for j in range(1, n):
        copy = pltpu.make_async_remote_copy(
            src_ref=qsend, dst_ref=qland.at[pl.ds(me, 1)], send_sem=send_sems.at[0, j - 1],
            recv_sem=recv_sems.at[0, j - 1], device_id={"req": lax.rem(me + j, n)}, device_id_type=MESH_ID)
        copy.start()
        copies.append(copy)

    zero_q = jnp.zeros_like(q)
    qm = jnp.concatenate([jnp.where(hm0, q, zero_q), jnp.where(hm0, zero_q, q)], axis=0)
    nt = (((1,), (1,)), ((), ()))
    loads[0].wait()
    loads[1].wait()
    s = lax.dot_general(qm, pk_ref[...], nt, preferred_element_type=jnp.float32) * scale
    length = jnp.zeros((rows, 1), jnp.int32)
    page0 = jnp.zeros((rows, 1), jnp.int32)
    page1 = jnp.zeros((rows, 1), jnp.int32)
    for r in range(rows):
        length = jnp.where(row_id == r, lens_ref[me * rows + r], length)
        page0 = jnp.where(row_id == r, bt_ref[0, r] - me * tokens // PAGE_SIZE, page0)
        page1 = jnp.where(row_id == r, bt_ref[1, r] - me * tokens // PAGE_SIZE, page1)
    tok = lax.broadcasted_iota(jnp.int32, (1, tokens), 1)
    tpage = tok // PAGE_SIZE
    tslot = tok % PAGE_SIZE
    usable = ((tpage == page0) & (tslot < length)) | ((tpage == page1) & (tslot + PAGE_SIZE < length))
    usable = usable & (length <= SHORT_MAX)
    usable2 = jnp.concatenate([usable, usable], axis=0)
    s = jnp.where(usable2, s, -jnp.inf)
    prod = q32 * k_ref[...].astype(jnp.float32)
    own0 = jnp.sum(jnp.where(hm0, prod, 0.0), axis=1, keepdims=True)
    own1 = jnp.sum(jnp.where(hm0, 0.0, prod), axis=1, keepdims=True)
    own = jnp.concatenate([own0, own1], axis=0) * scale
    m_s = jnp.maximum(jnp.max(s, axis=1, keepdims=True), own)
    w = jnp.exp(s - m_s)
    ow = jnp.exp(own - m_s)
    tot_s = jnp.sum(w, axis=1, keepdims=True) + ow
    nm = jnp.dot(w.astype(jnp.bfloat16), pv_ref[...], preferred_element_type=jnp.float32)
    owb = ow.astype(jnp.bfloat16).astype(jnp.float32)
    numer = jnp.where(hm0, nm[:rows], nm[rows:]) + jnp.where(
        hm0, owb[:rows], owb[rows:]) * v_ref[...].astype(jnp.float32)

    for copy in copies:
        copy.wait()
    qland[pl.ds(me, 1), :] = qsend[...]
    src_id = lax.broadcasted_iota(jnp.int32, (n, 1), 0)
    lq = jnp.sum(jnp.where(src_id == owner, qland[...], 0.0), axis=0, keepdims=True)
    lq = lq.astype(jnp.bfloat16)
    zero_l = jnp.zeros_like(lq)
    lqm = jnp.concatenate([jnp.where(hm0, lq, zero_l), jnp.where(hm0, zero_l, lq)], axis=0)
    loads[2].wait()
    loads[3].wait()
    ls = jnp.dot(lqm, lk_ref[...], preferred_element_type=jnp.float32) * scale
    m_l = jnp.max(ls, axis=1, keepdims=True)
    lw = jnp.exp(ls - m_l)
    l_l = jnp.sum(lw, axis=1, keepdims=True)
    acc = lax.dot_general(lw.astype(jnp.bfloat16), lv_ref[...], nt, preferred_element_type=jnp.float32)
    acc_row = jnp.where(hm0, acc[0:1], acc[1:2])
    width = psend.shape[1]
    psend[...] = jnp.zeros((1, width), jnp.float32)
    psend[:, 0:cols] = acc_row
    t = lax.broadcasted_iota(jnp.int32, (1, 128), 1)
    tail = jnp.where(t == 0, m_l[0:1], jnp.where(t == 1, m_l[1:2], jnp.where(
        t == 2, l_l[0:1], jnp.where(t == 3, l_l[1:2], 0.0))))
    psend[:, width - 128 : width] = tail

    copies = []
    for j in range(1, n):
        copy = pltpu.make_async_remote_copy(
            src_ref=psend, dst_ref=pland.at[pl.ds(me, 1)], send_sem=send_sems.at[1, j - 1],
            recv_sem=recv_sems.at[1, j - 1], device_id={"req": lax.rem(me + j, n)}, device_id_type=MESH_ID)
        copy.start()
        copies.append(copy)
    for copy in copies:
        copy.wait()
    pland[pl.ds(me, 1), :] = psend[...]

    parts = pland[...]
    base = width - 128
    sums_all = parts[:, 0:cols]
    whole = []
    for h in range(2):
        mh = parts[:, base + h : base + h + 1]
        lh = parts[:, base + 2 + h : base + 3 + h]
        wm = jnp.max(mh, axis=0, keepdims=True)
        keep = jnp.exp(mh - wm)
        wt = jnp.sum(lh * keep, axis=0, keepdims=True)
        ws = jnp.sum(sums_all * keep, axis=0, keepdims=True)
        whole.append((wm, wt, ws))
    whole_sums = jnp.where(hm0, whole[0][2], whole[1][2])
    chosen = (row_id == long_local) & (me == owner)
    kl, kg, tt = [], [], []
    for h in range(2):
        mh = m_s[h * rows : (h + 1) * rows]
        top = jnp.where(chosen, jnp.maximum(mh, whole[h][0]), mh)
        klh = jnp.exp(mh - top)
        kgh = jnp.where(chosen, jnp.exp(whole[h][0] - top), 0.0)
        kl.append(klh)
        kg.append(kgh)
        tt.append(tot_s[h * rows : (h + 1) * rows] * klh + kgh * whole[h][1])
    numer = numer * jnp.where(hm0, kl[0], kl[1]) + jnp.where(hm0, kg[0], kg[1]) * whole_sums
    out_ref[...] = (numer / jnp.where(hm0, tt[0], tt[1])).astype(out_ref.dtype)


def attention(n, cache_lengths, block_table, query, new_key, new_value, page_k, page_v, long_keys,
              long_values):
    scale = 1.0 / math.sqrt(HEAD_DIM)
    cols = query.shape[1]
    width = -(-cols // 128) * 128 + 128
    vmem = pl.BlockSpec(memory_space=pltpu.VMEM)
    smem = pl.BlockSpec(memory_space=pltpu.SMEM)
    anywhere = pl.BlockSpec(memory_space=pl.ANY)
    return pl.pallas_call(
        functools.partial(attention_kernel, n, scale),
        out_shape=jax.ShapeDtypeStruct(query.shape, jnp.bfloat16),
        in_specs=[vmem, smem, smem, vmem, vmem, vmem] + [anywhere] * 4,
        out_specs=vmem,
        scratch_shapes=[
            pltpu.VMEM(page_k.shape, page_k.dtype),
            pltpu.VMEM(page_v.shape, page_v.dtype),
            pltpu.VMEM(long_keys.shape[::-1], long_keys.dtype),
            pltpu.VMEM(long_values.shape[::-1], long_values.dtype),
            pltpu.VMEM((1, cols), jnp.float32),
            pltpu.VMEM((n, cols), jnp.float32),
            pltpu.VMEM((1, width), jnp.float32),
            pltpu.VMEM((n, width), jnp.float32),
            pltpu.SemaphoreType.DMA((4,)),
            pltpu.SemaphoreType.DMA((2, n - 1)),
            pltpu.SemaphoreType.DMA((2, n - 1)),
        ],
        compiler_params=pltpu.CompilerParams(collective_id=0, has_side_effects=True),
    )(
        cache_lengths.reshape(1, -1),
        cache_lengths,
        block_table.T,
        query,
        new_key,
        new_value,
        page_k,
        page_v,
        long_keys.T,
        long_values.T,
    )


def shards(
    n_req,
    n_mdl,
    query,
    new_key,
    new_value,
    page_keys,
    page_values,
    long_keys,
    long_values,
    cache_lengths,
    block_table,
    out_weight,
    residual,
    norm_gain,
    x_weight,
    bc_weight,
    dt_weight,
    z_weight,
    dt_bias,
    a_log,
    skip_gain,
    conv_x_weight,
    conv_bc_weight,
    conv_x_state,
    conv_bc_state,
    ssm_state,
    out_gain,
):
    req_count = query.shape[0]
    local_cols = query.shape[1]
    heads_here = local_cols // HEAD_DIM
    scale = 1.0 / math.sqrt(HEAD_DIM)
    device = lax.axis_index("req")
    pages_here = page_keys.shape[0]
    long_row = jnp.argmax(cache_lengths)
    owner = long_row // req_count
    long_local = long_row % req_count

    assert heads_here == 2
    tokens_here = pages_here * PAGE_SIZE
    attended = attention(
        n_req,
        cache_lengths,
        block_table,
        query,
        new_key,
        new_value,
        page_keys.reshape(tokens_here, local_cols),
        page_values.reshape(tokens_here, local_cols),
        long_keys,
        long_values,
    )

    projected = jnp.dot(attended, out_weight, preferred_element_type=jnp.float32)
    feature_cols = residual.shape[1]
    feature_start = lax.axis_index("mdl") * feature_cols
    partials, residuals = exchange([projected.astype(jnp.bfloat16), residual], "mdl", n_mdl, 2)
    residual_all = jnp.transpose(residuals, (1, 0, 2)).reshape(req_count, n_mdl * feature_cols)
    summed = jnp.sum(partials.astype(jnp.float32), axis=0)
    hidden_all = (residual_all.astype(jnp.float32) + summed).astype(jnp.bfloat16)
    hidden = lax.dynamic_slice_in_dim(hidden_all, feature_start, feature_cols, 1)
    hidden_f = hidden_all.astype(jnp.float32)
    squares = jnp.sum(hidden_f * hidden_f, axis=-1)
    inverse = lax.rsqrt(squares / MODEL_WIDTH + 1e-05)
    normed = (hidden_f * inverse[:, None] * norm_gain.astype(jnp.float32)[None, :]).astype(
        jnp.bfloat16
    )

    x_in = jnp.dot(normed, x_weight, preferred_element_type=jnp.float32)
    bc_in = jnp.dot(normed, bc_weight, preferred_element_type=jnp.float32)
    dt_in = jnp.dot(normed, dt_weight, preferred_element_type=jnp.float32)
    z_in = jnp.dot(normed, z_weight, preferred_element_type=jnp.float32)
    window_x = jnp.concatenate([conv_x_state.astype(jnp.float32), x_in[:, None, :]], axis=1)
    x_conv = jax.nn.silu(jnp.sum(window_x * conv_x_weight.astype(jnp.float32)[None], axis=1))
    window_bc = jnp.concatenate([conv_bc_state.astype(jnp.float32), bc_in[:, None, :]], axis=1)
    bc_conv = jax.nn.silu(jnp.sum(window_bc * conv_bc_weight.astype(jnp.float32)[None], axis=1))
    b_part = bc_conv[:, :STATE_DIM]
    c_part = bc_conv[:, STATE_DIM:]
    mamba_heads = dt_bias.shape[0]
    step = jax.nn.softplus(dt_in + dt_bias[None, :])
    decay = jnp.exp(-jnp.exp(a_log)[None, :] * step)
    x_heads = x_conv.reshape(req_count, mamba_heads, MHEAD_DIM)
    state = ssm_state.reshape(req_count, mamba_heads, MHEAD_DIM, STATE_DIM)
    state_new = (
        decay[:, :, None, None] * state
        + (step[:, :, None] * x_heads)[..., None] * b_part[:, None, None, :]
    )
    y_heads = (
        jnp.sum(state_new * c_part[:, None, None, :], axis=-1) + skip_gain[None, :, None] * x_heads
    )
    y_flat = y_heads.reshape(req_count, mamba_heads * MHEAD_DIM)
    gated = y_flat * jax.nn.silu(z_in)
    y_part = jnp.sum(gated * gated, axis=-1)
    y_pad = (-req_count) % 128
    y_msg = jnp.concatenate([y_part, jnp.zeros((y_pad,), jnp.float32)])[None, :]
    (y_all,) = exchange([y_msg], "mdl", n_mdl, 3)
    y_squares = jnp.sum(y_all[:, :req_count], axis=0)
    y_inverse = lax.rsqrt(y_squares / (MHEADS * MHEAD_DIM) + 1e-05)
    mixed = (gated * y_inverse[:, None] * out_gain.astype(jnp.float32)[None, :]).astype(
        jnp.bfloat16
    )
    return (hidden, mixed)


def solution(mesh):
    return jax.shard_map(
        functools.partial(shards, mesh.shape["req"], mesh.shape["mdl"]),
        mesh=mesh,
        in_specs=(
            P("req", "mdl"),
            P("req", "mdl"),
            P("req", "mdl"),
            P("req", None, "mdl"),
            P("req", None, "mdl"),
            P("req", "mdl"),
            P("req", "mdl"),
            P(),
            P("req", None),
            P("mdl", None),
            P("req", "mdl"),
            P(),
            P(None, "mdl"),
            P(),
            P(None, "mdl"),
            P(None, "mdl"),
            P("mdl"),
            P("mdl"),
            P("mdl"),
            P(None, "mdl"),
            P(),
            P("req", None, "mdl"),
            P("req", None, None),
            P("req", "mdl", None),
            P("mdl"),
        ),
        out_specs=(P("req", "mdl"), P("req", "mdl")),
        check_vma=False,
    )
```

```python
import functools
import math

import jax
import jax.numpy as jnp
from jax import lax
from jax.experimental import pallas as pl
from jax.experimental.pallas import tpu as pltpu
from jax.sharding import PartitionSpec as P

MODEL_WIDTH = 3584
HEAD_DIM = 224
MHEADS = 56
MHEAD_DIM = 64
STATE_DIM = 64
SHORT_MAX = 32
PAGE_SIZE = 16

MESH_ID = pl.DeviceIdType.MESH


def exchange_kernel(n, axis, count, *refs):
    x_refs = refs[:count]
    out_refs = refs[count : 2 * count]
    lands = refs[2 * count : 3 * count]
    send_sems, recv_sems = refs[3 * count :]
    me = lax.axis_index(axis)
    barrier = pltpu.get_barrier_semaphore()
    for j in range(1, n):
        peer = lax.rem(me + j, n)
        pl.semaphore_signal(barrier, inc=1, device_id={axis: peer}, device_id_type=MESH_ID)
    pl.semaphore_wait(barrier, n - 1)
    copies = []
    for k in range(count):
        rows = len(x_refs[k].shape) == 2 and x_refs[k].shape[0] == 1
        slot = lands[k].at[pl.ds(me, 1)] if rows else lands[k].at[me]
        for j in range(1, n):
            peer = lax.rem(me + j, n)
            copy = pltpu.make_async_remote_copy(
                src_ref=x_refs[k],
                dst_ref=slot,
                send_sem=send_sems.at[k, j - 1],
                recv_sem=recv_sems.at[k, j - 1],
                device_id={axis: peer},
                device_id_type=MESH_ID,
            )
            copy.start()
            copies.append(copy)
    for copy in copies:
        copy.wait()
    for k in range(count):
        rows = len(x_refs[k].shape) == 2 and x_refs[k].shape[0] == 1
        if rows:
            lands[k][pl.ds(me, 1), :] = x_refs[k][...]
        else:
            lands[k][me] = x_refs[k][...]
        out_refs[k][...] = lands[k][...]


def exchange(xs, axis, n, cid):
    shapes = []
    for x in xs:
        rows = x.ndim == 2 and x.shape[0] == 1
        shapes.append(jax.ShapeDtypeStruct((n, x.shape[1]) if rows else (n,) + x.shape, x.dtype))
    count = len(xs)
    return pl.pallas_call(
        functools.partial(exchange_kernel, n, axis, count),
        out_shape=tuple(shapes),
        in_specs=[pl.BlockSpec(memory_space=pltpu.VMEM)] * count,
        out_specs=tuple([pl.BlockSpec(memory_space=pltpu.VMEM)] * count),
        scratch_shapes=[pltpu.VMEM(s.shape, s.dtype) for s in shapes]
        + [pltpu.SemaphoreType.DMA((count, n - 1)), pltpu.SemaphoreType.DMA((count, n - 1))],
        compiler_params=pltpu.CompilerParams(collective_id=cid, has_side_effects=True),
    )(*xs)


def by_head(values, head_mask):
    out = jnp.zeros(values.shape[:-1] + (head_mask.shape[1],), values.dtype)
    for h in range(head_mask.shape[0]):
        out = jnp.where(head_mask[h], values[..., h : h + 1], out)
    return out


def pick_head(values, head_mask):
    out = values[..., 0, :]
    for h in range(1, head_mask.shape[0]):
        out = jnp.where(head_mask[h], values[..., h, :], out)
    return out


def attention_kernel(n, scale, cl_ref, lens_ref, bt_ref, q_ref, k_ref, v_ref, pk_hbm, pv_hbm,
                     lk_hbm, lv_hbm, out_ref, pk_ref, pv_ref, lk_ref, lv_ref, qsend, qland, psend,
                     pland, load_sems, send_sems, recv_sems):
    me = lax.axis_index("req")
    rows, cols = q_ref.shape
    tokens = pk_ref.shape[0]
    loads = []
    for i, (src, dst) in enumerate(((pk_hbm, pk_ref), (pv_hbm, pv_ref), (lk_hbm, lk_ref), (lv_hbm, lv_ref))):
        load = pltpu.make_async_copy(src, dst, load_sems.at[i])
        load.start()
        loads.append(load)
    barrier = pltpu.get_barrier_semaphore()
    for j in range(1, n):
        pl.semaphore_signal(barrier, inc=1, device_id={"req": lax.rem(me + j, n)}, device_id_type=MESH_ID)

    cl = cl_ref[...]
    longest = jnp.max(cl, axis=1, keepdims=True)
    where_long = jnp.where(cl == longest, lax.broadcasted_iota(jnp.int32, cl.shape, 1), cl.shape[1])
    long_row = jnp.min(where_long, axis=1, keepdims=True)
    owner = long_row // rows
    long_local = long_row - owner * rows
    lane = lax.broadcasted_iota(jnp.int32, (1, cols), 1)
    hm0 = lane < HEAD_DIM
    row_id = lax.broadcasted_iota(jnp.int32, (rows, 1), 0)
    q = q_ref[...]
    q32 = q.astype(jnp.float32)
    qsend[...] = jnp.sum(jnp.where(row_id == long_local, q32, 0.0), axis=0, keepdims=True)
    pl.semaphore_wait(barrier, n - 1)

    copies = []
    for j in range(1, n):
        copy = pltpu.make_async_remote_copy(
            src_ref=qsend, dst_ref=qland.at[pl.ds(me, 1)], send_sem=send_sems.at[0, j - 1],
            recv_sem=recv_sems.at[0, j - 1], device_id={"req": lax.rem(me + j, n)}, device_id_type=MESH_ID)
        copy.start()
        copies.append(copy)

    zero_q = jnp.zeros_like(q)
    qm = jnp.concatenate([jnp.where(hm0, q, zero_q), jnp.where(hm0, zero_q, q)], axis=0)
    nt = (((1,), (1,)), ((), ()))
    loads[0].wait()
    loads[1].wait()
    s = lax.dot_general(qm, pk_ref[...], nt, preferred_element_type=jnp.float32) * scale
    length = jnp.zeros((rows, 1), jnp.int32)
    page0 = jnp.zeros((rows, 1), jnp.int32)
    page1 = jnp.zeros((rows, 1), jnp.int32)
    for r in range(rows):
        length = jnp.where(row_id == r, lens_ref[me * rows + r], length)
        page0 = jnp.where(row_id == r, bt_ref[0, r] - me * tokens // PAGE_SIZE, page0)
        page1 = jnp.where(row_id == r, bt_ref[1, r] - me * tokens // PAGE_SIZE, page1)
    tok = lax.broadcasted_iota(jnp.int32, (1, tokens), 1)
    tpage = tok // PAGE_SIZE
    tslot = tok % PAGE_SIZE
    usable = ((tpage == page0) & (tslot < length)) | ((tpage == page1) & (tslot + PAGE_SIZE < length))
    usable = usable & (length <= SHORT_MAX)
    usable2 = jnp.concatenate([usable, usable], axis=0)
    s = jnp.where(usable2, s, -jnp.inf)
    prod = q32 * k_ref[...].astype(jnp.float32)
    own0 = jnp.sum(jnp.where(hm0, prod, 0.0), axis=1, keepdims=True)
    own1 = jnp.sum(jnp.where(hm0, 0.0, prod), axis=1, keepdims=True)
    own = jnp.concatenate([own0, own1], axis=0) * scale
    m_s = jnp.maximum(jnp.max(s, axis=1, keepdims=True), own)
    w = jnp.exp(s - m_s)
    ow = jnp.exp(own - m_s)
    tot_s = jnp.sum(w, axis=1, keepdims=True) + ow
    nm = jnp.dot(w.astype(jnp.bfloat16), pv_ref[...], preferred_element_type=jnp.float32)
    owb = ow.astype(jnp.bfloat16).astype(jnp.float32)
    numer = jnp.where(hm0, nm[:rows], nm[rows:]) + jnp.where(
        hm0, owb[:rows], owb[rows:]) * v_ref[...].astype(jnp.float32)

    for copy in copies:
        copy.wait()
    qland[pl.ds(me, 1), :] = qsend[...]
    src_id = lax.broadcasted_iota(jnp.int32, (n, 1), 0)
    lq = jnp.sum(jnp.where(src_id == owner, qland[...], 0.0), axis=0, keepdims=True)
    lq = lq.astype(jnp.bfloat16)
    zero_l = jnp.zeros_like(lq)
    lqm = jnp.concatenate([jnp.where(hm0, lq, zero_l), jnp.where(hm0, zero_l, lq)], axis=0)
    loads[2].wait()
    loads[3].wait()
    ls = jnp.dot(lqm, lk_ref[...], preferred_element_type=jnp.float32) * scale
    m_l = jnp.max(ls, axis=1, keepdims=True)
    lw = jnp.exp(ls - m_l)
    l_l = jnp.sum(lw, axis=1, keepdims=True)
    acc = lax.dot_general(lw.astype(jnp.bfloat16), lv_ref[...], nt, preferred_element_type=jnp.float32)
    acc_row = jnp.where(hm0, acc[0:1], acc[1:2])
    width = psend.shape[1]
    psend[...] = jnp.zeros((1, width), jnp.float32)
    psend[:, 0:cols] = acc_row
    t = lax.broadcasted_iota(jnp.int32, (1, 128), 1)
    tail = jnp.where(t == 0, m_l[0:1], jnp.where(t == 1, m_l[1:2], jnp.where(
        t == 2, l_l[0:1], jnp.where(t == 3, l_l[1:2], 0.0))))
    psend[:, width - 128 : width] = tail

    copies = []
    for j in range(1, n):
        copy = pltpu.make_async_remote_copy(
            src_ref=psend, dst_ref=pland.at[pl.ds(me, 1)], send_sem=send_sems.at[1, j - 1],
            recv_sem=recv_sems.at[1, j - 1], device_id={"req": lax.rem(me + j, n)}, device_id_type=MESH_ID)
        copy.start()
        copies.append(copy)
    for copy in copies:
        copy.wait()
    pland[pl.ds(me, 1), :] = psend[...]

    parts = pland[...]
    base = width - 128
    sums_all = parts[:, 0:cols]
    whole = []
    for h in range(2):
        mh = parts[:, base + h : base + h + 1]
        lh = parts[:, base + 2 + h : base + 3 + h]
        wm = jnp.max(mh, axis=0, keepdims=True)
        keep = jnp.exp(mh - wm)
        wt = jnp.sum(lh * keep, axis=0, keepdims=True)
        ws = jnp.sum(sums_all * keep, axis=0, keepdims=True)
        whole.append((wm, wt, ws))
    whole_sums = jnp.where(hm0, whole[0][2], whole[1][2])
    chosen = (row_id == long_local) & (me == owner)
    kl, kg, tt = [], [], []
    for h in range(2):
        mh = m_s[h * rows : (h + 1) * rows]
        top = jnp.where(chosen, jnp.maximum(mh, whole[h][0]), mh)
        klh = jnp.exp(mh - top)
        kgh = jnp.where(chosen, jnp.exp(whole[h][0] - top), 0.0)
        kl.append(klh)
        kg.append(kgh)
        tt.append(tot_s[h * rows : (h + 1) * rows] * klh + kgh * whole[h][1])
    numer = numer * jnp.where(hm0, kl[0], kl[1]) + jnp.where(hm0, kg[0], kg[1]) * whole_sums
    out_ref[...] = (numer / jnp.where(hm0, tt[0], tt[1])).astype(out_ref.dtype)


def attention(n, cache_lengths, block_table, query, new_key, new_value, page_k, page_v, long_keys,
              long_values):
    scale = 1.0 / math.sqrt(HEAD_DIM)
    cols = query.shape[1]
    width = -(-cols // 128) * 128 + 128
    vmem = pl.BlockSpec(memory_space=pltpu.VMEM)
    smem = pl.BlockSpec(memory_space=pltpu.SMEM)
    anywhere = pl.BlockSpec(memory_space=pl.ANY)
    return pl.pallas_call(
        functools.partial(attention_kernel, n, scale),
        out_shape=jax.ShapeDtypeStruct(query.shape, jnp.bfloat16),
        in_specs=[vmem, smem, smem, vmem, vmem, vmem] + [anywhere] * 4,
        out_specs=vmem,
        scratch_shapes=[
            pltpu.VMEM(page_k.shape, page_k.dtype),
            pltpu.VMEM(page_v.shape, page_v.dtype),
            pltpu.VMEM(long_keys.shape[::-1], long_keys.dtype),
            pltpu.VMEM(long_values.shape[::-1], long_values.dtype),
            pltpu.VMEM((1, cols), jnp.float32),
            pltpu.VMEM((n, cols), jnp.float32),
            pltpu.VMEM((1, width), jnp.float32),
            pltpu.VMEM((n, width), jnp.float32),
            pltpu.SemaphoreType.DMA((4,)),
            pltpu.SemaphoreType.DMA((2, n - 1)),
            pltpu.SemaphoreType.DMA((2, n - 1)),
        ],
        compiler_params=pltpu.CompilerParams(collective_id=0, has_side_effects=True),
    )(
        cache_lengths.reshape(1, -1),
        cache_lengths,
        block_table.T,
        query,
        new_key,
        new_value,
        page_k,
        page_v,
        long_keys.T,
        long_values.T,
    )


def shards(
    n_req,
    n_mdl,
    query,
    new_key,
    new_value,
    page_keys,
    page_values,
    long_keys,
    long_values,
    cache_lengths,
    block_table,
    out_weight,
    residual,
    norm_gain,
    x_weight,
    bc_weight,
    dt_weight,
    z_weight,
    dt_bias,
    a_log,
    skip_gain,
    conv_x_weight,
    conv_bc_weight,
    conv_x_state,
    conv_bc_state,
    ssm_state,
    out_gain,
):
    req_count = query.shape[0]
    local_cols = query.shape[1]
    heads_here = local_cols // HEAD_DIM
    scale = 1.0 / math.sqrt(HEAD_DIM)
    device = lax.axis_index("req")
    pages_here = page_keys.shape[0]
    long_row = jnp.argmax(cache_lengths)
    owner = long_row // req_count
    long_local = long_row % req_count

    assert heads_here == 2
    tokens_here = pages_here * PAGE_SIZE
    attended = attention(
        n_req,
        cache_lengths,
        block_table,
        query,
        new_key,
        new_value,
        page_keys.reshape(tokens_here, local_cols),
        page_values.reshape(tokens_here, local_cols),
        long_keys,
        long_values,
    )

    projected = jnp.dot(attended, out_weight, preferred_element_type=jnp.float32)
    feature_cols = residual.shape[1]
    feature_start = lax.axis_index("mdl") * feature_cols
    partials, residuals = exchange([projected.astype(jnp.bfloat16), residual], "mdl", n_mdl, 2)
    residual_all = jnp.transpose(residuals, (1, 0, 2)).reshape(req_count, n_mdl * feature_cols)
    summed = jnp.sum(partials.astype(jnp.float32), axis=0)
    hidden_all = (residual_all.astype(jnp.float32) + summed).astype(jnp.bfloat16)
    hidden = lax.dynamic_slice_in_dim(hidden_all, feature_start, feature_cols, 1)
    hidden_f = hidden_all.astype(jnp.float32)
    squares = jnp.sum(hidden_f * hidden_f, axis=-1)
    inverse = lax.rsqrt(squares / MODEL_WIDTH + 1e-05)
    normed = (hidden_f * inverse[:, None] * norm_gain.astype(jnp.float32)[None, :]).astype(
        jnp.bfloat16
    )

    x_in = jnp.dot(normed, x_weight, preferred_element_type=jnp.float32)
    bc_in = jnp.dot(normed, bc_weight, preferred_element_type=jnp.float32)
    dt_in = jnp.dot(normed, dt_weight, preferred_element_type=jnp.float32)
    z_in = jnp.dot(normed, z_weight, preferred_element_type=jnp.float32)
    window_x = jnp.concatenate([conv_x_state.astype(jnp.float32), x_in[:, None, :]], axis=1)
    x_conv = jax.nn.silu(jnp.sum(window_x * conv_x_weight.astype(jnp.float32)[None], axis=1))
    window_bc = jnp.concatenate([conv_bc_state.astype(jnp.float32), bc_in[:, None, :]], axis=1)
    bc_conv = jax.nn.silu(jnp.sum(window_bc * conv_bc_weight.astype(jnp.float32)[None], axis=1))
    b_part = bc_conv[:, :STATE_DIM]
    c_part = bc_conv[:, STATE_DIM:]
    mamba_heads = dt_bias.shape[0]
    step = jax.nn.softplus(dt_in + dt_bias[None, :])
    decay = jnp.exp(-jnp.exp(a_log)[None, :] * step)
    x_heads = x_conv.reshape(req_count, mamba_heads, MHEAD_DIM)
    c_tiled = jnp.tile(c_part, (1, MHEAD_DIM))
    group = (
        jnp.arange(MHEAD_DIM * STATE_DIM, dtype=jnp.int32)[:, None] // STATE_DIM
        == jnp.arange(MHEAD_DIM, dtype=jnp.int32)[None, :]
    ).astype(jnp.float32)
    state_c = jnp.einsum(
        "rhk,kp->rhp",
        ssm_state * c_tiled[:, None, :],
        group,
        precision=lax.Precision.HIGHEST,
        preferred_element_type=jnp.float32,
    )
    b_dot_c = jnp.sum(b_part * c_part, axis=-1)
    y_heads = (
        decay[:, :, None] * state_c
        + (step * b_dot_c[:, None])[:, :, None] * x_heads
        + skip_gain[None, :, None] * x_heads
    )
    y_flat = y_heads.reshape(req_count, mamba_heads * MHEAD_DIM)
    gated = y_flat * jax.nn.silu(z_in)
    y_part = jnp.sum(gated * gated, axis=-1)
    y_pad = (-req_count) % 128
    y_msg = jnp.concatenate([y_part, jnp.zeros((y_pad,), jnp.float32)])[None, :]
    (y_all,) = exchange([y_msg], "mdl", n_mdl, 3)
    y_squares = jnp.sum(y_all[:, :req_count], axis=0)
    y_inverse = lax.rsqrt(y_squares / (MHEADS * MHEAD_DIM) + 1e-05)
    mixed = (gated * y_inverse[:, None] * out_gain.astype(jnp.float32)[None, :]).astype(
        jnp.bfloat16
    )
    return (hidden, mixed)


def solution(mesh):
    return jax.shard_map(
        functools.partial(shards, mesh.shape["req"], mesh.shape["mdl"]),
        mesh=mesh,
        in_specs=(
            P("req", "mdl"),
            P("req", "mdl"),
            P("req", "mdl"),
            P("req", None, "mdl"),
            P("req", None, "mdl"),
            P("req", "mdl"),
            P("req", "mdl"),
            P(),
            P("req", None),
            P("mdl", None),
            P("req", "mdl"),
            P(),
            P(None, "mdl"),
            P(),
            P(None, "mdl"),
            P(None, "mdl"),
            P("mdl"),
            P("mdl"),
            P("mdl"),
            P(None, "mdl"),
            P(),
            P("req", None, "mdl"),
            P("req", None, None),
            P("req", "mdl", None),
            P("mdl"),
        ),
        out_specs=(P("req", "mdl"), P("req", "mdl")),
        check_vma=False,
    )
```

```python
import functools
import math

import jax
import jax.numpy as jnp
from jax import lax
from jax.experimental import pallas as pl
from jax.experimental.pallas import tpu as pltpu
from jax.sharding import PartitionSpec as P

MODEL_WIDTH = 3584
HEAD_DIM = 224
MHEADS = 56
MHEAD_DIM = 64
STATE_DIM = 64
SHORT_MAX = 32
PAGE_SIZE = 16

MESH_ID = pl.DeviceIdType.MESH


def exchange_kernel(n, axis, count, *refs):
    x_refs = refs[:count]
    out_refs = refs[count : 2 * count]
    lands = refs[2 * count : 3 * count]
    send_sems, recv_sems = refs[3 * count :]
    me = lax.axis_index(axis)
    barrier = pltpu.get_barrier_semaphore()
    for j in range(1, n):
        peer = lax.rem(me + j, n)
        pl.semaphore_signal(barrier, inc=1, device_id={axis: peer}, device_id_type=MESH_ID)
    pl.semaphore_wait(barrier, n - 1)
    copies = []
    for k in range(count):
        rows = len(x_refs[k].shape) == 2 and x_refs[k].shape[0] == 1
        slot = lands[k].at[pl.ds(me, 1)] if rows else lands[k].at[me]
        for j in range(1, n):
            peer = lax.rem(me + j, n)
            copy = pltpu.make_async_remote_copy(
                src_ref=x_refs[k],
                dst_ref=slot,
                send_sem=send_sems.at[k, j - 1],
                recv_sem=recv_sems.at[k, j - 1],
                device_id={axis: peer},
                device_id_type=MESH_ID,
            )
            copy.start()
            copies.append(copy)
    for copy in copies:
        copy.wait()
    for k in range(count):
        rows = len(x_refs[k].shape) == 2 and x_refs[k].shape[0] == 1
        if rows:
            lands[k][pl.ds(me, 1), :] = x_refs[k][...]
        else:
            lands[k][me] = x_refs[k][...]
        out_refs[k][...] = lands[k][...]


def exchange(xs, axis, n, cid):
    shapes = []
    for x in xs:
        rows = x.ndim == 2 and x.shape[0] == 1
        shapes.append(jax.ShapeDtypeStruct((n, x.shape[1]) if rows else (n,) + x.shape, x.dtype))
    count = len(xs)
    return pl.pallas_call(
        functools.partial(exchange_kernel, n, axis, count),
        out_shape=tuple(shapes),
        in_specs=[pl.BlockSpec(memory_space=pltpu.VMEM)] * count,
        out_specs=tuple([pl.BlockSpec(memory_space=pltpu.VMEM)] * count),
        scratch_shapes=[pltpu.VMEM(s.shape, s.dtype) for s in shapes]
        + [pltpu.SemaphoreType.DMA((count, n - 1)), pltpu.SemaphoreType.DMA((count, n - 1))],
        compiler_params=pltpu.CompilerParams(collective_id=cid, has_side_effects=True),
    )(*xs)


def by_head(values, head_mask):
    out = jnp.zeros(values.shape[:-1] + (head_mask.shape[1],), values.dtype)
    for h in range(head_mask.shape[0]):
        out = jnp.where(head_mask[h], values[..., h : h + 1], out)
    return out


def pick_head(values, head_mask):
    out = values[..., 0, :]
    for h in range(1, head_mask.shape[0]):
        out = jnp.where(head_mask[h], values[..., h, :], out)
    return out


def attention_kernel(n, scale, cl_ref, lens_ref, bt_ref, q_ref, k_ref, v_ref, pk_hbm, pv_hbm,
                     lk_hbm, lv_hbm, out_ref, pk_ref, pv_ref, lk_ref, lv_ref, qsend, qland, psend,
                     pland, load_sems, send_sems, recv_sems):
    me = lax.axis_index("req")
    rows, cols = q_ref.shape
    tokens = pk_ref.shape[0]
    loads = []
    for i, (src, dst) in enumerate(((pk_hbm, pk_ref), (pv_hbm, pv_ref), (lk_hbm, lk_ref), (lv_hbm, lv_ref))):
        load = pltpu.make_async_copy(src, dst, load_sems.at[i])
        load.start()
        loads.append(load)
    barrier = pltpu.get_barrier_semaphore()
    for j in range(1, n):
        pl.semaphore_signal(barrier, inc=1, device_id={"req": lax.rem(me + j, n)}, device_id_type=MESH_ID)

    cl = cl_ref[...]
    longest = jnp.max(cl, axis=1, keepdims=True)
    where_long = jnp.where(cl == longest, lax.broadcasted_iota(jnp.int32, cl.shape, 1), cl.shape[1])
    long_row = jnp.min(where_long, axis=1, keepdims=True)
    owner = long_row // rows
    long_local = long_row - owner * rows
    lane = lax.broadcasted_iota(jnp.int32, (1, cols), 1)
    hm0 = lane < HEAD_DIM
    row_id = lax.broadcasted_iota(jnp.int32, (rows, 1), 0)
    q = q_ref[...]
    q32 = q.astype(jnp.float32)
    qsend[...] = jnp.sum(jnp.where(row_id == long_local, q32, 0.0), axis=0, keepdims=True)
    pl.semaphore_wait(barrier, n - 1)

    copies = []
    for j in range(1, n):
        copy = pltpu.make_async_remote_copy(
            src_ref=qsend, dst_ref=qland.at[pl.ds(me, 1)], send_sem=send_sems.at[0, j - 1],
            recv_sem=recv_sems.at[0, j - 1], device_id={"req": lax.rem(me + j, n)}, device_id_type=MESH_ID)
        copy.start()
        copies.append(copy)

    zero_q = jnp.zeros_like(q)
    qm = jnp.concatenate([jnp.where(hm0, q, zero_q), jnp.where(hm0, zero_q, q)], axis=0)
    nt = (((1,), (1,)), ((), ()))
    loads[0].wait()
    loads[1].wait()
    s = lax.dot_general(qm, pk_ref[...], nt, preferred_element_type=jnp.float32) * scale
    length = jnp.zeros((rows, 1), jnp.int32)
    page0 = jnp.zeros((rows, 1), jnp.int32)
    page1 = jnp.zeros((rows, 1), jnp.int32)
    for r in range(rows):
        length = jnp.where(row_id == r, lens_ref[me * rows + r], length)
        page0 = jnp.where(row_id == r, bt_ref[0, r] - me * tokens // PAGE_SIZE, page0)
        page1 = jnp.where(row_id == r, bt_ref[1, r] - me * tokens // PAGE_SIZE, page1)
    tok = lax.broadcasted_iota(jnp.int32, (1, tokens), 1)
    tpage = tok // PAGE_SIZE
    tslot = tok % PAGE_SIZE
    usable = ((tpage == page0) & (tslot < length)) | ((tpage == page1) & (tslot + PAGE_SIZE < length))
    usable = usable & (length <= SHORT_MAX)
    usable2 = jnp.concatenate([usable, usable], axis=0)
    s = jnp.where(usable2, s, -jnp.inf)
    prod = q32 * k_ref[...].astype(jnp.float32)
    own0 = jnp.sum(jnp.where(hm0, prod, 0.0), axis=1, keepdims=True)
    own1 = jnp.sum(jnp.where(hm0, 0.0, prod), axis=1, keepdims=True)
    own = jnp.concatenate([own0, own1], axis=0) * scale
    m_s = jnp.maximum(jnp.max(s, axis=1, keepdims=True), own)
    w = jnp.exp(s - m_s)
    ow = jnp.exp(own - m_s)
    tot_s = jnp.sum(w, axis=1, keepdims=True) + ow
    nm = jnp.dot(w.astype(jnp.bfloat16), pv_ref[...], preferred_element_type=jnp.float32)
    owb = ow.astype(jnp.bfloat16).astype(jnp.float32)
    numer = jnp.where(hm0, nm[:rows], nm[rows:]) + jnp.where(
        hm0, owb[:rows], owb[rows:]) * v_ref[...].astype(jnp.float32)

    for copy in copies:
        copy.wait()
    qland[pl.ds(me, 1), :] = qsend[...]
    src_id = lax.broadcasted_iota(jnp.int32, (n, 1), 0)
    lq = jnp.sum(jnp.where(src_id == owner, qland[...], 0.0), axis=0, keepdims=True)
    lq = lq.astype(jnp.bfloat16)
    zero_l = jnp.zeros_like(lq)
    lqm = jnp.concatenate([jnp.where(hm0, lq, zero_l), jnp.where(hm0, zero_l, lq)], axis=0)
    loads[2].wait()
    loads[3].wait()
    ls = jnp.dot(lqm, lk_ref[...], preferred_element_type=jnp.float32) * scale
    m_l = jnp.max(ls, axis=1, keepdims=True)
    lw = jnp.exp(ls - m_l)
    l_l = jnp.sum(lw, axis=1, keepdims=True)
    acc = lax.dot_general(lw.astype(jnp.bfloat16), lv_ref[...], nt, preferred_element_type=jnp.float32)
    acc_row = jnp.where(hm0, acc[0:1], acc[1:2])
    width = psend.shape[1]
    psend[...] = jnp.zeros((1, width), jnp.float32)
    psend[:, 0:cols] = acc_row
    t = lax.broadcasted_iota(jnp.int32, (1, 128), 1)
    tail = jnp.where(t == 0, m_l[0:1], jnp.where(t == 1, m_l[1:2], jnp.where(
        t == 2, l_l[0:1], jnp.where(t == 3, l_l[1:2], 0.0))))
    psend[:, width - 128 : width] = tail

    copies = []
    for j in range(1, n):
        copy = pltpu.make_async_remote_copy(
            src_ref=psend, dst_ref=pland.at[pl.ds(me, 1)], send_sem=send_sems.at[1, j - 1],
            recv_sem=recv_sems.at[1, j - 1], device_id={"req": lax.rem(me + j, n)}, device_id_type=MESH_ID)
        copy.start()
        copies.append(copy)
    for copy in copies:
        copy.wait()
    pland[pl.ds(me, 1), :] = psend[...]

    parts = pland[...]
    base = width - 128
    sums_all = parts[:, 0:cols]
    whole = []
    for h in range(2):
        mh = parts[:, base + h : base + h + 1]
        lh = parts[:, base + 2 + h : base + 3 + h]
        wm = jnp.max(mh, axis=0, keepdims=True)
        keep = jnp.exp(mh - wm)
        wt = jnp.sum(lh * keep, axis=0, keepdims=True)
        ws = jnp.sum(sums_all * keep, axis=0, keepdims=True)
        whole.append((wm, wt, ws))
    whole_sums = jnp.where(hm0, whole[0][2], whole[1][2])
    chosen = (row_id == long_local) & (me == owner)
    kl, kg, tt = [], [], []
    for h in range(2):
        mh = m_s[h * rows : (h + 1) * rows]
        top = jnp.where(chosen, jnp.maximum(mh, whole[h][0]), mh)
        klh = jnp.exp(mh - top)
        kgh = jnp.where(chosen, jnp.exp(whole[h][0] - top), 0.0)
        kl.append(klh)
        kg.append(kgh)
        tt.append(tot_s[h * rows : (h + 1) * rows] * klh + kgh * whole[h][1])
    numer = numer * jnp.where(hm0, kl[0], kl[1]) + jnp.where(hm0, kg[0], kg[1]) * whole_sums
    out_ref[...] = (numer / jnp.where(hm0, tt[0], tt[1])).astype(out_ref.dtype)


def attention(n, cache_lengths, block_table, query, new_key, new_value, page_k, page_v, long_keys,
              long_values):
    scale = 1.0 / math.sqrt(HEAD_DIM)
    cols = query.shape[1]
    width = -(-cols // 128) * 128 + 128
    vmem = pl.BlockSpec(memory_space=pltpu.VMEM)
    smem = pl.BlockSpec(memory_space=pltpu.SMEM)
    anywhere = pl.BlockSpec(memory_space=pl.ANY)
    return pl.pallas_call(
        functools.partial(attention_kernel, n, scale),
        out_shape=jax.ShapeDtypeStruct(query.shape, jnp.bfloat16),
        in_specs=[vmem, smem, smem, vmem, vmem, vmem] + [anywhere] * 4,
        out_specs=vmem,
        scratch_shapes=[
            pltpu.VMEM(page_k.shape, page_k.dtype),
            pltpu.VMEM(page_v.shape, page_v.dtype),
            pltpu.VMEM(long_keys.shape[::-1], long_keys.dtype),
            pltpu.VMEM(long_values.shape[::-1], long_values.dtype),
            pltpu.VMEM((1, cols), jnp.float32),
            pltpu.VMEM((n, cols), jnp.float32),
            pltpu.VMEM((1, width), jnp.float32),
            pltpu.VMEM((n, width), jnp.float32),
            pltpu.SemaphoreType.DMA((4,)),
            pltpu.SemaphoreType.DMA((2, n - 1)),
            pltpu.SemaphoreType.DMA((2, n - 1)),
        ],
        compiler_params=pltpu.CompilerParams(collective_id=0, has_side_effects=True),
    )(
        cache_lengths.reshape(1, -1),
        cache_lengths,
        block_table.T,
        query,
        new_key,
        new_value,
        page_k,
        page_v,
        long_keys.T,
        long_values.T,
    )


def barrier_all(n, axis, me):
    barrier = pltpu.get_barrier_semaphore()
    for j in range(1, n):
        pl.semaphore_signal(barrier, inc=1, device_id={axis: lax.rem(me + j, n)}, device_id_type=MESH_ID)
    pl.semaphore_wait(barrier, n - 1)


def send_all(n, axis, me, pairs, send_sems, recv_sems):
    copies = []
    for k, (src, land) in enumerate(pairs):
        for j in range(1, n):
            copy = pltpu.make_async_remote_copy(
                src_ref=src, dst_ref=land.at[me], send_sem=send_sems.at[k, j - 1],
                recv_sem=recv_sems.at[k, j - 1], device_id={axis: lax.rem(me + j, n)},
                device_id_type=MESH_ID)
            copy.start()
            copies.append(copy)
    for copy in copies:
        copy.wait()
    for src, land in pairs:
        land[me] = src[...]


def norm_kernel(n, p_ref, r_ref, g_ref, hidden_ref, normed_ref, p_land, r_land, send_sems, recv_sems):
    me = lax.axis_index("mdl")
    barrier_all(n, "mdl", me)
    send_all(n, "mdl", me, ((p_ref, p_land), (r_ref, r_land)), send_sems, recv_sems)
    cols = r_ref.shape[1]
    summed = p_land[0].astype(jnp.float32)
    for j in range(1, n):
        summed = summed + p_land[j].astype(jnp.float32)
    residual_all = jnp.concatenate([r_land[j] for j in range(n)], axis=1).astype(jnp.float32)
    hidden_all = (residual_all + summed).astype(jnp.bfloat16)
    hidden_f = hidden_all.astype(jnp.float32)
    squares = jnp.sum(hidden_f * hidden_f, axis=1, keepdims=True)
    inverse = lax.rsqrt(squares / MODEL_WIDTH + 1e-05)
    normed_ref[...] = (hidden_f * inverse * g_ref[...].astype(jnp.float32)).astype(normed_ref.dtype)
    own = jnp.zeros(hidden_ref.shape, jnp.float32)
    for j in range(n):
        own = jnp.where(me == j, hidden_f[:, j * cols : (j + 1) * cols], own)
    hidden_ref[...] = own.astype(hidden_ref.dtype)


def norm_exchange(n, projected, residual, norm_gain):
    rows, cols = residual.shape
    vmem = pl.BlockSpec(memory_space=pltpu.VMEM)
    return pl.pallas_call(
        functools.partial(norm_kernel, n),
        out_shape=(
            jax.ShapeDtypeStruct(residual.shape, jnp.bfloat16),
            jax.ShapeDtypeStruct(projected.shape, jnp.bfloat16),
        ),
        in_specs=[vmem] * 3,
        out_specs=(vmem, vmem),
        scratch_shapes=[
            pltpu.VMEM((n,) + projected.shape, projected.dtype),
            pltpu.VMEM((n,) + residual.shape, residual.dtype),
            pltpu.SemaphoreType.DMA((2, n - 1)),
            pltpu.SemaphoreType.DMA((2, n - 1)),
        ],
        compiler_params=pltpu.CompilerParams(collective_id=2, has_side_effects=True),
    )(projected, residual, norm_gain.reshape(1, -1))


def mix_kernel(n, width, g_ref, gain_ref, mixed_ref, msg, land, send_sems, recv_sems):
    me = lax.axis_index("mdl")
    gated = g_ref[...]
    msg[...] = jnp.broadcast_to(jnp.sum(gated * gated, axis=1, keepdims=True), msg.shape)
    barrier_all(n, "mdl", me)
    send_all(n, "mdl", me, ((msg, land),), send_sems, recv_sems)
    total = land[0]
    for j in range(1, n):
        total = total + land[j]
    inverse = lax.rsqrt(total[:, 0:1] / width + 1e-05)
    mixed_ref[...] = (gated * inverse * gain_ref[...].astype(jnp.float32)).astype(mixed_ref.dtype)


def mix_exchange(n, gated, out_gain, width):
    rows = gated.shape[0]
    vmem = pl.BlockSpec(memory_space=pltpu.VMEM)
    return pl.pallas_call(
        functools.partial(mix_kernel, n, width),
        out_shape=jax.ShapeDtypeStruct(gated.shape, jnp.bfloat16),
        in_specs=[vmem] * 2,
        out_specs=vmem,
        scratch_shapes=[
            pltpu.VMEM((rows, 128), jnp.float32),
            pltpu.VMEM((n, rows, 128), jnp.float32),
            pltpu.SemaphoreType.DMA((1, n - 1)),
            pltpu.SemaphoreType.DMA((1, n - 1)),
        ],
        compiler_params=pltpu.CompilerParams(collective_id=3, has_side_effects=True),
    )(gated, out_gain.reshape(1, -1))


def shards(
    n_req,
    n_mdl,
    query,
    new_key,
    new_value,
    page_keys,
    page_values,
    long_keys,
    long_values,
    cache_lengths,
    block_table,
    out_weight,
    residual,
    norm_gain,
    x_weight,
    bc_weight,
    dt_weight,
    z_weight,
    dt_bias,
    a_log,
    skip_gain,
    conv_x_weight,
    conv_bc_weight,
    conv_x_state,
    conv_bc_state,
    ssm_state,
    out_gain,
):
    req_count = query.shape[0]
    local_cols = query.shape[1]
    heads_here = local_cols // HEAD_DIM
    scale = 1.0 / math.sqrt(HEAD_DIM)
    device = lax.axis_index("req")
    pages_here = page_keys.shape[0]
    long_row = jnp.argmax(cache_lengths)
    owner = long_row // req_count
    long_local = long_row % req_count

    assert heads_here == 2
    tokens_here = pages_here * PAGE_SIZE
    attended = attention(
        n_req,
        cache_lengths,
        block_table,
        query,
        new_key,
        new_value,
        page_keys.reshape(tokens_here, local_cols),
        page_values.reshape(tokens_here, local_cols),
        long_keys,
        long_values,
    )

    projected = jnp.dot(attended, out_weight, preferred_element_type=jnp.float32)
    feature_cols = residual.shape[1]
    feature_start = lax.axis_index("mdl") * feature_cols
    hidden, normed = norm_exchange(n_mdl, projected.astype(jnp.bfloat16), residual, norm_gain)

    x_in = jnp.dot(normed, x_weight, preferred_element_type=jnp.float32)
    bc_in = jnp.dot(normed, bc_weight, preferred_element_type=jnp.float32)
    dt_in = jnp.dot(normed, dt_weight, preferred_element_type=jnp.float32)
    z_in = jnp.dot(normed, z_weight, preferred_element_type=jnp.float32)
    window_x = jnp.concatenate([conv_x_state.astype(jnp.float32), x_in[:, None, :]], axis=1)
    x_conv = jax.nn.silu(jnp.sum(window_x * conv_x_weight.astype(jnp.float32)[None], axis=1))
    window_bc = jnp.concatenate([conv_bc_state.astype(jnp.float32), bc_in[:, None, :]], axis=1)
    bc_conv = jax.nn.silu(jnp.sum(window_bc * conv_bc_weight.astype(jnp.float32)[None], axis=1))
    b_part = bc_conv[:, :STATE_DIM]
    c_part = bc_conv[:, STATE_DIM:]
    mamba_heads = dt_bias.shape[0]
    step = jax.nn.softplus(dt_in + dt_bias[None, :])
    decay = jnp.exp(-jnp.exp(a_log)[None, :] * step)
    x_heads = x_conv.reshape(req_count, mamba_heads, MHEAD_DIM)
    state = ssm_state.reshape(req_count, mamba_heads, MHEAD_DIM, STATE_DIM)
    state_new = (
        decay[:, :, None, None] * state
        + (step[:, :, None] * x_heads)[..., None] * b_part[:, None, None, :]
    )
    y_heads = (
        jnp.sum(state_new * c_part[:, None, None, :], axis=-1) + skip_gain[None, :, None] * x_heads
    )
    y_flat = y_heads.reshape(req_count, mamba_heads * MHEAD_DIM)
    gated = y_flat * jax.nn.silu(z_in)
    mixed = mix_exchange(n_mdl, gated, out_gain, MHEADS * MHEAD_DIM)
    return (hidden, mixed)


def solution(mesh):
    return jax.shard_map(
        functools.partial(shards, mesh.shape["req"], mesh.shape["mdl"]),
        mesh=mesh,
        in_specs=(
            P("req", "mdl"),
            P("req", "mdl"),
            P("req", "mdl"),
            P("req", None, "mdl"),
            P("req", None, "mdl"),
            P("req", "mdl"),
            P("req", "mdl"),
            P(),
            P("req", None),
            P("mdl", None),
            P("req", "mdl"),
            P(),
            P(None, "mdl"),
            P(),
            P(None, "mdl"),
            P(None, "mdl"),
            P("mdl"),
            P("mdl"),
            P("mdl"),
            P(None, "mdl"),
            P(),
            P("req", None, "mdl"),
            P("req", None, None),
            P("req", "mdl", None),
            P("mdl"),
        ),
        out_specs=(P("req", "mdl"), P("req", "mdl")),
        check_vma=False,
    )
```

```python
import functools
import math

import jax
import jax.numpy as jnp
from jax import lax
from jax.experimental import pallas as pl
from jax.experimental.pallas import tpu as pltpu
from jax.sharding import PartitionSpec as P

MODEL_WIDTH = 3584
HEAD_DIM = 224
MHEADS = 56
MHEAD_DIM = 64
STATE_DIM = 64
SHORT_MAX = 32
PAGE_SIZE = 16

MESH_ID = pl.DeviceIdType.MESH


def exchange_kernel(n, axis, count, *refs):
    x_refs = refs[:count]
    out_refs = refs[count : 2 * count]
    lands = refs[2 * count : 3 * count]
    send_sems, recv_sems = refs[3 * count :]
    me = lax.axis_index(axis)
    barrier = pltpu.get_barrier_semaphore()
    for j in range(1, n):
        peer = lax.rem(me + j, n)
        pl.semaphore_signal(barrier, inc=1, device_id={axis: peer}, device_id_type=MESH_ID)
    pl.semaphore_wait(barrier, n - 1)
    copies = []
    for k in range(count):
        rows = len(x_refs[k].shape) == 2 and x_refs[k].shape[0] == 1
        slot = lands[k].at[pl.ds(me, 1)] if rows else lands[k].at[me]
        for j in range(1, n):
            peer = lax.rem(me + j, n)
            copy = pltpu.make_async_remote_copy(
                src_ref=x_refs[k],
                dst_ref=slot,
                send_sem=send_sems.at[k, j - 1],
                recv_sem=recv_sems.at[k, j - 1],
                device_id={axis: peer},
                device_id_type=MESH_ID,
            )
            copy.start()
            copies.append(copy)
    for copy in copies:
        copy.wait()
    for k in range(count):
        rows = len(x_refs[k].shape) == 2 and x_refs[k].shape[0] == 1
        if rows:
            lands[k][pl.ds(me, 1), :] = x_refs[k][...]
        else:
            lands[k][me] = x_refs[k][...]
        out_refs[k][...] = lands[k][...]


def exchange(xs, axis, n, cid):
    shapes = []
    for x in xs:
        rows = x.ndim == 2 and x.shape[0] == 1
        shapes.append(jax.ShapeDtypeStruct((n, x.shape[1]) if rows else (n,) + x.shape, x.dtype))
    count = len(xs)
    return pl.pallas_call(
        functools.partial(exchange_kernel, n, axis, count),
        out_shape=tuple(shapes),
        in_specs=[pl.BlockSpec(memory_space=pltpu.VMEM)] * count,
        out_specs=tuple([pl.BlockSpec(memory_space=pltpu.VMEM)] * count),
        scratch_shapes=[pltpu.VMEM(s.shape, s.dtype) for s in shapes]
        + [pltpu.SemaphoreType.DMA((count, n - 1)), pltpu.SemaphoreType.DMA((count, n - 1))],
        compiler_params=pltpu.CompilerParams(collective_id=cid, has_side_effects=True),
    )(*xs)


def by_head(values, head_mask):
    out = jnp.zeros(values.shape[:-1] + (head_mask.shape[1],), values.dtype)
    for h in range(head_mask.shape[0]):
        out = jnp.where(head_mask[h], values[..., h : h + 1], out)
    return out


def pick_head(values, head_mask):
    out = values[..., 0, :]
    for h in range(1, head_mask.shape[0]):
        out = jnp.where(head_mask[h], values[..., h, :], out)
    return out


def attention_kernel(n, scale, cl_ref, lens_ref, bt_ref, q_ref, k_ref, v_ref, pk_hbm, pv_hbm,
                     lk_hbm, lv_hbm, out_ref, pk_ref, pv_ref, lk_ref, lv_ref, qsend, qland, psend,
                     pland, load_sems, send_sems, recv_sems):
    me = lax.axis_index("req")
    rows, cols = q_ref.shape
    tokens = pk_ref.shape[0]
    loads = []
    for i, (src, dst) in enumerate(((pk_hbm, pk_ref), (pv_hbm, pv_ref), (lk_hbm, lk_ref), (lv_hbm, lv_ref))):
        load = pltpu.make_async_copy(src, dst, load_sems.at[i])
        load.start()
        loads.append(load)
    barrier = pltpu.get_barrier_semaphore()
    for j in range(1, n):
        pl.semaphore_signal(barrier, inc=1, device_id={"req": lax.rem(me + j, n)}, device_id_type=MESH_ID)

    cl = cl_ref[...]
    longest = jnp.max(cl, axis=1, keepdims=True)
    where_long = jnp.where(cl == longest, lax.broadcasted_iota(jnp.int32, cl.shape, 1), cl.shape[1])
    long_row = jnp.min(where_long, axis=1, keepdims=True)
    owner = long_row // rows
    long_local = long_row - owner * rows
    lane = lax.broadcasted_iota(jnp.int32, (1, cols), 1)
    hm0 = lane < HEAD_DIM
    row_id = lax.broadcasted_iota(jnp.int32, (rows, 1), 0)
    q = q_ref[...]
    q32 = q.astype(jnp.float32)
    qsend[...] = jnp.sum(jnp.where(row_id == long_local, q32, 0.0), axis=0, keepdims=True)
    pl.semaphore_wait(barrier, n - 1)

    copies = []
    for j in range(1, n):
        copy = pltpu.make_async_remote_copy(
            src_ref=qsend, dst_ref=qland.at[pl.ds(me, 1)], send_sem=send_sems.at[0, j - 1],
            recv_sem=recv_sems.at[0, j - 1], device_id={"req": lax.rem(me + j, n)}, device_id_type=MESH_ID)
        copy.start()
        copies.append(copy)

    zero_q = jnp.zeros_like(q)
    qm = jnp.concatenate([jnp.where(hm0, q, zero_q), jnp.where(hm0, zero_q, q)], axis=0)
    nt = (((1,), (1,)), ((), ()))
    loads[0].wait()
    loads[1].wait()
    s = lax.dot_general(qm, pk_ref[...], nt, preferred_element_type=jnp.float32) * scale
    length = jnp.zeros((rows, 1), jnp.int32)
    page0 = jnp.zeros((rows, 1), jnp.int32)
    page1 = jnp.zeros((rows, 1), jnp.int32)
    for r in range(rows):
        length = jnp.where(row_id == r, lens_ref[me * rows + r], length)
        page0 = jnp.where(row_id == r, bt_ref[0, r] - me * tokens // PAGE_SIZE, page0)
        page1 = jnp.where(row_id == r, bt_ref[1, r] - me * tokens // PAGE_SIZE, page1)
    tok = lax.broadcasted_iota(jnp.int32, (1, tokens), 1)
    tpage = tok // PAGE_SIZE
    tslot = tok % PAGE_SIZE
    usable = ((tpage == page0) & (tslot < length)) | ((tpage == page1) & (tslot + PAGE_SIZE < length))
    usable = usable & (length <= SHORT_MAX)
    usable2 = jnp.concatenate([usable, usable], axis=0)
    s = jnp.where(usable2, s, -jnp.inf)
    prod = q32 * k_ref[...].astype(jnp.float32)
    own0 = jnp.sum(jnp.where(hm0, prod, 0.0), axis=1, keepdims=True)
    own1 = jnp.sum(jnp.where(hm0, 0.0, prod), axis=1, keepdims=True)
    own = jnp.concatenate([own0, own1], axis=0) * scale
    m_s = jnp.maximum(jnp.max(s, axis=1, keepdims=True), own)
    w = jnp.exp(s - m_s)
    ow = jnp.exp(own - m_s)
    tot_s = jnp.sum(w, axis=1, keepdims=True) + ow
    nm = jnp.dot(w.astype(jnp.bfloat16), pv_ref[...], preferred_element_type=jnp.float32)
    owb = ow.astype(jnp.bfloat16).astype(jnp.float32)
    numer = jnp.where(hm0, nm[:rows], nm[rows:]) + jnp.where(
        hm0, owb[:rows], owb[rows:]) * v_ref[...].astype(jnp.float32)

    for copy in copies:
        copy.wait()
    qland[pl.ds(me, 1), :] = qsend[...]
    src_id = lax.broadcasted_iota(jnp.int32, (n, 1), 0)
    lq = jnp.sum(jnp.where(src_id == owner, qland[...], 0.0), axis=0, keepdims=True)
    lq = lq.astype(jnp.bfloat16)
    zero_l = jnp.zeros_like(lq)
    lqm = jnp.concatenate([jnp.where(hm0, lq, zero_l), jnp.where(hm0, zero_l, lq)], axis=0)
    loads[2].wait()
    loads[3].wait()
    ls = jnp.dot(lqm, lk_ref[...], preferred_element_type=jnp.float32) * scale
    m_l = jnp.max(ls, axis=1, keepdims=True)
    lw = jnp.exp(ls - m_l)
    l_l = jnp.sum(lw, axis=1, keepdims=True)
    acc = lax.dot_general(lw.astype(jnp.bfloat16), lv_ref[...], nt, preferred_element_type=jnp.float32)
    acc_row = jnp.where(hm0, acc[0:1], acc[1:2])
    width = psend.shape[1]
    psend[...] = jnp.zeros((1, width), jnp.float32)
    psend[:, 0:cols] = acc_row
    t = lax.broadcasted_iota(jnp.int32, (1, 128), 1)
    tail = jnp.where(t == 0, m_l[0:1], jnp.where(t == 1, m_l[1:2], jnp.where(
        t == 2, l_l[0:1], jnp.where(t == 3, l_l[1:2], 0.0))))
    psend[:, width - 128 : width] = tail

    copies = []
    for j in range(1, n):
        copy = pltpu.make_async_remote_copy(
            src_ref=psend, dst_ref=pland.at[pl.ds(me, 1)], send_sem=send_sems.at[1, j - 1],
            recv_sem=recv_sems.at[1, j - 1], device_id={"req": lax.rem(me + j, n)}, device_id_type=MESH_ID)
        copy.start()
        copies.append(copy)
    for copy in copies:
        copy.wait()
    pland[pl.ds(me, 1), :] = psend[...]

    parts = pland[...]
    base = width - 128
    sums_all = parts[:, 0:cols]
    whole = []
    for h in range(2):
        mh = parts[:, base + h : base + h + 1]
        lh = parts[:, base + 2 + h : base + 3 + h]
        wm = jnp.max(mh, axis=0, keepdims=True)
        keep = jnp.exp(mh - wm)
        wt = jnp.sum(lh * keep, axis=0, keepdims=True)
        ws = jnp.sum(sums_all * keep, axis=0, keepdims=True)
        whole.append((wm, wt, ws))
    whole_sums = jnp.where(hm0, whole[0][2], whole[1][2])
    chosen = (row_id == long_local) & (me == owner)
    kl, kg, tt = [], [], []
    for h in range(2):
        mh = m_s[h * rows : (h + 1) * rows]
        top = jnp.where(chosen, jnp.maximum(mh, whole[h][0]), mh)
        klh = jnp.exp(mh - top)
        kgh = jnp.where(chosen, jnp.exp(whole[h][0] - top), 0.0)
        kl.append(klh)
        kg.append(kgh)
        tt.append(tot_s[h * rows : (h + 1) * rows] * klh + kgh * whole[h][1])
    numer = numer * jnp.where(hm0, kl[0], kl[1]) + jnp.where(hm0, kg[0], kg[1]) * whole_sums
    out_ref[...] = (numer / jnp.where(hm0, tt[0], tt[1])).astype(out_ref.dtype)


def attention(n, cache_lengths, block_table, query, new_key, new_value, page_k, page_v, long_keys,
              long_values):
    scale = 1.0 / math.sqrt(HEAD_DIM)
    cols = query.shape[1]
    width = -(-cols // 128) * 128 + 128
    vmem = pl.BlockSpec(memory_space=pltpu.VMEM)
    smem = pl.BlockSpec(memory_space=pltpu.SMEM)
    anywhere = pl.BlockSpec(memory_space=pl.ANY)
    return pl.pallas_call(
        functools.partial(attention_kernel, n, scale),
        out_shape=jax.ShapeDtypeStruct(query.shape, jnp.bfloat16),
        in_specs=[vmem, smem, smem, vmem, vmem, vmem] + [anywhere] * 4,
        out_specs=vmem,
        scratch_shapes=[
            pltpu.VMEM(page_k.shape, page_k.dtype),
            pltpu.VMEM(page_v.shape, page_v.dtype),
            pltpu.VMEM(long_keys.shape[::-1], long_keys.dtype),
            pltpu.VMEM(long_values.shape[::-1], long_values.dtype),
            pltpu.VMEM((1, cols), jnp.float32),
            pltpu.VMEM((n, cols), jnp.float32),
            pltpu.VMEM((1, width), jnp.float32),
            pltpu.VMEM((n, width), jnp.float32),
            pltpu.SemaphoreType.DMA((4,)),
            pltpu.SemaphoreType.DMA((2, n - 1)),
            pltpu.SemaphoreType.DMA((2, n - 1)),
        ],
        compiler_params=pltpu.CompilerParams(collective_id=0, has_side_effects=True),
    )(
        cache_lengths.reshape(1, -1),
        cache_lengths,
        block_table.T,
        query,
        new_key,
        new_value,
        page_k,
        page_v,
        long_keys.T,
        long_values.T,
    )


def barrier_all(n, axis, me):
    barrier = pltpu.get_barrier_semaphore()
    for j in range(1, n):
        pl.semaphore_signal(barrier, inc=1, device_id={axis: lax.rem(me + j, n)}, device_id_type=MESH_ID)
    pl.semaphore_wait(barrier, n - 1)


def send_all(n, axis, me, pairs, send_sems, recv_sems):
    copies = []
    for k, (src, land) in enumerate(pairs):
        for j in range(1, n):
            copy = pltpu.make_async_remote_copy(
                src_ref=src, dst_ref=land.at[me], send_sem=send_sems.at[k, j - 1],
                recv_sem=recv_sems.at[k, j - 1], device_id={axis: lax.rem(me + j, n)},
                device_id_type=MESH_ID)
            copy.start()
            copies.append(copy)
    for copy in copies:
        copy.wait()
    for src, land in pairs:
        land[me] = src[...]


def norm_kernel(n, p_ref, r_ref, g_ref, hidden_ref, normed_ref, blocks, land, hsend, qsend,
                h_land, q_land, send_sems, recv_sems):
    me = lax.axis_index("mdl")
    cols = r_ref.shape[1]
    projected = p_ref[...]
    for j in range(n):
        blocks[j] = projected[:, j * cols : (j + 1) * cols].astype(blocks.dtype)
    barrier_all(n, "mdl", me)
    copies = []
    for j in range(1, n):
        peer = lax.rem(me + j, n)
        copy = pltpu.make_async_remote_copy(
            src_ref=blocks.at[peer], dst_ref=land.at[me], send_sem=send_sems.at[0, j - 1],
            recv_sem=recv_sems.at[0, j - 1], device_id={"mdl": peer}, device_id_type=MESH_ID)
        copy.start()
        copies.append(copy)
    for copy in copies:
        copy.wait()
    land[me] = blocks[me]
    summed = r_ref[...].astype(jnp.float32)
    for j in range(n):
        summed = summed + land[j].astype(jnp.float32)
    hidden = summed.astype(jnp.bfloat16)
    hidden_ref[...] = hidden
    hsend[...] = hidden
    hidden_f = hidden.astype(jnp.float32)
    qsend[...] = jnp.broadcast_to(jnp.sum(hidden_f * hidden_f, axis=1, keepdims=True), qsend.shape)
    send_all(n, "mdl", me, ((hsend, h_land), (qsend, q_land)), send_sems.at[1:3], recv_sems.at[1:3])
    hidden_all = jnp.concatenate([h_land[j] for j in range(n)], axis=1).astype(jnp.float32)
    squares = q_land[0]
    for j in range(1, n):
        squares = squares + q_land[j]
    inverse = lax.rsqrt(squares[:, 0:1] / MODEL_WIDTH + 1e-05)
    gain = g_ref[...].astype(jnp.float32).reshape(1, -1)
    normed_ref[...] = (hidden_all * inverse * gain).astype(normed_ref.dtype)


def norm_exchange(n, projected, residual, norm_gain):
    rows, cols = residual.shape
    vmem = pl.BlockSpec(memory_space=pltpu.VMEM)
    return pl.pallas_call(
        functools.partial(norm_kernel, n),
        out_shape=(
            jax.ShapeDtypeStruct(residual.shape, jnp.bfloat16),
            jax.ShapeDtypeStruct(projected.shape, jnp.bfloat16),
        ),
        in_specs=[vmem] * 3,
        out_specs=(vmem, vmem),
        scratch_shapes=[
            pltpu.VMEM((n, rows, cols), jnp.bfloat16),
            pltpu.VMEM((n, rows, cols), jnp.bfloat16),
            pltpu.VMEM((rows, cols), jnp.bfloat16),
            pltpu.VMEM((rows, 128), jnp.float32),
            pltpu.VMEM((n, rows, cols), jnp.bfloat16),
            pltpu.VMEM((n, rows, 128), jnp.float32),
            pltpu.SemaphoreType.DMA((3, n - 1)),
            pltpu.SemaphoreType.DMA((3, n - 1)),
        ],
        compiler_params=pltpu.CompilerParams(collective_id=2, has_side_effects=True),
    )(projected, residual, norm_gain)


def mix_kernel(n, width, g_ref, gain_ref, mixed_ref, msg, land, send_sems, recv_sems):
    me = lax.axis_index("mdl")
    gated = g_ref[...]
    msg[...] = jnp.broadcast_to(jnp.sum(gated * gated, axis=1, keepdims=True), msg.shape)
    barrier_all(n, "mdl", me)
    send_all(n, "mdl", me, ((msg, land),), send_sems, recv_sems)
    total = land[0]
    for j in range(1, n):
        total = total + land[j]
    inverse = lax.rsqrt(total[:, 0:1] / width + 1e-05)
    gain = gain_ref[...].astype(jnp.float32).reshape(1, -1)
    mixed_ref[...] = (gated * inverse * gain).astype(mixed_ref.dtype)


def mix_exchange(n, gated, out_gain, width):
    rows = gated.shape[0]
    vmem = pl.BlockSpec(memory_space=pltpu.VMEM)
    return pl.pallas_call(
        functools.partial(mix_kernel, n, width),
        out_shape=jax.ShapeDtypeStruct(gated.shape, jnp.bfloat16),
        in_specs=[vmem] * 2,
        out_specs=vmem,
        scratch_shapes=[
            pltpu.VMEM((rows, 128), jnp.float32),
            pltpu.VMEM((n, rows, 128), jnp.float32),
            pltpu.SemaphoreType.DMA((1, n - 1)),
            pltpu.SemaphoreType.DMA((1, n - 1)),
        ],
        compiler_params=pltpu.CompilerParams(collective_id=3, has_side_effects=True),
    )(gated, out_gain)


def shards(
    n_req,
    n_mdl,
    query,
    new_key,
    new_value,
    page_keys,
    page_values,
    long_keys,
    long_values,
    cache_lengths,
    block_table,
    out_weight,
    residual,
    norm_gain,
    x_weight,
    bc_weight,
    dt_weight,
    z_weight,
    dt_bias,
    a_log,
    skip_gain,
    conv_x_weight,
    conv_bc_weight,
    conv_x_state,
    conv_bc_state,
    ssm_state,
    out_gain,
):
    req_count = query.shape[0]
    local_cols = query.shape[1]
    heads_here = local_cols // HEAD_DIM
    scale = 1.0 / math.sqrt(HEAD_DIM)
    device = lax.axis_index("req")
    pages_here = page_keys.shape[0]
    long_row = jnp.argmax(cache_lengths)
    owner = long_row // req_count
    long_local = long_row % req_count

    assert heads_here == 2
    tokens_here = pages_here * PAGE_SIZE
    attended = attention(
        n_req,
        cache_lengths,
        block_table,
        query,
        new_key,
        new_value,
        page_keys.reshape(tokens_here, local_cols),
        page_values.reshape(tokens_here, local_cols),
        long_keys,
        long_values,
    )

    projected = jnp.dot(attended, out_weight, preferred_element_type=jnp.float32)
    feature_cols = residual.shape[1]
    feature_start = lax.axis_index("mdl") * feature_cols
    hidden, normed = norm_exchange(n_mdl, projected, residual, norm_gain)

    x_in = jnp.dot(normed, x_weight, preferred_element_type=jnp.float32)
    bc_in = jnp.dot(normed, bc_weight, preferred_element_type=jnp.float32)
    dt_in = jnp.dot(normed, dt_weight, preferred_element_type=jnp.float32)
    z_in = jnp.dot(normed, z_weight, preferred_element_type=jnp.float32)
    window_x = jnp.concatenate([conv_x_state.astype(jnp.float32), x_in[:, None, :]], axis=1)
    x_conv = jax.nn.silu(jnp.sum(window_x * conv_x_weight.astype(jnp.float32)[None], axis=1))
    window_bc = jnp.concatenate([conv_bc_state.astype(jnp.float32), bc_in[:, None, :]], axis=1)
    bc_conv = jax.nn.silu(jnp.sum(window_bc * conv_bc_weight.astype(jnp.float32)[None], axis=1))
    b_part = bc_conv[:, :STATE_DIM]
    c_part = bc_conv[:, STATE_DIM:]
    mamba_heads = dt_bias.shape[0]
    step = jax.nn.softplus(dt_in + dt_bias[None, :])
    decay = jnp.exp(-jnp.exp(a_log)[None, :] * step)
    x_heads = x_conv.reshape(req_count, mamba_heads, MHEAD_DIM)
    state = ssm_state.reshape(req_count, mamba_heads, MHEAD_DIM, STATE_DIM)
    state_new = (
        decay[:, :, None, None] * state
        + (step[:, :, None] * x_heads)[..., None] * b_part[:, None, None, :]
    )
    y_heads = (
        jnp.sum(state_new * c_part[:, None, None, :], axis=-1) + skip_gain[None, :, None] * x_heads
    )
    y_flat = y_heads.reshape(req_count, mamba_heads * MHEAD_DIM)
    gated = y_flat * jax.nn.silu(z_in)
    mixed = mix_exchange(n_mdl, gated, out_gain, MHEADS * MHEAD_DIM)
    return (hidden, mixed)


def solution(mesh):
    return jax.shard_map(
        functools.partial(shards, mesh.shape["req"], mesh.shape["mdl"]),
        mesh=mesh,
        in_specs=(
            P("req", "mdl"),
            P("req", "mdl"),
            P("req", "mdl"),
            P("req", None, "mdl"),
            P("req", None, "mdl"),
            P("req", "mdl"),
            P("req", "mdl"),
            P(),
            P("req", None),
            P("mdl", None),
            P("req", "mdl"),
            P(),
            P(None, "mdl"),
            P(),
            P(None, "mdl"),
            P(None, "mdl"),
            P("mdl"),
            P("mdl"),
            P("mdl"),
            P(None, "mdl"),
            P(),
            P("req", None, "mdl"),
            P("req", None, None),
            P("req", "mdl", None),
            P("mdl"),
        ),
        out_specs=(P("req", "mdl"), P("req", "mdl")),
        check_vma=False,
    )
```

```python
import functools
import math

import jax
import jax.numpy as jnp
from jax import lax
from jax.experimental import pallas as pl
from jax.experimental.pallas import tpu as pltpu
from jax.sharding import PartitionSpec as P

MODEL_WIDTH = 3584
HEAD_DIM = 224
MHEADS = 56
MHEAD_DIM = 64
STATE_DIM = 64
SHORT_MAX = 32
PAGE_SIZE = 16

MESH_ID = pl.DeviceIdType.MESH


def exchange_kernel(n, axis, count, *refs):
    x_refs = refs[:count]
    out_refs = refs[count : 2 * count]
    lands = refs[2 * count : 3 * count]
    send_sems, recv_sems = refs[3 * count :]
    me = lax.axis_index(axis)
    barrier = pltpu.get_barrier_semaphore()
    for j in range(1, n):
        peer = lax.rem(me + j, n)
        pl.semaphore_signal(barrier, inc=1, device_id={axis: peer}, device_id_type=MESH_ID)
    pl.semaphore_wait(barrier, n - 1)
    copies = []
    for k in range(count):
        rows = len(x_refs[k].shape) == 2 and x_refs[k].shape[0] == 1
        slot = lands[k].at[pl.ds(me, 1)] if rows else lands[k].at[me]
        for j in range(1, n):
            peer = lax.rem(me + j, n)
            copy = pltpu.make_async_remote_copy(
                src_ref=x_refs[k],
                dst_ref=slot,
                send_sem=send_sems.at[k, j - 1],
                recv_sem=recv_sems.at[k, j - 1],
                device_id={axis: peer},
                device_id_type=MESH_ID,
            )
            copy.start()
            copies.append(copy)
    for copy in copies:
        copy.wait()
    for k in range(count):
        rows = len(x_refs[k].shape) == 2 and x_refs[k].shape[0] == 1
        if rows:
            lands[k][pl.ds(me, 1), :] = x_refs[k][...]
        else:
            lands[k][me] = x_refs[k][...]
        out_refs[k][...] = lands[k][...]


def exchange(xs, axis, n, cid):
    shapes = []
    for x in xs:
        rows = x.ndim == 2 and x.shape[0] == 1
        shapes.append(jax.ShapeDtypeStruct((n, x.shape[1]) if rows else (n,) + x.shape, x.dtype))
    count = len(xs)
    return pl.pallas_call(
        functools.partial(exchange_kernel, n, axis, count),
        out_shape=tuple(shapes),
        in_specs=[pl.BlockSpec(memory_space=pltpu.VMEM)] * count,
        out_specs=tuple([pl.BlockSpec(memory_space=pltpu.VMEM)] * count),
        scratch_shapes=[pltpu.VMEM(s.shape, s.dtype) for s in shapes]
        + [pltpu.SemaphoreType.DMA((count, n - 1)), pltpu.SemaphoreType.DMA((count, n - 1))],
        compiler_params=pltpu.CompilerParams(collective_id=cid, has_side_effects=True),
    )(*xs)


def by_head(values, head_mask):
    out = jnp.zeros(values.shape[:-1] + (head_mask.shape[1],), values.dtype)
    for h in range(head_mask.shape[0]):
        out = jnp.where(head_mask[h], values[..., h : h + 1], out)
    return out


def pick_head(values, head_mask):
    out = values[..., 0, :]
    for h in range(1, head_mask.shape[0]):
        out = jnp.where(head_mask[h], values[..., h, :], out)
    return out


def attention_kernel(n, scale, cl_ref, lens_ref, bt_ref, q_ref, k_ref, v_ref, pk_hbm, pv_hbm,
                     lk_hbm, lv_hbm, out_ref, pk_ref, pv_ref, lk_ref, lv_ref, qsend, qland, psend,
                     pland, load_sems, send_sems, recv_sems):
    me = lax.axis_index("req")
    rows, cols = q_ref.shape
    tokens = pk_ref.shape[0]
    loads = []
    for i, (src, dst) in enumerate(((pk_hbm, pk_ref), (pv_hbm, pv_ref), (lk_hbm, lk_ref), (lv_hbm, lv_ref))):
        load = pltpu.make_async_copy(src, dst, load_sems.at[i])
        load.start()
        loads.append(load)
    barrier = pltpu.get_barrier_semaphore()
    for j in range(1, n):
        pl.semaphore_signal(barrier, inc=1, device_id={"req": lax.rem(me + j, n)}, device_id_type=MESH_ID)

    cl = cl_ref[...]
    longest = jnp.max(cl, axis=1, keepdims=True)
    where_long = jnp.where(cl == longest, lax.broadcasted_iota(jnp.int32, cl.shape, 1), cl.shape[1])
    long_row = jnp.min(where_long, axis=1, keepdims=True)
    owner = long_row // rows
    long_local = long_row - owner * rows
    lane = lax.broadcasted_iota(jnp.int32, (1, cols), 1)
    hm0 = lane < HEAD_DIM
    row_id = lax.broadcasted_iota(jnp.int32, (rows, 1), 0)
    q = q_ref[...]
    q32 = q.astype(jnp.float32)
    qsend[...] = jnp.sum(jnp.where(row_id == long_local, q32, 0.0), axis=0, keepdims=True)
    pl.semaphore_wait(barrier, n - 1)

    copies = []
    for j in range(1, n):
        copy = pltpu.make_async_remote_copy(
            src_ref=qsend, dst_ref=qland.at[pl.ds(me, 1)], send_sem=send_sems.at[0, j - 1],
            recv_sem=recv_sems.at[0, j - 1], device_id={"req": lax.rem(me + j, n)}, device_id_type=MESH_ID)
        copy.start()
        copies.append(copy)

    zero_q = jnp.zeros_like(q)
    qm = jnp.concatenate([jnp.where(hm0, q, zero_q), jnp.where(hm0, zero_q, q)], axis=0)
    nt = (((1,), (1,)), ((), ()))
    loads[0].wait()
    loads[1].wait()
    s = lax.dot_general(qm, pk_ref[...], nt, preferred_element_type=jnp.float32) * scale
    length = jnp.zeros((rows, 1), jnp.int32)
    page0 = jnp.zeros((rows, 1), jnp.int32)
    page1 = jnp.zeros((rows, 1), jnp.int32)
    for r in range(rows):
        length = jnp.where(row_id == r, lens_ref[me * rows + r], length)
        page0 = jnp.where(row_id == r, bt_ref[0, r] - me * tokens // PAGE_SIZE, page0)
        page1 = jnp.where(row_id == r, bt_ref[1, r] - me * tokens // PAGE_SIZE, page1)
    tok = lax.broadcasted_iota(jnp.int32, (1, tokens), 1)
    tpage = tok // PAGE_SIZE
    tslot = tok % PAGE_SIZE
    usable = ((tpage == page0) & (tslot < length)) | ((tpage == page1) & (tslot + PAGE_SIZE < length))
    usable = usable & (length <= SHORT_MAX)
    usable2 = jnp.concatenate([usable, usable], axis=0)
    s = jnp.where(usable2, s, -jnp.inf)
    prod = q32 * k_ref[...].astype(jnp.float32)
    own0 = jnp.sum(jnp.where(hm0, prod, 0.0), axis=1, keepdims=True)
    own1 = jnp.sum(jnp.where(hm0, 0.0, prod), axis=1, keepdims=True)
    own = jnp.concatenate([own0, own1], axis=0) * scale
    m_s = jnp.maximum(jnp.max(s, axis=1, keepdims=True), own)
    w = jnp.exp(s - m_s)
    ow = jnp.exp(own - m_s)
    tot_s = jnp.sum(w, axis=1, keepdims=True) + ow
    nm = jnp.dot(w.astype(jnp.bfloat16), pv_ref[...], preferred_element_type=jnp.float32)
    owb = ow.astype(jnp.bfloat16).astype(jnp.float32)
    numer = jnp.where(hm0, nm[:rows], nm[rows:]) + jnp.where(
        hm0, owb[:rows], owb[rows:]) * v_ref[...].astype(jnp.float32)

    for copy in copies:
        copy.wait()
    qland[pl.ds(me, 1), :] = qsend[...]
    src_id = lax.broadcasted_iota(jnp.int32, (n, 1), 0)
    lq = jnp.sum(jnp.where(src_id == owner, qland[...], 0.0), axis=0, keepdims=True)
    lq = lq.astype(jnp.bfloat16)
    zero_l = jnp.zeros_like(lq)
    lqm = jnp.concatenate([jnp.where(hm0, lq, zero_l), jnp.where(hm0, zero_l, lq)], axis=0)
    loads[2].wait()
    loads[3].wait()
    ls = jnp.dot(lqm, lk_ref[...], preferred_element_type=jnp.float32) * scale
    m_l = jnp.max(ls, axis=1, keepdims=True)
    lw = jnp.exp(ls - m_l)
    l_l = jnp.sum(lw, axis=1, keepdims=True)
    acc = lax.dot_general(lw.astype(jnp.bfloat16), lv_ref[...], nt, preferred_element_type=jnp.float32)
    acc_row = jnp.where(hm0, acc[0:1], acc[1:2])
    width = psend.shape[1]
    psend[...] = jnp.zeros((1, width), jnp.float32)
    psend[:, 0:cols] = acc_row
    t = lax.broadcasted_iota(jnp.int32, (1, 128), 1)
    tail = jnp.where(t == 0, m_l[0:1], jnp.where(t == 1, m_l[1:2], jnp.where(
        t == 2, l_l[0:1], jnp.where(t == 3, l_l[1:2], 0.0))))
    psend[:, width - 128 : width] = tail

    copies = []
    for j in range(1, n):
        copy = pltpu.make_async_remote_copy(
            src_ref=psend, dst_ref=pland.at[pl.ds(me, 1)], send_sem=send_sems.at[1, j - 1],
            recv_sem=recv_sems.at[1, j - 1], device_id={"req": lax.rem(me + j, n)}, device_id_type=MESH_ID)
        copy.start()
        copies.append(copy)
    for copy in copies:
        copy.wait()
    pland[pl.ds(me, 1), :] = psend[...]

    parts = pland[...]
    base = width - 128
    sums_all = parts[:, 0:cols]
    whole = []
    for h in range(2):
        mh = parts[:, base + h : base + h + 1]
        lh = parts[:, base + 2 + h : base + 3 + h]
        wm = jnp.max(mh, axis=0, keepdims=True)
        keep = jnp.exp(mh - wm)
        wt = jnp.sum(lh * keep, axis=0, keepdims=True)
        ws = jnp.sum(sums_all * keep, axis=0, keepdims=True)
        whole.append((wm, wt, ws))
    whole_sums = jnp.where(hm0, whole[0][2], whole[1][2])
    chosen = (row_id == long_local) & (me == owner)
    kl, kg, tt = [], [], []
    for h in range(2):
        mh = m_s[h * rows : (h + 1) * rows]
        top = jnp.where(chosen, jnp.maximum(mh, whole[h][0]), mh)
        klh = jnp.exp(mh - top)
        kgh = jnp.where(chosen, jnp.exp(whole[h][0] - top), 0.0)
        kl.append(klh)
        kg.append(kgh)
        tt.append(tot_s[h * rows : (h + 1) * rows] * klh + kgh * whole[h][1])
    numer = numer * jnp.where(hm0, kl[0], kl[1]) + jnp.where(hm0, kg[0], kg[1]) * whole_sums
    out_ref[...] = (numer / jnp.where(hm0, tt[0], tt[1])).astype(out_ref.dtype)


def attention(n, cache_lengths, block_table, query, new_key, new_value, page_k, page_v, long_keys,
              long_values):
    scale = 1.0 / math.sqrt(HEAD_DIM)
    cols = query.shape[1]
    width = -(-cols // 128) * 128 + 128
    vmem = pl.BlockSpec(memory_space=pltpu.VMEM)
    smem = pl.BlockSpec(memory_space=pltpu.SMEM)
    anywhere = pl.BlockSpec(memory_space=pl.ANY)
    return pl.pallas_call(
        functools.partial(attention_kernel, n, scale),
        out_shape=jax.ShapeDtypeStruct(query.shape, jnp.bfloat16),
        in_specs=[vmem, smem, smem, vmem, vmem, vmem] + [anywhere] * 4,
        out_specs=vmem,
        scratch_shapes=[
            pltpu.VMEM(page_k.shape, page_k.dtype),
            pltpu.VMEM(page_v.shape, page_v.dtype),
            pltpu.VMEM(long_keys.shape[::-1], long_keys.dtype),
            pltpu.VMEM(long_values.shape[::-1], long_values.dtype),
            pltpu.VMEM((1, cols), jnp.float32),
            pltpu.VMEM((n, cols), jnp.float32),
            pltpu.VMEM((1, width), jnp.float32),
            pltpu.VMEM((n, width), jnp.float32),
            pltpu.SemaphoreType.DMA((4,)),
            pltpu.SemaphoreType.DMA((2, n - 1)),
            pltpu.SemaphoreType.DMA((2, n - 1)),
        ],
        compiler_params=pltpu.CompilerParams(collective_id=0, has_side_effects=True),
    )(
        cache_lengths.reshape(1, -1),
        cache_lengths,
        block_table.T,
        query,
        new_key,
        new_value,
        page_k,
        page_v,
        long_keys.T,
        long_values.T,
    )


def barrier_all(n, axis, me):
    barrier = pltpu.get_barrier_semaphore()
    for j in range(1, n):
        pl.semaphore_signal(barrier, inc=1, device_id={axis: lax.rem(me + j, n)}, device_id_type=MESH_ID)
    pl.semaphore_wait(barrier, n - 1)


def send_all(n, axis, me, pairs, send_sems, recv_sems):
    copies = []
    for k, (src, land) in enumerate(pairs):
        for j in range(1, n):
            copy = pltpu.make_async_remote_copy(
                src_ref=src, dst_ref=land.at[me], send_sem=send_sems.at[k, j - 1],
                recv_sem=recv_sems.at[k, j - 1], device_id={axis: lax.rem(me + j, n)},
                device_id_type=MESH_ID)
            copy.start()
            copies.append(copy)
    for copy in copies:
        copy.wait()
    for src, land in pairs:
        land[me] = src[...]


def norm_kernel(n, p_ref, r_ref, g_ref, hidden_ref, normed_ref, blocks, land, hsend, qsend,
                h_land, q_land, send_sems, recv_sems):
    me = lax.axis_index("mdl")
    cols = r_ref.shape[1]
    projected = p_ref[...]
    for j in range(n):
        blocks[j] = projected[:, j * cols : (j + 1) * cols].astype(blocks.dtype)
    barrier_all(n, "mdl", me)
    copies = []
    for j in range(1, n):
        peer = lax.rem(me + j, n)
        copy = pltpu.make_async_remote_copy(
            src_ref=blocks.at[peer], dst_ref=land.at[me], send_sem=send_sems.at[0, j - 1],
            recv_sem=recv_sems.at[0, j - 1], device_id={"mdl": peer}, device_id_type=MESH_ID)
        copy.start()
        copies.append(copy)
    for copy in copies:
        copy.wait()
    land[me] = blocks[me]
    summed = r_ref[...].astype(jnp.float32)
    for j in range(n):
        summed = summed + land[j].astype(jnp.float32)
    hidden = summed.astype(jnp.bfloat16)
    hidden_ref[...] = hidden
    hsend[...] = hidden
    hidden_f = hidden.astype(jnp.float32)
    qsend[...] = jnp.broadcast_to(jnp.sum(hidden_f * hidden_f, axis=1, keepdims=True), qsend.shape)
    send_all(n, "mdl", me, ((hsend, h_land), (qsend, q_land)), send_sems.at[1:3], recv_sems.at[1:3])
    hidden_all = jnp.concatenate([h_land[j] for j in range(n)], axis=1).astype(jnp.float32)
    squares = q_land[0]
    for j in range(1, n):
        squares = squares + q_land[j]
    inverse = lax.rsqrt(squares[:, 0:1] / MODEL_WIDTH + 1e-05)
    gain = g_ref[...].astype(jnp.float32).reshape(1, -1)
    normed_ref[...] = (hidden_all * inverse * gain).astype(normed_ref.dtype)


def norm_exchange(n, projected, residual, norm_gain):
    rows, cols = residual.shape
    vmem = pl.BlockSpec(memory_space=pltpu.VMEM)
    return pl.pallas_call(
        functools.partial(norm_kernel, n),
        out_shape=(
            jax.ShapeDtypeStruct(residual.shape, jnp.bfloat16),
            jax.ShapeDtypeStruct(projected.shape, jnp.bfloat16),
        ),
        in_specs=[vmem] * 3,
        out_specs=(vmem, vmem),
        scratch_shapes=[
            pltpu.VMEM((n, rows, cols), jnp.bfloat16),
            pltpu.VMEM((n, rows, cols), jnp.bfloat16),
            pltpu.VMEM((rows, cols), jnp.bfloat16),
            pltpu.VMEM((rows, 128), jnp.float32),
            pltpu.VMEM((n, rows, cols), jnp.bfloat16),
            pltpu.VMEM((n, rows, 128), jnp.float32),
            pltpu.SemaphoreType.DMA((3, n - 1)),
            pltpu.SemaphoreType.DMA((3, n - 1)),
        ],
        compiler_params=pltpu.CompilerParams(collective_id=2, has_side_effects=True),
    )(projected, residual, norm_gain)


def mix_kernel(n, width, x_ref, z_ref, bc_ref, ct_ref, step_ref, decay_ref, skip_ref, s_ref,
               gain_ref, mixed_ref, msg, land, send_sems, recv_sems):
    me = lax.axis_index("mdl")
    rows, heads = step_ref.shape
    head_dim = x_ref.shape[1] // heads
    state_dim = ct_ref.shape[1] // head_dim
    group = (
        lax.broadcasted_iota(jnp.int32, (ct_ref.shape[1], head_dim), 0) // state_dim
        == lax.broadcasted_iota(jnp.int32, (ct_ref.shape[1], head_dim), 1)
    ).astype(jnp.bfloat16)
    bc = bc_ref[...]
    b_dot_c = jnp.sum(bc[:, :state_dim] * bc[:, state_dim:], axis=1, keepdims=True)
    ct = ct_ref[...]
    x = x_ref[...]
    step = step_ref[...]
    decay = decay_ref[...]
    skip = skip_ref[...]
    pieces = []
    for h in range(heads):
        prod = s_ref[:, h, :] * ct
        high = prod.astype(jnp.bfloat16)
        low = (prod - high.astype(jnp.float32)).astype(jnp.bfloat16)
        state_c = jnp.dot(high, group, preferred_element_type=jnp.float32) + jnp.dot(
            low, group, preferred_element_type=jnp.float32)
        x_h = x[:, h * head_dim : (h + 1) * head_dim]
        pieces.append(
            decay[:, h : h + 1] * state_c
            + (step[:, h : h + 1] * b_dot_c) * x_h
            + skip[:, h : h + 1] * x_h
        )
    y = jnp.concatenate(pieces, axis=1)
    z = z_ref[...]
    gated = y * (z * jax.nn.sigmoid(z))
    msg[...] = jnp.broadcast_to(jnp.sum(gated * gated, axis=1, keepdims=True), msg.shape)
    barrier_all(n, "mdl", me)
    send_all(n, "mdl", me, ((msg, land),), send_sems, recv_sems)
    total = land[0]
    for j in range(1, n):
        total = total + land[j]
    inverse = lax.rsqrt(total[:, 0:1] / width + 1e-05)
    gain = gain_ref[...].astype(jnp.float32).reshape(1, -1)
    mixed_ref[...] = (gated * inverse * gain).astype(mixed_ref.dtype)


def mix_exchange(n, width, x_conv, z_in, bc_conv, c_tiled, step, decay, skip_gain, ssm_state,
                 out_gain):
    rows = x_conv.shape[0]
    vmem = pl.BlockSpec(memory_space=pltpu.VMEM)
    return pl.pallas_call(
        functools.partial(mix_kernel, n, width),
        out_shape=jax.ShapeDtypeStruct(x_conv.shape, jnp.bfloat16),
        in_specs=[vmem] * 9,
        out_specs=vmem,
        scratch_shapes=[
            pltpu.VMEM((rows, 128), jnp.float32),
            pltpu.VMEM((n, rows, 128), jnp.float32),
            pltpu.SemaphoreType.DMA((1, n - 1)),
            pltpu.SemaphoreType.DMA((1, n - 1)),
        ],
        compiler_params=pltpu.CompilerParams(collective_id=3, has_side_effects=True),
    )(x_conv, z_in, bc_conv, c_tiled, step, decay, skip_gain.reshape(1, -1), ssm_state, out_gain)


def shards(
    n_req,
    n_mdl,
    query,
    new_key,
    new_value,
    page_keys,
    page_values,
    long_keys,
    long_values,
    cache_lengths,
    block_table,
    out_weight,
    residual,
    norm_gain,
    x_weight,
    bc_weight,
    dt_weight,
    z_weight,
    dt_bias,
    a_log,
    skip_gain,
    conv_x_weight,
    conv_bc_weight,
    conv_x_state,
    conv_bc_state,
    ssm_state,
    out_gain,
):
    req_count = query.shape[0]
    local_cols = query.shape[1]
    heads_here = local_cols // HEAD_DIM
    scale = 1.0 / math.sqrt(HEAD_DIM)
    device = lax.axis_index("req")
    pages_here = page_keys.shape[0]
    long_row = jnp.argmax(cache_lengths)
    owner = long_row // req_count
    long_local = long_row % req_count

    assert heads_here == 2
    tokens_here = pages_here * PAGE_SIZE
    attended = attention(
        n_req,
        cache_lengths,
        block_table,
        query,
        new_key,
        new_value,
        page_keys.reshape(tokens_here, local_cols),
        page_values.reshape(tokens_here, local_cols),
        long_keys,
        long_values,
    )

    projected = jnp.dot(attended, out_weight, preferred_element_type=jnp.float32)
    feature_cols = residual.shape[1]
    feature_start = lax.axis_index("mdl") * feature_cols
    hidden, normed = norm_exchange(n_mdl, projected, residual, norm_gain)

    x_in = jnp.dot(normed, x_weight, preferred_element_type=jnp.float32)
    bc_in = jnp.dot(normed, bc_weight, preferred_element_type=jnp.float32)
    dt_in = jnp.dot(normed, dt_weight, preferred_element_type=jnp.float32)
    z_in = jnp.dot(normed, z_weight, preferred_element_type=jnp.float32)
    window_x = jnp.concatenate([conv_x_state.astype(jnp.float32), x_in[:, None, :]], axis=1)
    x_conv = jax.nn.silu(jnp.sum(window_x * conv_x_weight.astype(jnp.float32)[None], axis=1))
    window_bc = jnp.concatenate([conv_bc_state.astype(jnp.float32), bc_in[:, None, :]], axis=1)
    bc_conv = jax.nn.silu(jnp.sum(window_bc * conv_bc_weight.astype(jnp.float32)[None], axis=1))
    b_part = bc_conv[:, :STATE_DIM]
    c_part = bc_conv[:, STATE_DIM:]
    mamba_heads = dt_bias.shape[0]
    step = jax.nn.softplus(dt_in + dt_bias[None, :])
    decay = jnp.exp(-jnp.exp(a_log)[None, :] * step)
    mixed = mix_exchange(
        n_mdl,
        MHEADS * MHEAD_DIM,
        x_conv,
        z_in,
        bc_conv,
        jnp.tile(c_part, (1, MHEAD_DIM)),
        step,
        decay,
        skip_gain,
        ssm_state,
        out_gain,
    )
    return (hidden, mixed)


def solution(mesh):
    return jax.shard_map(
        functools.partial(shards, mesh.shape["req"], mesh.shape["mdl"]),
        mesh=mesh,
        in_specs=(
            P("req", "mdl"),
            P("req", "mdl"),
            P("req", "mdl"),
            P("req", None, "mdl"),
            P("req", None, "mdl"),
            P("req", "mdl"),
            P("req", "mdl"),
            P(),
            P("req", None),
            P("mdl", None),
            P("req", "mdl"),
            P(),
            P(None, "mdl"),
            P(),
            P(None, "mdl"),
            P(None, "mdl"),
            P("mdl"),
            P("mdl"),
            P("mdl"),
            P(None, "mdl"),
            P(),
            P("req", None, "mdl"),
            P("req", None, None),
            P("req", "mdl", None),
            P("mdl"),
        ),
        out_specs=(P("req", "mdl"), P("req", "mdl")),
        check_vma=False,
    )
```

```python
import functools
import math

import jax
import jax.numpy as jnp
from jax import lax
from jax.experimental import pallas as pl
from jax.experimental.pallas import tpu as pltpu
from jax.sharding import PartitionSpec as P

MODEL_WIDTH = 3584
HEAD_DIM = 224
MHEADS = 56
MHEAD_DIM = 64
STATE_DIM = 64
SHORT_MAX = 32
PAGE_SIZE = 16

MESH_ID = pl.DeviceIdType.MESH


def exchange_kernel(n, axis, count, *refs):
    x_refs = refs[:count]
    out_refs = refs[count : 2 * count]
    lands = refs[2 * count : 3 * count]
    send_sems, recv_sems = refs[3 * count :]
    me = lax.axis_index(axis)
    barrier = pltpu.get_barrier_semaphore()
    for j in range(1, n):
        peer = lax.rem(me + j, n)
        pl.semaphore_signal(barrier, inc=1, device_id={axis: peer}, device_id_type=MESH_ID)
    pl.semaphore_wait(barrier, n - 1)
    copies = []
    for k in range(count):
        rows = len(x_refs[k].shape) == 2 and x_refs[k].shape[0] == 1
        slot = lands[k].at[pl.ds(me, 1)] if rows else lands[k].at[me]
        for j in range(1, n):
            peer = lax.rem(me + j, n)
            copy = pltpu.make_async_remote_copy(
                src_ref=x_refs[k],
                dst_ref=slot,
                send_sem=send_sems.at[k, j - 1],
                recv_sem=recv_sems.at[k, j - 1],
                device_id={axis: peer},
                device_id_type=MESH_ID,
            )
            copy.start()
            copies.append(copy)
    for copy in copies:
        copy.wait()
    for k in range(count):
        rows = len(x_refs[k].shape) == 2 and x_refs[k].shape[0] == 1
        if rows:
            lands[k][pl.ds(me, 1), :] = x_refs[k][...]
        else:
            lands[k][me] = x_refs[k][...]
        out_refs[k][...] = lands[k][...]


def exchange(xs, axis, n, cid):
    shapes = []
    for x in xs:
        rows = x.ndim == 2 and x.shape[0] == 1
        shapes.append(jax.ShapeDtypeStruct((n, x.shape[1]) if rows else (n,) + x.shape, x.dtype))
    count = len(xs)
    return pl.pallas_call(
        functools.partial(exchange_kernel, n, axis, count),
        out_shape=tuple(shapes),
        in_specs=[pl.BlockSpec(memory_space=pltpu.VMEM)] * count,
        out_specs=tuple([pl.BlockSpec(memory_space=pltpu.VMEM)] * count),
        scratch_shapes=[pltpu.VMEM(s.shape, s.dtype) for s in shapes]
        + [pltpu.SemaphoreType.DMA((count, n - 1)), pltpu.SemaphoreType.DMA((count, n - 1))],
        compiler_params=pltpu.CompilerParams(collective_id=cid, has_side_effects=True),
    )(*xs)


def by_head(values, head_mask):
    out = jnp.zeros(values.shape[:-1] + (head_mask.shape[1],), values.dtype)
    for h in range(head_mask.shape[0]):
        out = jnp.where(head_mask[h], values[..., h : h + 1], out)
    return out


def pick_head(values, head_mask):
    out = values[..., 0, :]
    for h in range(1, head_mask.shape[0]):
        out = jnp.where(head_mask[h], values[..., h, :], out)
    return out


def attention_kernel(n, scale, cl_ref, lens_ref, bt_ref, q_ref, k_ref, v_ref, pk_hbm, pv_hbm,
                     lk_hbm, lv_hbm, out_ref, pk_ref, pv_ref, lk_ref, lv_ref, qsend, qland, psend,
                     pland, load_sems, send_sems, recv_sems):
    me = lax.axis_index("req")
    rows, cols = q_ref.shape
    tokens = pk_ref.shape[0]
    loads = []
    for i, (src, dst) in enumerate(((pk_hbm, pk_ref), (pv_hbm, pv_ref), (lk_hbm, lk_ref), (lv_hbm, lv_ref))):
        load = pltpu.make_async_copy(src, dst, load_sems.at[i])
        load.start()
        loads.append(load)
    barrier = pltpu.get_barrier_semaphore()
    for j in range(1, n):
        pl.semaphore_signal(barrier, inc=1, device_id={"req": lax.rem(me + j, n)}, device_id_type=MESH_ID)

    cl = cl_ref[...]
    longest = jnp.max(cl, axis=1, keepdims=True)
    where_long = jnp.where(cl == longest, lax.broadcasted_iota(jnp.int32, cl.shape, 1), cl.shape[1])
    long_row = jnp.min(where_long, axis=1, keepdims=True)
    owner = long_row // rows
    long_local = long_row - owner * rows
    lane = lax.broadcasted_iota(jnp.int32, (1, cols), 1)
    hm0 = lane < HEAD_DIM
    row_id = lax.broadcasted_iota(jnp.int32, (rows, 1), 0)
    q = q_ref[...]
    q32 = q.astype(jnp.float32)
    qsend[...] = jnp.sum(jnp.where(row_id == long_local, q32, 0.0), axis=0, keepdims=True)
    pl.semaphore_wait(barrier, n - 1)

    copies = []
    for j in range(1, n):
        copy = pltpu.make_async_remote_copy(
            src_ref=qsend, dst_ref=qland.at[pl.ds(me, 1)], send_sem=send_sems.at[0, j - 1],
            recv_sem=recv_sems.at[0, j - 1], device_id={"req": lax.rem(me + j, n)}, device_id_type=MESH_ID)
        copy.start()
        copies.append(copy)

    zero_q = jnp.zeros_like(q)
    qm = jnp.concatenate([jnp.where(hm0, q, zero_q), jnp.where(hm0, zero_q, q)], axis=0)
    nt = (((1,), (1,)), ((), ()))
    loads[0].wait()
    loads[1].wait()
    s = lax.dot_general(qm, pk_ref[...], nt, preferred_element_type=jnp.float32) * scale
    length = jnp.zeros((rows, 1), jnp.int32)
    page0 = jnp.zeros((rows, 1), jnp.int32)
    page1 = jnp.zeros((rows, 1), jnp.int32)
    for r in range(rows):
        length = jnp.where(row_id == r, lens_ref[me * rows + r], length)
        page0 = jnp.where(row_id == r, bt_ref[0, r] - me * tokens // PAGE_SIZE, page0)
        page1 = jnp.where(row_id == r, bt_ref[1, r] - me * tokens // PAGE_SIZE, page1)
    tok = lax.broadcasted_iota(jnp.int32, (1, tokens), 1)
    tpage = tok // PAGE_SIZE
    tslot = tok % PAGE_SIZE
    usable = ((tpage == page0) & (tslot < length)) | ((tpage == page1) & (tslot + PAGE_SIZE < length))
    usable = usable & (length <= SHORT_MAX)
    usable2 = jnp.concatenate([usable, usable], axis=0)
    s = jnp.where(usable2, s, -jnp.inf)
    prod = q32 * k_ref[...].astype(jnp.float32)
    own0 = jnp.sum(jnp.where(hm0, prod, 0.0), axis=1, keepdims=True)
    own1 = jnp.sum(jnp.where(hm0, 0.0, prod), axis=1, keepdims=True)
    own = jnp.concatenate([own0, own1], axis=0) * scale
    m_s = jnp.maximum(jnp.max(s, axis=1, keepdims=True), own)
    w = jnp.exp(s - m_s)
    ow = jnp.exp(own - m_s)
    tot_s = jnp.sum(w, axis=1, keepdims=True) + ow
    nm = jnp.dot(w.astype(jnp.bfloat16), pv_ref[...], preferred_element_type=jnp.float32)
    owb = ow.astype(jnp.bfloat16).astype(jnp.float32)
    numer = jnp.where(hm0, nm[:rows], nm[rows:]) + jnp.where(
        hm0, owb[:rows], owb[rows:]) * v_ref[...].astype(jnp.float32)

    for copy in copies:
        copy.wait()
    qland[pl.ds(me, 1), :] = qsend[...]
    src_id = lax.broadcasted_iota(jnp.int32, (n, 1), 0)
    lq = jnp.sum(jnp.where(src_id == owner, qland[...], 0.0), axis=0, keepdims=True)
    lq = lq.astype(jnp.bfloat16)
    zero_l = jnp.zeros_like(lq)
    lqm = jnp.concatenate([jnp.where(hm0, lq, zero_l), jnp.where(hm0, zero_l, lq)], axis=0)
    loads[2].wait()
    loads[3].wait()
    ls = jnp.dot(lqm, lk_ref[...], preferred_element_type=jnp.float32) * scale
    m_l = jnp.max(ls, axis=1, keepdims=True)
    lw = jnp.exp(ls - m_l)
    l_l = jnp.sum(lw, axis=1, keepdims=True)
    acc = lax.dot_general(lw.astype(jnp.bfloat16), lv_ref[...], nt, preferred_element_type=jnp.float32)
    acc_row = jnp.where(hm0, acc[0:1], acc[1:2])
    width = psend.shape[1]
    psend[...] = jnp.zeros((1, width), jnp.float32)
    psend[:, 0:cols] = acc_row
    t = lax.broadcasted_iota(jnp.int32, (1, 128), 1)
    tail = jnp.where(t == 0, m_l[0:1], jnp.where(t == 1, m_l[1:2], jnp.where(
        t == 2, l_l[0:1], jnp.where(t == 3, l_l[1:2], 0.0))))
    psend[:, width - 128 : width] = tail

    copies = []
    for j in range(1, n):
        copy = pltpu.make_async_remote_copy(
            src_ref=psend, dst_ref=pland.at[pl.ds(me, 1)], send_sem=send_sems.at[1, j - 1],
            recv_sem=recv_sems.at[1, j - 1], device_id={"req": lax.rem(me + j, n)}, device_id_type=MESH_ID)
        copy.start()
        copies.append(copy)
    for copy in copies:
        copy.wait()
    pland[pl.ds(me, 1), :] = psend[...]

    parts = pland[...]
    base = width - 128
    sums_all = parts[:, 0:cols]
    whole = []
    for h in range(2):
        mh = parts[:, base + h : base + h + 1]
        lh = parts[:, base + 2 + h : base + 3 + h]
        wm = jnp.max(mh, axis=0, keepdims=True)
        keep = jnp.exp(mh - wm)
        wt = jnp.sum(lh * keep, axis=0, keepdims=True)
        ws = jnp.sum(sums_all * keep, axis=0, keepdims=True)
        whole.append((wm, wt, ws))
    whole_sums = jnp.where(hm0, whole[0][2], whole[1][2])
    chosen = (row_id == long_local) & (me == owner)
    kl, kg, tt = [], [], []
    for h in range(2):
        mh = m_s[h * rows : (h + 1) * rows]
        top = jnp.where(chosen, jnp.maximum(mh, whole[h][0]), mh)
        klh = jnp.exp(mh - top)
        kgh = jnp.where(chosen, jnp.exp(whole[h][0] - top), 0.0)
        kl.append(klh)
        kg.append(kgh)
        tt.append(tot_s[h * rows : (h + 1) * rows] * klh + kgh * whole[h][1])
    numer = numer * jnp.where(hm0, kl[0], kl[1]) + jnp.where(hm0, kg[0], kg[1]) * whole_sums
    out_ref[...] = (numer / jnp.where(hm0, tt[0], tt[1])).astype(out_ref.dtype)


def attention(n, cache_lengths, block_table, query, new_key, new_value, page_k, page_v, long_keys,
              long_values):
    scale = 1.0 / math.sqrt(HEAD_DIM)
    cols = query.shape[1]
    width = -(-cols // 128) * 128 + 128
    vmem = pl.BlockSpec(memory_space=pltpu.VMEM)
    smem = pl.BlockSpec(memory_space=pltpu.SMEM)
    anywhere = pl.BlockSpec(memory_space=pl.ANY)
    return pl.pallas_call(
        functools.partial(attention_kernel, n, scale),
        out_shape=jax.ShapeDtypeStruct(query.shape, jnp.bfloat16),
        in_specs=[vmem, smem, smem, vmem, vmem, vmem] + [anywhere] * 4,
        out_specs=vmem,
        scratch_shapes=[
            pltpu.VMEM(page_k.shape, page_k.dtype),
            pltpu.VMEM(page_v.shape, page_v.dtype),
            pltpu.VMEM(long_keys.shape[::-1], long_keys.dtype),
            pltpu.VMEM(long_values.shape[::-1], long_values.dtype),
            pltpu.VMEM((1, cols), jnp.float32),
            pltpu.VMEM((n, cols), jnp.float32),
            pltpu.VMEM((1, width), jnp.float32),
            pltpu.VMEM((n, width), jnp.float32),
            pltpu.SemaphoreType.DMA((4,)),
            pltpu.SemaphoreType.DMA((2, n - 1)),
            pltpu.SemaphoreType.DMA((2, n - 1)),
        ],
        compiler_params=pltpu.CompilerParams(collective_id=0, has_side_effects=True),
    )(
        cache_lengths.reshape(1, -1),
        cache_lengths,
        block_table.T,
        query,
        new_key,
        new_value,
        page_k,
        page_v,
        long_keys.T,
        long_values.T,
    )


def barrier_all(n, axis, me):
    barrier = pltpu.get_barrier_semaphore()
    for j in range(1, n):
        pl.semaphore_signal(barrier, inc=1, device_id={axis: lax.rem(me + j, n)}, device_id_type=MESH_ID)
    pl.semaphore_wait(barrier, n - 1)


def send_all(n, axis, me, pairs, send_sems, recv_sems):
    copies = []
    for k, (src, land) in enumerate(pairs):
        for j in range(1, n):
            copy = pltpu.make_async_remote_copy(
                src_ref=src, dst_ref=land.at[me], send_sem=send_sems.at[k, j - 1],
                recv_sem=recv_sems.at[k, j - 1], device_id={axis: lax.rem(me + j, n)},
                device_id_type=MESH_ID)
            copy.start()
            copies.append(copy)
    for copy in copies:
        copy.wait()
    for src, land in pairs:
        land[me] = src[...]


def norm_kernel(n, p_ref, r_ref, g_ref, hidden_ref, normed_ref, blocks, land, hsend, qsend,
                h_land, q_land, send_sems, recv_sems):
    me = lax.axis_index("mdl")
    cols = r_ref.shape[1]
    projected = p_ref[...]
    for j in range(n):
        blocks[j] = projected[:, j * cols : (j + 1) * cols].astype(blocks.dtype)
    barrier_all(n, "mdl", me)
    copies = []
    for j in range(1, n):
        peer = lax.rem(me + j, n)
        copy = pltpu.make_async_remote_copy(
            src_ref=blocks.at[peer], dst_ref=land.at[me], send_sem=send_sems.at[0, j - 1],
            recv_sem=recv_sems.at[0, j - 1], device_id={"mdl": peer}, device_id_type=MESH_ID)
        copy.start()
        copies.append(copy)
    for copy in copies:
        copy.wait()
    land[me] = blocks[me]
    summed = r_ref[...].astype(jnp.float32)
    for j in range(n):
        summed = summed + land[j].astype(jnp.float32)
    hidden = summed.astype(jnp.bfloat16)
    hidden_ref[...] = hidden
    hsend[...] = hidden
    hidden_f = hidden.astype(jnp.float32)
    qsend[...] = jnp.broadcast_to(jnp.sum(hidden_f * hidden_f, axis=1, keepdims=True), qsend.shape)
    send_all(n, "mdl", me, ((hsend, h_land), (qsend, q_land)), send_sems.at[1:3], recv_sems.at[1:3])
    hidden_all = jnp.concatenate([h_land[j] for j in range(n)], axis=1).astype(jnp.float32)
    squares = q_land[0]
    for j in range(1, n):
        squares = squares + q_land[j]
    inverse = lax.rsqrt(squares[:, 0:1] / MODEL_WIDTH + 1e-05)
    gain = g_ref[...].astype(jnp.float32).reshape(1, -1)
    normed_ref[...] = (hidden_all * inverse * gain).astype(normed_ref.dtype)


def norm_exchange(n, projected, residual, norm_gain):
    rows, cols = residual.shape
    vmem = pl.BlockSpec(memory_space=pltpu.VMEM)
    return pl.pallas_call(
        functools.partial(norm_kernel, n),
        out_shape=(
            jax.ShapeDtypeStruct(residual.shape, jnp.bfloat16),
            jax.ShapeDtypeStruct(projected.shape, jnp.bfloat16),
        ),
        in_specs=[vmem] * 3,
        out_specs=(vmem, vmem),
        scratch_shapes=[
            pltpu.VMEM((n, rows, cols), jnp.bfloat16),
            pltpu.VMEM((n, rows, cols), jnp.bfloat16),
            pltpu.VMEM((rows, cols), jnp.bfloat16),
            pltpu.VMEM((rows, 128), jnp.float32),
            pltpu.VMEM((n, rows, cols), jnp.bfloat16),
            pltpu.VMEM((n, rows, 128), jnp.float32),
            pltpu.SemaphoreType.DMA((3, n - 1)),
            pltpu.SemaphoreType.DMA((3, n - 1)),
        ],
        compiler_params=pltpu.CompilerParams(collective_id=2, has_side_effects=True),
    )(projected, residual, norm_gain)


def mix_kernel(n, width, x_ref, z_ref, bc_ref, ct_ref, step_ref, decay_ref, skip_ref, s_hbm,
               gain_ref, mixed_ref, s_ref, msg, land, load_sem, send_sems, recv_sems):
    me = lax.axis_index("mdl")
    load = pltpu.make_async_copy(s_hbm, s_ref, load_sem.at[0])
    load.start()
    rows, heads = step_ref.shape
    head_dim = x_ref.shape[1] // heads
    state_dim = ct_ref.shape[1] // head_dim
    group = (
        lax.broadcasted_iota(jnp.int32, (ct_ref.shape[1], head_dim), 0) // state_dim
        == lax.broadcasted_iota(jnp.int32, (ct_ref.shape[1], head_dim), 1)
    ).astype(jnp.bfloat16)
    bc = bc_ref[...]
    b_dot_c = jnp.sum(bc[:, :state_dim] * bc[:, state_dim:], axis=1, keepdims=True)
    ct = ct_ref[...]
    x = x_ref[...]
    step = step_ref[...]
    decay = decay_ref[...]
    skip = skip_ref[...]
    pieces = []
    load.wait()
    for h in range(heads):
        prod = s_ref[h] * ct
        high = prod.astype(jnp.bfloat16)
        low = (prod - high.astype(jnp.float32)).astype(jnp.bfloat16)
        state_c = jnp.dot(high, group, preferred_element_type=jnp.float32) + jnp.dot(
            low, group, preferred_element_type=jnp.float32)
        x_h = x[:, h * head_dim : (h + 1) * head_dim]
        pieces.append(
            decay[:, h : h + 1] * state_c
            + (step[:, h : h + 1] * b_dot_c) * x_h
            + skip[:, h : h + 1] * x_h
        )
    y = jnp.concatenate(pieces, axis=1)
    z = z_ref[...]
    gated = y * (z * jax.nn.sigmoid(z))
    msg[...] = jnp.broadcast_to(jnp.sum(gated * gated, axis=1, keepdims=True), msg.shape)
    barrier_all(n, "mdl", me)
    send_all(n, "mdl", me, ((msg, land),), send_sems, recv_sems)
    total = land[0]
    for j in range(1, n):
        total = total + land[j]
    inverse = lax.rsqrt(total[:, 0:1] / width + 1e-05)
    gain = gain_ref[...].astype(jnp.float32).reshape(1, -1)
    mixed_ref[...] = (gated * inverse * gain).astype(mixed_ref.dtype)


def mix_exchange(n, width, x_conv, z_in, bc_conv, c_tiled, step, decay, skip_gain, ssm_state,
                 out_gain):
    rows = x_conv.shape[0]
    vmem = pl.BlockSpec(memory_space=pltpu.VMEM)
    return pl.pallas_call(
        functools.partial(mix_kernel, n, width),
        out_shape=jax.ShapeDtypeStruct(x_conv.shape, jnp.bfloat16),
        in_specs=[vmem] * 7 + [pl.BlockSpec(memory_space=pl.ANY), vmem],
        out_specs=vmem,
        scratch_shapes=[
            pltpu.VMEM(ssm_state.shape[1::-1] + ssm_state.shape[2:], ssm_state.dtype),
            pltpu.VMEM((rows, 128), jnp.float32),
            pltpu.VMEM((n, rows, 128), jnp.float32),
            pltpu.SemaphoreType.DMA((1,)),
            pltpu.SemaphoreType.DMA((1, n - 1)),
            pltpu.SemaphoreType.DMA((1, n - 1)),
        ],
        compiler_params=pltpu.CompilerParams(collective_id=3, has_side_effects=True),
    )(
        x_conv,
        z_in,
        bc_conv,
        c_tiled,
        step,
        decay,
        skip_gain.reshape(1, -1),
        jnp.transpose(ssm_state, (1, 0, 2)),
        out_gain,
    )


def shards(
    n_req,
    n_mdl,
    query,
    new_key,
    new_value,
    page_keys,
    page_values,
    long_keys,
    long_values,
    cache_lengths,
    block_table,
    out_weight,
    residual,
    norm_gain,
    x_weight,
    bc_weight,
    dt_weight,
    z_weight,
    dt_bias,
    a_log,
    skip_gain,
    conv_x_weight,
    conv_bc_weight,
    conv_x_state,
    conv_bc_state,
    ssm_state,
    out_gain,
):
    req_count = query.shape[0]
    local_cols = query.shape[1]
    heads_here = local_cols // HEAD_DIM
    scale = 1.0 / math.sqrt(HEAD_DIM)
    device = lax.axis_index("req")
    pages_here = page_keys.shape[0]
    long_row = jnp.argmax(cache_lengths)
    owner = long_row // req_count
    long_local = long_row % req_count

    assert heads_here == 2
    tokens_here = pages_here * PAGE_SIZE
    attended = attention(
        n_req,
        cache_lengths,
        block_table,
        query,
        new_key,
        new_value,
        page_keys.reshape(tokens_here, local_cols),
        page_values.reshape(tokens_here, local_cols),
        long_keys,
        long_values,
    )

    projected = jnp.dot(attended, out_weight, preferred_element_type=jnp.float32)
    feature_cols = residual.shape[1]
    feature_start = lax.axis_index("mdl") * feature_cols
    hidden, normed = norm_exchange(n_mdl, projected, residual, norm_gain)

    x_in = jnp.dot(normed, x_weight, preferred_element_type=jnp.float32)
    bc_in = jnp.dot(normed, bc_weight, preferred_element_type=jnp.float32)
    dt_in = jnp.dot(normed, dt_weight, preferred_element_type=jnp.float32)
    z_in = jnp.dot(normed, z_weight, preferred_element_type=jnp.float32)
    taps = conv_x_state.shape[1]
    x_pre = x_in * conv_x_weight[taps].astype(jnp.float32)
    bc_pre = bc_in * conv_bc_weight[taps].astype(jnp.float32)
    for k in range(taps):
        x_pre = x_pre + conv_x_state[:, k, :].astype(jnp.float32) * conv_x_weight[k].astype(jnp.float32)
        bc_pre = bc_pre + conv_bc_state[:, k, :].astype(jnp.float32) * conv_bc_weight[k].astype(
            jnp.float32
        )
    x_conv = jax.nn.silu(x_pre)
    bc_conv = jax.nn.silu(bc_pre)
    b_part = bc_conv[:, :STATE_DIM]
    c_part = bc_conv[:, STATE_DIM:]
    mamba_heads = dt_bias.shape[0]
    step = jax.nn.softplus(dt_in + dt_bias[None, :])
    decay = jnp.exp(-jnp.exp(a_log)[None, :] * step)
    mixed = mix_exchange(
        n_mdl,
        MHEADS * MHEAD_DIM,
        x_conv,
        z_in,
        bc_conv,
        jnp.tile(c_part, (1, MHEAD_DIM)),
        step,
        decay,
        skip_gain,
        ssm_state,
        out_gain,
    )
    return (hidden, mixed)


def solution(mesh):
    return jax.shard_map(
        functools.partial(shards, mesh.shape["req"], mesh.shape["mdl"]),
        mesh=mesh,
        in_specs=(
            P("req", "mdl"),
            P("req", "mdl"),
            P("req", "mdl"),
            P("req", None, "mdl"),
            P("req", None, "mdl"),
            P("req", "mdl"),
            P("req", "mdl"),
            P(),
            P("req", None),
            P("mdl", None),
            P("req", "mdl"),
            P(),
            P(None, "mdl"),
            P(),
            P(None, "mdl"),
            P(None, "mdl"),
            P("mdl"),
            P("mdl"),
            P("mdl"),
            P(None, "mdl"),
            P(),
            P("req", None, "mdl"),
            P("req", None, None),
            P("req", "mdl", None),
            P("mdl"),
        ),
        out_specs=(P("req", "mdl"), P("req", "mdl")),
        check_vma=False,
    )
```

```python
import functools
import math

import jax
import jax.numpy as jnp
from jax import lax
from jax.experimental import pallas as pl
from jax.experimental.pallas import tpu as pltpu
from jax.sharding import PartitionSpec as P

MODEL_WIDTH = 3584
HEAD_DIM = 224
MHEADS = 56
MHEAD_DIM = 64
STATE_DIM = 64
SHORT_MAX = 32
PAGE_SIZE = 16

MESH_ID = pl.DeviceIdType.MESH


def exchange_kernel(n, axis, count, *refs):
    x_refs = refs[:count]
    out_refs = refs[count : 2 * count]
    lands = refs[2 * count : 3 * count]
    send_sems, recv_sems = refs[3 * count :]
    me = lax.axis_index(axis)
    barrier = pltpu.get_barrier_semaphore()
    for j in range(1, n):
        peer = lax.rem(me + j, n)
        pl.semaphore_signal(barrier, inc=1, device_id={axis: peer}, device_id_type=MESH_ID)
    pl.semaphore_wait(barrier, n - 1)
    copies = []
    for k in range(count):
        rows = len(x_refs[k].shape) == 2 and x_refs[k].shape[0] == 1
        slot = lands[k].at[pl.ds(me, 1)] if rows else lands[k].at[me]
        for j in range(1, n):
            peer = lax.rem(me + j, n)
            copy = pltpu.make_async_remote_copy(
                src_ref=x_refs[k],
                dst_ref=slot,
                send_sem=send_sems.at[k, j - 1],
                recv_sem=recv_sems.at[k, j - 1],
                device_id={axis: peer},
                device_id_type=MESH_ID,
            )
            copy.start()
            copies.append(copy)
    for copy in copies:
        copy.wait()
    for k in range(count):
        rows = len(x_refs[k].shape) == 2 and x_refs[k].shape[0] == 1
        if rows:
            lands[k][pl.ds(me, 1), :] = x_refs[k][...]
        else:
            lands[k][me] = x_refs[k][...]
        out_refs[k][...] = lands[k][...]


def exchange(xs, axis, n, cid):
    shapes = []
    for x in xs:
        rows = x.ndim == 2 and x.shape[0] == 1
        shapes.append(jax.ShapeDtypeStruct((n, x.shape[1]) if rows else (n,) + x.shape, x.dtype))
    count = len(xs)
    return pl.pallas_call(
        functools.partial(exchange_kernel, n, axis, count),
        out_shape=tuple(shapes),
        in_specs=[pl.BlockSpec(memory_space=pltpu.VMEM)] * count,
        out_specs=tuple([pl.BlockSpec(memory_space=pltpu.VMEM)] * count),
        scratch_shapes=[pltpu.VMEM(s.shape, s.dtype) for s in shapes]
        + [pltpu.SemaphoreType.DMA((count, n - 1)), pltpu.SemaphoreType.DMA((count, n - 1))],
        compiler_params=pltpu.CompilerParams(collective_id=cid, has_side_effects=True),
    )(*xs)


def by_head(values, head_mask):
    out = jnp.zeros(values.shape[:-1] + (head_mask.shape[1],), values.dtype)
    for h in range(head_mask.shape[0]):
        out = jnp.where(head_mask[h], values[..., h : h + 1], out)
    return out


def pick_head(values, head_mask):
    out = values[..., 0, :]
    for h in range(1, head_mask.shape[0]):
        out = jnp.where(head_mask[h], values[..., h, :], out)
    return out


def attention_kernel(n, scale, cl_ref, lens_ref, bt_ref, q_ref, k_ref, v_ref, pk_hbm, pv_hbm,
                     lk_hbm, lv_hbm, out_ref, pk_ref, pv_ref, lk_ref, lv_ref, qsend, qland, psend,
                     pland, load_sems, send_sems, recv_sems):
    me = lax.axis_index("req")
    rows, cols = q_ref.shape
    tokens = pk_ref.shape[0]
    loads = []
    for i, (src, dst) in enumerate(((pk_hbm, pk_ref), (pv_hbm, pv_ref), (lk_hbm, lk_ref), (lv_hbm, lv_ref))):
        load = pltpu.make_async_copy(src, dst, load_sems.at[i])
        load.start()
        loads.append(load)
    barrier = pltpu.get_barrier_semaphore()
    for j in range(1, n):
        pl.semaphore_signal(barrier, inc=1, device_id={"req": lax.rem(me + j, n)}, device_id_type=MESH_ID)

    cl = cl_ref[...]
    longest = jnp.max(cl, axis=1, keepdims=True)
    where_long = jnp.where(cl == longest, lax.broadcasted_iota(jnp.int32, cl.shape, 1), cl.shape[1])
    long_row = jnp.min(where_long, axis=1, keepdims=True)
    owner = long_row // rows
    long_local = long_row - owner * rows
    lane = lax.broadcasted_iota(jnp.int32, (1, cols), 1)
    hm0 = lane < HEAD_DIM
    row_id = lax.broadcasted_iota(jnp.int32, (rows, 1), 0)
    q = q_ref[...]
    q32 = q.astype(jnp.float32)
    qsend[...] = jnp.sum(jnp.where(row_id == long_local, q32, 0.0), axis=0, keepdims=True)
    pl.semaphore_wait(barrier, n - 1)

    copies = []
    for j in range(1, n):
        copy = pltpu.make_async_remote_copy(
            src_ref=qsend, dst_ref=qland.at[pl.ds(me, 1)], send_sem=send_sems.at[0, j - 1],
            recv_sem=recv_sems.at[0, j - 1], device_id={"req": lax.rem(me + j, n)}, device_id_type=MESH_ID)
        copy.start()
        copies.append(copy)

    zero_q = jnp.zeros_like(q)
    qm = jnp.concatenate([jnp.where(hm0, q, zero_q), jnp.where(hm0, zero_q, q)], axis=0)
    nt = (((1,), (1,)), ((), ()))
    loads[0].wait()
    loads[1].wait()
    s = lax.dot_general(qm, pk_ref[...], nt, preferred_element_type=jnp.float32) * scale
    length = jnp.zeros((rows, 1), jnp.int32)
    page0 = jnp.zeros((rows, 1), jnp.int32)
    page1 = jnp.zeros((rows, 1), jnp.int32)
    for r in range(rows):
        length = jnp.where(row_id == r, lens_ref[me * rows + r], length)
        page0 = jnp.where(row_id == r, bt_ref[0, r] - me * tokens // PAGE_SIZE, page0)
        page1 = jnp.where(row_id == r, bt_ref[1, r] - me * tokens // PAGE_SIZE, page1)
    tok = lax.broadcasted_iota(jnp.int32, (1, tokens), 1)
    tpage = tok // PAGE_SIZE
    tslot = tok % PAGE_SIZE
    usable = ((tpage == page0) & (tslot < length)) | ((tpage == page1) & (tslot + PAGE_SIZE < length))
    usable = usable & (length <= SHORT_MAX)
    usable2 = jnp.concatenate([usable, usable], axis=0)
    s = jnp.where(usable2, s, -jnp.inf)
    prod = q32 * k_ref[...].astype(jnp.float32)
    own0 = jnp.sum(jnp.where(hm0, prod, 0.0), axis=1, keepdims=True)
    own1 = jnp.sum(jnp.where(hm0, 0.0, prod), axis=1, keepdims=True)
    own = jnp.concatenate([own0, own1], axis=0) * scale
    m_s = jnp.maximum(jnp.max(s, axis=1, keepdims=True), own)
    w = jnp.exp(s - m_s)
    ow = jnp.exp(own - m_s)
    tot_s = jnp.sum(w, axis=1, keepdims=True) + ow
    nm = jnp.dot(w.astype(jnp.bfloat16), pv_ref[...], preferred_element_type=jnp.float32)
    owb = ow.astype(jnp.bfloat16).astype(jnp.float32)
    numer = jnp.where(hm0, nm[:rows], nm[rows:]) + jnp.where(
        hm0, owb[:rows], owb[rows:]) * v_ref[...].astype(jnp.float32)

    for copy in copies:
        copy.wait()
    qland[pl.ds(me, 1), :] = qsend[...]
    src_id = lax.broadcasted_iota(jnp.int32, (n, 1), 0)
    lq = jnp.sum(jnp.where(src_id == owner, qland[...], 0.0), axis=0, keepdims=True)
    lq = lq.astype(jnp.bfloat16)
    zero_l = jnp.zeros_like(lq)
    lqm = jnp.concatenate([jnp.where(hm0, lq, zero_l), jnp.where(hm0, zero_l, lq)], axis=0)
    loads[2].wait()
    loads[3].wait()
    ls = jnp.dot(lqm, lk_ref[...], preferred_element_type=jnp.float32) * scale
    m_l = jnp.max(ls, axis=1, keepdims=True)
    lw = jnp.exp(ls - m_l)
    l_l = jnp.sum(lw, axis=1, keepdims=True)
    acc = lax.dot_general(lw.astype(jnp.bfloat16), lv_ref[...], nt, preferred_element_type=jnp.float32)
    acc_row = jnp.where(hm0, acc[0:1], acc[1:2])
    width = psend.shape[1]
    psend[...] = jnp.zeros((1, width), jnp.float32)
    psend[:, 0:cols] = acc_row
    t = lax.broadcasted_iota(jnp.int32, (1, 128), 1)
    tail = jnp.where(t == 0, m_l[0:1], jnp.where(t == 1, m_l[1:2], jnp.where(
        t == 2, l_l[0:1], jnp.where(t == 3, l_l[1:2], 0.0))))
    psend[:, width - 128 : width] = tail

    copies = []
    for j in range(1, n):
        copy = pltpu.make_async_remote_copy(
            src_ref=psend, dst_ref=pland.at[pl.ds(me, 1)], send_sem=send_sems.at[1, j - 1],
            recv_sem=recv_sems.at[1, j - 1], device_id={"req": lax.rem(me + j, n)}, device_id_type=MESH_ID)
        copy.start()
        copies.append(copy)
    for copy in copies:
        copy.wait()
    pland[pl.ds(me, 1), :] = psend[...]

    parts = pland[...]
    base = width - 128
    sums_all = parts[:, 0:cols]
    whole = []
    for h in range(2):
        mh = parts[:, base + h : base + h + 1]
        lh = parts[:, base + 2 + h : base + 3 + h]
        wm = jnp.max(mh, axis=0, keepdims=True)
        keep = jnp.exp(mh - wm)
        wt = jnp.sum(lh * keep, axis=0, keepdims=True)
        ws = jnp.sum(sums_all * keep, axis=0, keepdims=True)
        whole.append((wm, wt, ws))
    whole_sums = jnp.where(hm0, whole[0][2], whole[1][2])
    chosen = (row_id == long_local) & (me == owner)
    kl, kg, tt = [], [], []
    for h in range(2):
        mh = m_s[h * rows : (h + 1) * rows]
        top = jnp.where(chosen, jnp.maximum(mh, whole[h][0]), mh)
        klh = jnp.exp(mh - top)
        kgh = jnp.where(chosen, jnp.exp(whole[h][0] - top), 0.0)
        kl.append(klh)
        kg.append(kgh)
        tt.append(tot_s[h * rows : (h + 1) * rows] * klh + kgh * whole[h][1])
    numer = numer * jnp.where(hm0, kl[0], kl[1]) + jnp.where(hm0, kg[0], kg[1]) * whole_sums
    out_ref[...] = (numer / jnp.where(hm0, tt[0], tt[1])).astype(out_ref.dtype)


def attention(n, cache_lengths, block_table, query, new_key, new_value, page_k, page_v, long_keys,
              long_values):
    scale = 1.0 / math.sqrt(HEAD_DIM)
    cols = query.shape[1]
    width = -(-cols // 128) * 128 + 128
    vmem = pl.BlockSpec(memory_space=pltpu.VMEM)
    smem = pl.BlockSpec(memory_space=pltpu.SMEM)
    anywhere = pl.BlockSpec(memory_space=pl.ANY)
    return pl.pallas_call(
        functools.partial(attention_kernel, n, scale),
        out_shape=jax.ShapeDtypeStruct(query.shape, jnp.bfloat16),
        in_specs=[vmem, smem, smem, vmem, vmem, vmem] + [anywhere] * 4,
        out_specs=vmem,
        scratch_shapes=[
            pltpu.VMEM(page_k.shape, page_k.dtype),
            pltpu.VMEM(page_v.shape, page_v.dtype),
            pltpu.VMEM(long_keys.shape[::-1], long_keys.dtype),
            pltpu.VMEM(long_values.shape[::-1], long_values.dtype),
            pltpu.VMEM((1, cols), jnp.float32),
            pltpu.VMEM((n, cols), jnp.float32),
            pltpu.VMEM((1, width), jnp.float32),
            pltpu.VMEM((n, width), jnp.float32),
            pltpu.SemaphoreType.DMA((4,)),
            pltpu.SemaphoreType.DMA((2, n - 1)),
            pltpu.SemaphoreType.DMA((2, n - 1)),
        ],
        compiler_params=pltpu.CompilerParams(collective_id=0, has_side_effects=True),
    )(
        cache_lengths.reshape(1, -1),
        cache_lengths,
        block_table.T,
        query,
        new_key,
        new_value,
        page_k,
        page_v,
        long_keys.T,
        long_values.T,
    )


def barrier_all(n, axis, me):
    barrier = pltpu.get_barrier_semaphore()
    for j in range(1, n):
        pl.semaphore_signal(barrier, inc=1, device_id={axis: lax.rem(me + j, n)}, device_id_type=MESH_ID)
    pl.semaphore_wait(barrier, n - 1)


def send_all(n, axis, me, pairs, send_sems, recv_sems):
    copies = []
    for k, (src, land) in enumerate(pairs):
        for j in range(1, n):
            copy = pltpu.make_async_remote_copy(
                src_ref=src, dst_ref=land.at[me], send_sem=send_sems.at[k, j - 1],
                recv_sem=recv_sems.at[k, j - 1], device_id={axis: lax.rem(me + j, n)},
                device_id_type=MESH_ID)
            copy.start()
            copies.append(copy)
    for copy in copies:
        copy.wait()
    for src, land in pairs:
        land[me] = src[...]


def norm_kernel(n, p_ref, r_ref, g_ref, hidden_ref, normed_ref, blocks, land, hsend, qsend,
                h_land, q_land, send_sems, recv_sems):
    me = lax.axis_index("mdl")
    cols = r_ref.shape[1]
    projected = p_ref[...]
    for j in range(n):
        blocks[j] = projected[:, j * cols : (j + 1) * cols].astype(blocks.dtype)
    barrier_all(n, "mdl", me)
    copies = []
    for j in range(1, n):
        peer = lax.rem(me + j, n)
        copy = pltpu.make_async_remote_copy(
            src_ref=blocks.at[peer], dst_ref=land.at[me], send_sem=send_sems.at[0, j - 1],
            recv_sem=recv_sems.at[0, j - 1], device_id={"mdl": peer}, device_id_type=MESH_ID)
        copy.start()
        copies.append(copy)
    for copy in copies:
        copy.wait()
    land[me] = blocks[me]
    summed = r_ref[...].astype(jnp.float32)
    for j in range(n):
        summed = summed + land[j].astype(jnp.float32)
    hidden = summed.astype(jnp.bfloat16)
    hidden_ref[...] = hidden
    hsend[...] = hidden
    hidden_f = hidden.astype(jnp.float32)
    qsend[...] = jnp.broadcast_to(jnp.sum(hidden_f * hidden_f, axis=1, keepdims=True), qsend.shape)
    send_all(n, "mdl", me, ((hsend, h_land), (qsend, q_land)), send_sems.at[1:3], recv_sems.at[1:3])
    hidden_all = jnp.concatenate([h_land[j] for j in range(n)], axis=1).astype(jnp.float32)
    squares = q_land[0]
    for j in range(1, n):
        squares = squares + q_land[j]
    inverse = lax.rsqrt(squares[:, 0:1] / MODEL_WIDTH + 1e-05)
    gain = g_ref[...].astype(jnp.float32).reshape(1, -1)
    normed_ref[...] = (hidden_all * inverse * gain).astype(normed_ref.dtype)


def norm_exchange(n, projected, residual, norm_gain):
    rows, cols = residual.shape
    vmem = pl.BlockSpec(memory_space=pltpu.VMEM)
    return pl.pallas_call(
        functools.partial(norm_kernel, n),
        out_shape=(
            jax.ShapeDtypeStruct(residual.shape, jnp.bfloat16),
            jax.ShapeDtypeStruct(projected.shape, jnp.bfloat16),
        ),
        in_specs=[vmem] * 3,
        out_specs=(vmem, vmem),
        scratch_shapes=[
            pltpu.VMEM((n, rows, cols), jnp.bfloat16),
            pltpu.VMEM((n, rows, cols), jnp.bfloat16),
            pltpu.VMEM((rows, cols), jnp.bfloat16),
            pltpu.VMEM((rows, 128), jnp.float32),
            pltpu.VMEM((n, rows, cols), jnp.bfloat16),
            pltpu.VMEM((n, rows, 128), jnp.float32),
            pltpu.SemaphoreType.DMA((3, n - 1)),
            pltpu.SemaphoreType.DMA((3, n - 1)),
        ],
        compiler_params=pltpu.CompilerParams(collective_id=2, has_side_effects=True),
    )(projected, residual, norm_gain)


def mix_kernel(n, width, x_ref, z_ref, bc_ref, ct_ref, step_ref, decay_ref, skip_ref, s_hbm,
               gain_ref, mixed_ref, s_ref, msg, land, load_sem, send_sems, recv_sems):
    me = lax.axis_index("mdl")
    load = pltpu.make_async_copy(s_hbm, s_ref, load_sem.at[0])
    load.start()
    rows, heads = step_ref.shape
    head_dim = x_ref.shape[1] // heads
    state_dim = ct_ref.shape[1] // head_dim
    group = (
        lax.broadcasted_iota(jnp.int32, (ct_ref.shape[1], head_dim), 0) // state_dim
        == lax.broadcasted_iota(jnp.int32, (ct_ref.shape[1], head_dim), 1)
    ).astype(jnp.bfloat16)
    bc = bc_ref[...]
    b_dot_c = jnp.sum(bc[:, :state_dim] * bc[:, state_dim:], axis=1, keepdims=True)
    ct = ct_ref[...]
    x = x_ref[...]
    step = step_ref[...]
    decay = decay_ref[...]
    skip = skip_ref[...]
    load.wait()
    highs, lows = [], []
    for h in range(heads):
        prod = s_ref[h] * ct
        high = prod.astype(jnp.bfloat16)
        highs.append(high)
        lows.append((prod - high.astype(jnp.float32)).astype(jnp.bfloat16))
    stacked = jnp.concatenate(highs + lows, axis=0)
    sums = jnp.dot(stacked, group, preferred_element_type=jnp.float32)
    pieces = []
    for h in range(heads):
        state_c = sums[h * rows : (h + 1) * rows] + sums[(heads + h) * rows : (heads + h + 1) * rows]
        x_h = x[:, h * head_dim : (h + 1) * head_dim]
        pieces.append(
            decay[:, h : h + 1] * state_c
            + (step[:, h : h + 1] * b_dot_c) * x_h
            + skip[:, h : h + 1] * x_h
        )
    y = jnp.concatenate(pieces, axis=1)
    z = z_ref[...]
    gated = y * (z * jax.nn.sigmoid(z))
    msg[...] = jnp.broadcast_to(jnp.sum(gated * gated, axis=1, keepdims=True), msg.shape)
    barrier_all(n, "mdl", me)
    send_all(n, "mdl", me, ((msg, land),), send_sems, recv_sems)
    total = land[0]
    for j in range(1, n):
        total = total + land[j]
    inverse = lax.rsqrt(total[:, 0:1] / width + 1e-05)
    gain = gain_ref[...].astype(jnp.float32).reshape(1, -1)
    mixed_ref[...] = (gated * inverse * gain).astype(mixed_ref.dtype)


def mix_exchange(n, width, x_conv, z_in, bc_conv, c_tiled, step, decay, skip_gain, ssm_state,
                 out_gain):
    rows = x_conv.shape[0]
    vmem = pl.BlockSpec(memory_space=pltpu.VMEM)
    return pl.pallas_call(
        functools.partial(mix_kernel, n, width),
        out_shape=jax.ShapeDtypeStruct(x_conv.shape, jnp.bfloat16),
        in_specs=[vmem] * 7 + [pl.BlockSpec(memory_space=pl.ANY), vmem],
        out_specs=vmem,
        scratch_shapes=[
            pltpu.VMEM(ssm_state.shape[1::-1] + ssm_state.shape[2:], ssm_state.dtype),
            pltpu.VMEM((rows, 128), jnp.float32),
            pltpu.VMEM((n, rows, 128), jnp.float32),
            pltpu.SemaphoreType.DMA((1,)),
            pltpu.SemaphoreType.DMA((1, n - 1)),
            pltpu.SemaphoreType.DMA((1, n - 1)),
        ],
        compiler_params=pltpu.CompilerParams(collective_id=3, has_side_effects=True),
    )(
        x_conv,
        z_in,
        bc_conv,
        c_tiled,
        step,
        decay,
        skip_gain.reshape(1, -1),
        jnp.transpose(ssm_state, (1, 0, 2)),
        out_gain,
    )


def shards(
    n_req,
    n_mdl,
    query,
    new_key,
    new_value,
    page_keys,
    page_values,
    long_keys,
    long_values,
    cache_lengths,
    block_table,
    out_weight,
    residual,
    norm_gain,
    x_weight,
    bc_weight,
    dt_weight,
    z_weight,
    dt_bias,
    a_log,
    skip_gain,
    conv_x_weight,
    conv_bc_weight,
    conv_x_state,
    conv_bc_state,
    ssm_state,
    out_gain,
):
    req_count = query.shape[0]
    local_cols = query.shape[1]
    heads_here = local_cols // HEAD_DIM
    scale = 1.0 / math.sqrt(HEAD_DIM)
    device = lax.axis_index("req")
    pages_here = page_keys.shape[0]
    long_row = jnp.argmax(cache_lengths)
    owner = long_row // req_count
    long_local = long_row % req_count

    assert heads_here == 2
    tokens_here = pages_here * PAGE_SIZE
    attended = attention(
        n_req,
        cache_lengths,
        block_table,
        query,
        new_key,
        new_value,
        page_keys.reshape(tokens_here, local_cols),
        page_values.reshape(tokens_here, local_cols),
        long_keys,
        long_values,
    )

    projected = jnp.dot(attended, out_weight, preferred_element_type=jnp.float32)
    feature_cols = residual.shape[1]
    feature_start = lax.axis_index("mdl") * feature_cols
    hidden, normed = norm_exchange(n_mdl, projected, residual, norm_gain)

    x_in = jnp.dot(normed, x_weight, preferred_element_type=jnp.float32)
    bc_in = jnp.dot(normed, bc_weight, preferred_element_type=jnp.float32)
    dt_in = jnp.dot(normed, dt_weight, preferred_element_type=jnp.float32)
    z_in = jnp.dot(normed, z_weight, preferred_element_type=jnp.float32)
    taps = conv_x_state.shape[1]
    x_pre = x_in * conv_x_weight[taps].astype(jnp.float32)
    bc_pre = bc_in * conv_bc_weight[taps].astype(jnp.float32)
    for k in range(taps):
        x_pre = x_pre + conv_x_state[:, k, :].astype(jnp.float32) * conv_x_weight[k].astype(jnp.float32)
        bc_pre = bc_pre + conv_bc_state[:, k, :].astype(jnp.float32) * conv_bc_weight[k].astype(
            jnp.float32
        )
    x_conv = jax.nn.silu(x_pre)
    bc_conv = jax.nn.silu(bc_pre)
    b_part = bc_conv[:, :STATE_DIM]
    c_part = bc_conv[:, STATE_DIM:]
    mamba_heads = dt_bias.shape[0]
    step = jax.nn.softplus(dt_in + dt_bias[None, :])
    decay = jnp.exp(-jnp.exp(a_log)[None, :] * step)
    mixed = mix_exchange(
        n_mdl,
        MHEADS * MHEAD_DIM,
        x_conv,
        z_in,
        bc_conv,
        jnp.tile(c_part, (1, MHEAD_DIM)),
        step,
        decay,
        skip_gain,
        ssm_state,
        out_gain,
    )
    return (hidden, mixed)


def solution(mesh):
    return jax.shard_map(
        functools.partial(shards, mesh.shape["req"], mesh.shape["mdl"]),
        mesh=mesh,
        in_specs=(
            P("req", "mdl"),
            P("req", "mdl"),
            P("req", "mdl"),
            P("req", None, "mdl"),
            P("req", None, "mdl"),
            P("req", "mdl"),
            P("req", "mdl"),
            P(),
            P("req", None),
            P("mdl", None),
            P("req", "mdl"),
            P(),
            P(None, "mdl"),
            P(),
            P(None, "mdl"),
            P(None, "mdl"),
            P("mdl"),
            P("mdl"),
            P("mdl"),
            P(None, "mdl"),
            P(),
            P("req", None, "mdl"),
            P("req", None, None),
            P("req", "mdl", None),
            P("mdl"),
        ),
        out_specs=(P("req", "mdl"), P("req", "mdl")),
        check_vma=False,
    )
```

```python
import functools
import math

import jax
import jax.numpy as jnp
from jax import lax
from jax.experimental import pallas as pl
from jax.experimental.pallas import tpu as pltpu
from jax.sharding import PartitionSpec as P

MODEL_WIDTH = 3584
HEAD_DIM = 224
MHEADS = 56
MHEAD_DIM = 64
STATE_DIM = 64
SHORT_MAX = 32
PAGE_SIZE = 16

MESH_ID = pl.DeviceIdType.MESH


def exchange_kernel(n, axis, count, *refs):
    x_refs = refs[:count]
    out_refs = refs[count : 2 * count]
    lands = refs[2 * count : 3 * count]
    send_sems, recv_sems = refs[3 * count :]
    me = lax.axis_index(axis)
    barrier = pltpu.get_barrier_semaphore()
    for j in range(1, n):
        peer = lax.rem(me + j, n)
        pl.semaphore_signal(barrier, inc=1, device_id={axis: peer}, device_id_type=MESH_ID)
    pl.semaphore_wait(barrier, n - 1)
    copies = []
    for k in range(count):
        rows = len(x_refs[k].shape) == 2 and x_refs[k].shape[0] == 1
        slot = lands[k].at[pl.ds(me, 1)] if rows else lands[k].at[me]
        for j in range(1, n):
            peer = lax.rem(me + j, n)
            copy = pltpu.make_async_remote_copy(
                src_ref=x_refs[k],
                dst_ref=slot,
                send_sem=send_sems.at[k, j - 1],
                recv_sem=recv_sems.at[k, j - 1],
                device_id={axis: peer},
                device_id_type=MESH_ID,
            )
            copy.start()
            copies.append(copy)
    for copy in copies:
        copy.wait()
    for k in range(count):
        rows = len(x_refs[k].shape) == 2 and x_refs[k].shape[0] == 1
        if rows:
            lands[k][pl.ds(me, 1), :] = x_refs[k][...]
        else:
            lands[k][me] = x_refs[k][...]
        out_refs[k][...] = lands[k][...]


def exchange(xs, axis, n, cid):
    shapes = []
    for x in xs:
        rows = x.ndim == 2 and x.shape[0] == 1
        shapes.append(jax.ShapeDtypeStruct((n, x.shape[1]) if rows else (n,) + x.shape, x.dtype))
    count = len(xs)
    return pl.pallas_call(
        functools.partial(exchange_kernel, n, axis, count),
        out_shape=tuple(shapes),
        in_specs=[pl.BlockSpec(memory_space=pltpu.VMEM)] * count,
        out_specs=tuple([pl.BlockSpec(memory_space=pltpu.VMEM)] * count),
        scratch_shapes=[pltpu.VMEM(s.shape, s.dtype) for s in shapes]
        + [pltpu.SemaphoreType.DMA((count, n - 1)), pltpu.SemaphoreType.DMA((count, n - 1))],
        compiler_params=pltpu.CompilerParams(collective_id=cid, has_side_effects=True),
    )(*xs)


def by_head(values, head_mask):
    out = jnp.zeros(values.shape[:-1] + (head_mask.shape[1],), values.dtype)
    for h in range(head_mask.shape[0]):
        out = jnp.where(head_mask[h], values[..., h : h + 1], out)
    return out


def pick_head(values, head_mask):
    out = values[..., 0, :]
    for h in range(1, head_mask.shape[0]):
        out = jnp.where(head_mask[h], values[..., h, :], out)
    return out


def attention_kernel(n, scale, cl_ref, lens_ref, bt_ref, q_ref, k_ref, v_ref, pk_hbm, pv_hbm,
                     lk_hbm, lv_hbm, out_ref, pk_ref, pv_ref, lk_ref, lv_ref, qsend, qland, psend,
                     pland, load_sems, send_sems, recv_sems):
    me = lax.axis_index("req")
    rows, cols = q_ref.shape
    tokens = pk_ref.shape[0]
    loads = []
    for i, (src, dst) in enumerate(((pk_hbm, pk_ref), (pv_hbm, pv_ref), (lk_hbm, lk_ref), (lv_hbm, lv_ref))):
        load = pltpu.make_async_copy(src, dst, load_sems.at[i])
        load.start()
        loads.append(load)
    barrier = pltpu.get_barrier_semaphore()
    for j in range(1, n):
        pl.semaphore_signal(barrier, inc=1, device_id={"req": lax.rem(me + j, n)}, device_id_type=MESH_ID)

    cl = cl_ref[...]
    longest = jnp.max(cl, axis=1, keepdims=True)
    where_long = jnp.where(cl == longest, lax.broadcasted_iota(jnp.int32, cl.shape, 1), cl.shape[1])
    long_row = jnp.min(where_long, axis=1, keepdims=True)
    owner = long_row // rows
    long_local = long_row - owner * rows
    lane = lax.broadcasted_iota(jnp.int32, (1, cols), 1)
    hm0 = lane < HEAD_DIM
    row_id = lax.broadcasted_iota(jnp.int32, (rows, 1), 0)
    q = q_ref[...]
    q32 = q.astype(jnp.float32)
    qsend[...] = jnp.sum(jnp.where(row_id == long_local, q32, 0.0), axis=0, keepdims=True)
    pl.semaphore_wait(barrier, n - 1)

    copies = []
    for j in range(1, n):
        copy = pltpu.make_async_remote_copy(
            src_ref=qsend, dst_ref=qland.at[pl.ds(me, 1)], send_sem=send_sems.at[0, j - 1],
            recv_sem=recv_sems.at[0, j - 1], device_id={"req": lax.rem(me + j, n)}, device_id_type=MESH_ID)
        copy.start()
        copies.append(copy)

    zero_q = jnp.zeros_like(q)
    qm = jnp.concatenate([jnp.where(hm0, q, zero_q), jnp.where(hm0, zero_q, q)], axis=0)
    nt = (((1,), (1,)), ((), ()))
    loads[0].wait()
    loads[1].wait()
    s = lax.dot_general(qm, pk_ref[...], nt, preferred_element_type=jnp.float32) * scale
    length = jnp.zeros((rows, 1), jnp.int32)
    page0 = jnp.zeros((rows, 1), jnp.int32)
    page1 = jnp.zeros((rows, 1), jnp.int32)
    for r in range(rows):
        length = jnp.where(row_id == r, lens_ref[me * rows + r], length)
        page0 = jnp.where(row_id == r, bt_ref[0, r] - me * tokens // PAGE_SIZE, page0)
        page1 = jnp.where(row_id == r, bt_ref[1, r] - me * tokens // PAGE_SIZE, page1)
    tok = lax.broadcasted_iota(jnp.int32, (1, tokens), 1)
    tpage = tok // PAGE_SIZE
    tslot = tok % PAGE_SIZE
    usable = ((tpage == page0) & (tslot < length)) | ((tpage == page1) & (tslot + PAGE_SIZE < length))
    usable = usable & (length <= SHORT_MAX)
    usable2 = jnp.concatenate([usable, usable], axis=0)
    s = jnp.where(usable2, s, -jnp.inf)
    prod = q32 * k_ref[...].astype(jnp.float32)
    own0 = jnp.sum(jnp.where(hm0, prod, 0.0), axis=1, keepdims=True)
    own1 = jnp.sum(jnp.where(hm0, 0.0, prod), axis=1, keepdims=True)
    own = jnp.concatenate([own0, own1], axis=0) * scale
    m_s = jnp.maximum(jnp.max(s, axis=1, keepdims=True), own)
    w = jnp.exp(s - m_s)
    ow = jnp.exp(own - m_s)
    tot_s = jnp.sum(w, axis=1, keepdims=True) + ow
    nm = jnp.dot(w.astype(jnp.bfloat16), pv_ref[...], preferred_element_type=jnp.float32)
    owb = ow.astype(jnp.bfloat16).astype(jnp.float32)
    numer = jnp.where(hm0, nm[:rows], nm[rows:]) + jnp.where(
        hm0, owb[:rows], owb[rows:]) * v_ref[...].astype(jnp.float32)

    for copy in copies:
        copy.wait()
    qland[pl.ds(me, 1), :] = qsend[...]
    src_id = lax.broadcasted_iota(jnp.int32, (n, 1), 0)
    lq = jnp.sum(jnp.where(src_id == owner, qland[...], 0.0), axis=0, keepdims=True)
    lq = lq.astype(jnp.bfloat16)
    zero_l = jnp.zeros_like(lq)
    lqm = jnp.concatenate([jnp.where(hm0, lq, zero_l), jnp.where(hm0, zero_l, lq)], axis=0)
    loads[2].wait()
    loads[3].wait()
    ls = jnp.dot(lqm, lk_ref[...], preferred_element_type=jnp.float32) * scale
    m_l = jnp.max(ls, axis=1, keepdims=True)
    lw = jnp.exp(ls - m_l)
    l_l = jnp.sum(lw, axis=1, keepdims=True)
    acc = lax.dot_general(lw.astype(jnp.bfloat16), lv_ref[...], nt, preferred_element_type=jnp.float32)
    acc_row = jnp.where(hm0, acc[0:1], acc[1:2])
    width = psend.shape[1]
    psend[...] = jnp.zeros((1, width), jnp.float32)
    psend[:, 0:cols] = acc_row
    t = lax.broadcasted_iota(jnp.int32, (1, 128), 1)
    tail = jnp.where(t == 0, m_l[0:1], jnp.where(t == 1, m_l[1:2], jnp.where(
        t == 2, l_l[0:1], jnp.where(t == 3, l_l[1:2], 0.0))))
    psend[:, width - 128 : width] = tail

    copies = []
    for j in range(1, n):
        copy = pltpu.make_async_remote_copy(
            src_ref=psend, dst_ref=pland.at[pl.ds(me, 1)], send_sem=send_sems.at[1, j - 1],
            recv_sem=recv_sems.at[1, j - 1], device_id={"req": lax.rem(me + j, n)}, device_id_type=MESH_ID)
        copy.start()
        copies.append(copy)
    for copy in copies:
        copy.wait()
    pland[pl.ds(me, 1), :] = psend[...]

    parts = pland[...]
    base = width - 128
    sums_all = parts[:, 0:cols]
    whole = []
    for h in range(2):
        mh = parts[:, base + h : base + h + 1]
        lh = parts[:, base + 2 + h : base + 3 + h]
        wm = jnp.max(mh, axis=0, keepdims=True)
        keep = jnp.exp(mh - wm)
        wt = jnp.sum(lh * keep, axis=0, keepdims=True)
        ws = jnp.sum(sums_all * keep, axis=0, keepdims=True)
        whole.append((wm, wt, ws))
    whole_sums = jnp.where(hm0, whole[0][2], whole[1][2])
    chosen = (row_id == long_local) & (me == owner)
    kl, kg, tt = [], [], []
    for h in range(2):
        mh = m_s[h * rows : (h + 1) * rows]
        top = jnp.where(chosen, jnp.maximum(mh, whole[h][0]), mh)
        klh = jnp.exp(mh - top)
        kgh = jnp.where(chosen, jnp.exp(whole[h][0] - top), 0.0)
        kl.append(klh)
        kg.append(kgh)
        tt.append(tot_s[h * rows : (h + 1) * rows] * klh + kgh * whole[h][1])
    numer = numer * jnp.where(hm0, kl[0], kl[1]) + jnp.where(hm0, kg[0], kg[1]) * whole_sums
    out_ref[...] = (numer / jnp.where(hm0, tt[0], tt[1])).astype(out_ref.dtype)


def attention(n, cache_lengths, block_table, query, new_key, new_value, page_k, page_v, long_keys,
              long_values):
    scale = 1.0 / math.sqrt(HEAD_DIM)
    cols = query.shape[1]
    width = -(-cols // 128) * 128 + 128
    vmem = pl.BlockSpec(memory_space=pltpu.VMEM)
    smem = pl.BlockSpec(memory_space=pltpu.SMEM)
    anywhere = pl.BlockSpec(memory_space=pl.ANY)
    return pl.pallas_call(
        functools.partial(attention_kernel, n, scale),
        out_shape=jax.ShapeDtypeStruct(query.shape, jnp.bfloat16),
        in_specs=[vmem, smem, smem, vmem, vmem, vmem] + [anywhere] * 4,
        out_specs=vmem,
        scratch_shapes=[
            pltpu.VMEM(page_k.shape, page_k.dtype),
            pltpu.VMEM(page_v.shape, page_v.dtype),
            pltpu.VMEM(long_keys.shape[::-1], long_keys.dtype),
            pltpu.VMEM(long_values.shape[::-1], long_values.dtype),
            pltpu.VMEM((1, cols), jnp.float32),
            pltpu.VMEM((n, cols), jnp.float32),
            pltpu.VMEM((1, width), jnp.float32),
            pltpu.VMEM((n, width), jnp.float32),
            pltpu.SemaphoreType.DMA((4,)),
            pltpu.SemaphoreType.DMA((2, n - 1)),
            pltpu.SemaphoreType.DMA((2, n - 1)),
        ],
        compiler_params=pltpu.CompilerParams(collective_id=0, has_side_effects=True),
    )(
        cache_lengths.reshape(1, -1),
        cache_lengths,
        block_table.T,
        query,
        new_key,
        new_value,
        page_k,
        page_v,
        long_keys.T,
        long_values.T,
    )


def barrier_all(n, axis, me):
    barrier = pltpu.get_barrier_semaphore()
    for j in range(1, n):
        pl.semaphore_signal(barrier, inc=1, device_id={axis: lax.rem(me + j, n)}, device_id_type=MESH_ID)
    pl.semaphore_wait(barrier, n - 1)


def send_all(n, axis, me, pairs, send_sems, recv_sems):
    copies = []
    for k, (src, land) in enumerate(pairs):
        for j in range(1, n):
            copy = pltpu.make_async_remote_copy(
                src_ref=src, dst_ref=land.at[me], send_sem=send_sems.at[k, j - 1],
                recv_sem=recv_sems.at[k, j - 1], device_id={axis: lax.rem(me + j, n)},
                device_id_type=MESH_ID)
            copy.start()
            copies.append(copy)
    for copy in copies:
        copy.wait()
    for src, land in pairs:
        land[me] = src[...]


def norm_kernel(n, p_ref, r_ref, g_ref, xw_hbm, zw_hbm, bw_hbm, dw_hbm, hidden_ref, x_ref, z_ref,
                bc_ref, dt_ref, blocks, land, hsend, qsend, h_land, q_land, xw, zw, bw, dw, load_sems,
                send_sems, recv_sems):
    me = lax.axis_index("mdl")
    loads = []
    for i, (src, dst) in enumerate(((xw_hbm, xw), (zw_hbm, zw), (bw_hbm, bw), (dw_hbm, dw))):
        load = pltpu.make_async_copy(src, dst, load_sems.at[i])
        load.start()
        loads.append(load)
    cols = r_ref.shape[1]
    projected = p_ref[...]
    for j in range(n):
        blocks[j] = projected[:, j * cols : (j + 1) * cols].astype(blocks.dtype)
    barrier_all(n, "mdl", me)
    copies = []
    for j in range(1, n):
        peer = lax.rem(me + j, n)
        copy = pltpu.make_async_remote_copy(
            src_ref=blocks.at[peer], dst_ref=land.at[me], send_sem=send_sems.at[0, j - 1],
            recv_sem=recv_sems.at[0, j - 1], device_id={"mdl": peer}, device_id_type=MESH_ID)
        copy.start()
        copies.append(copy)
    for copy in copies:
        copy.wait()
    land[me] = blocks[me]
    summed = r_ref[...].astype(jnp.float32)
    for j in range(n):
        summed = summed + land[j].astype(jnp.float32)
    hidden = summed.astype(jnp.bfloat16)
    hidden_ref[...] = hidden
    hsend[...] = hidden
    hidden_f = hidden.astype(jnp.float32)
    qsend[...] = jnp.broadcast_to(jnp.sum(hidden_f * hidden_f, axis=1, keepdims=True), qsend.shape)
    send_all(n, "mdl", me, ((hsend, h_land), (qsend, q_land)), send_sems.at[1:3], recv_sems.at[1:3])
    hidden_all = jnp.concatenate([h_land[j] for j in range(n)], axis=1).astype(jnp.float32)
    squares = q_land[0]
    for j in range(1, n):
        squares = squares + q_land[j]
    inverse = lax.rsqrt(squares[:, 0:1] / MODEL_WIDTH + 1e-05)
    gain = g_ref[...].astype(jnp.float32).reshape(1, -1)
    normed = (hidden_all * inverse * gain).astype(jnp.bfloat16)
    nt = (((1,), (1,)), ((), ()))
    for load in loads:
        load.wait()
    x_ref[...] = lax.dot_general(normed, xw[...], nt, preferred_element_type=jnp.float32)
    z_ref[...] = lax.dot_general(normed, zw[...], nt, preferred_element_type=jnp.float32)
    bc_ref[...] = jnp.dot(normed, bw[...], preferred_element_type=jnp.float32)
    dt_ref[...] = lax.dot_general(normed, dw[...], nt, preferred_element_type=jnp.float32)


def norm_exchange(n, projected, residual, norm_gain, x_weight_t, z_weight_t, bc_weight, dt_weight_t):
    rows, cols = residual.shape
    vmem = pl.BlockSpec(memory_space=pltpu.VMEM)
    anywhere = pl.BlockSpec(memory_space=pl.ANY)
    weights = (x_weight_t, z_weight_t, bc_weight, dt_weight_t)
    return pl.pallas_call(
        functools.partial(norm_kernel, n),
        out_shape=(
            jax.ShapeDtypeStruct(residual.shape, jnp.bfloat16),
            jax.ShapeDtypeStruct((rows, x_weight_t.shape[0]), jnp.float32),
            jax.ShapeDtypeStruct((rows, z_weight_t.shape[0]), jnp.float32),
            jax.ShapeDtypeStruct((rows, bc_weight.shape[1]), jnp.float32),
            jax.ShapeDtypeStruct((rows, dt_weight_t.shape[0]), jnp.float32),
        ),
        in_specs=[vmem] * 3 + [anywhere] * 4,
        out_specs=(vmem,) * 5,
        scratch_shapes=[
            pltpu.VMEM((n, rows, cols), jnp.bfloat16),
            pltpu.VMEM((n, rows, cols), jnp.bfloat16),
            pltpu.VMEM((rows, cols), jnp.bfloat16),
            pltpu.VMEM((rows, 128), jnp.float32),
            pltpu.VMEM((n, rows, cols), jnp.bfloat16),
            pltpu.VMEM((n, rows, 128), jnp.float32),
        ]
        + [pltpu.VMEM(w.shape, w.dtype) for w in weights]
        + [
            pltpu.SemaphoreType.DMA((4,)),
            pltpu.SemaphoreType.DMA((3, n - 1)),
            pltpu.SemaphoreType.DMA((3, n - 1)),
        ],
        compiler_params=pltpu.CompilerParams(collective_id=2, has_side_effects=True),
    )(projected, residual, norm_gain, *weights)


def mix_kernel(n, width, x_ref, z_ref, bc_ref, ct_ref, step_ref, decay_ref, skip_ref, s_hbm,
               gain_ref, mixed_ref, s_ref, msg, land, load_sem, send_sems, recv_sems):
    me = lax.axis_index("mdl")
    load = pltpu.make_async_copy(s_hbm, s_ref, load_sem.at[0])
    load.start()
    rows, heads = step_ref.shape
    head_dim = x_ref.shape[1] // heads
    state_dim = ct_ref.shape[1] // head_dim
    group = (
        lax.broadcasted_iota(jnp.int32, (ct_ref.shape[1], head_dim), 0) // state_dim
        == lax.broadcasted_iota(jnp.int32, (ct_ref.shape[1], head_dim), 1)
    ).astype(jnp.bfloat16)
    bc = bc_ref[...]
    b_dot_c = jnp.sum(bc[:, :state_dim] * bc[:, state_dim:], axis=1, keepdims=True)
    ct = ct_ref[...]
    x = x_ref[...]
    step = step_ref[...]
    decay = decay_ref[...]
    skip = skip_ref[...]
    load.wait()
    highs, lows = [], []
    for h in range(heads):
        prod = s_ref[h] * ct
        high = prod.astype(jnp.bfloat16)
        highs.append(high)
        lows.append((prod - high.astype(jnp.float32)).astype(jnp.bfloat16))
    stacked = jnp.concatenate(highs + lows, axis=0)
    sums = jnp.dot(stacked, group, preferred_element_type=jnp.float32)
    pieces = []
    for h in range(heads):
        state_c = sums[h * rows : (h + 1) * rows] + sums[(heads + h) * rows : (heads + h + 1) * rows]
        x_h = x[:, h * head_dim : (h + 1) * head_dim]
        pieces.append(
            decay[:, h : h + 1] * state_c
            + (step[:, h : h + 1] * b_dot_c) * x_h
            + skip[:, h : h + 1] * x_h
        )
    y = jnp.concatenate(pieces, axis=1)
    z = z_ref[...]
    gated = y * (z * jax.nn.sigmoid(z))
    msg[...] = jnp.broadcast_to(jnp.sum(gated * gated, axis=1, keepdims=True), msg.shape)
    barrier_all(n, "mdl", me)
    send_all(n, "mdl", me, ((msg, land),), send_sems, recv_sems)
    total = land[0]
    for j in range(1, n):
        total = total + land[j]
    inverse = lax.rsqrt(total[:, 0:1] / width + 1e-05)
    gain = gain_ref[...].astype(jnp.float32).reshape(1, -1)
    mixed_ref[...] = (gated * inverse * gain).astype(mixed_ref.dtype)


def mix_exchange(n, width, x_conv, z_in, bc_conv, c_tiled, step, decay, skip_gain, ssm_state,
                 out_gain):
    rows = x_conv.shape[0]
    vmem = pl.BlockSpec(memory_space=pltpu.VMEM)
    return pl.pallas_call(
        functools.partial(mix_kernel, n, width),
        out_shape=jax.ShapeDtypeStruct(x_conv.shape, jnp.bfloat16),
        in_specs=[vmem] * 7 + [pl.BlockSpec(memory_space=pl.ANY), vmem],
        out_specs=vmem,
        scratch_shapes=[
            pltpu.VMEM(ssm_state.shape[1::-1] + ssm_state.shape[2:], ssm_state.dtype),
            pltpu.VMEM((rows, 128), jnp.float32),
            pltpu.VMEM((n, rows, 128), jnp.float32),
            pltpu.SemaphoreType.DMA((1,)),
            pltpu.SemaphoreType.DMA((1, n - 1)),
            pltpu.SemaphoreType.DMA((1, n - 1)),
        ],
        compiler_params=pltpu.CompilerParams(collective_id=3, has_side_effects=True),
    )(
        x_conv,
        z_in,
        bc_conv,
        c_tiled,
        step,
        decay,
        skip_gain.reshape(1, -1),
        jnp.transpose(ssm_state, (1, 0, 2)),
        out_gain,
    )


def shards(
    n_req,
    n_mdl,
    query,
    new_key,
    new_value,
    page_keys,
    page_values,
    long_keys,
    long_values,
    cache_lengths,
    block_table,
    out_weight,
    residual,
    norm_gain,
    x_weight,
    bc_weight,
    dt_weight,
    z_weight,
    dt_bias,
    a_log,
    skip_gain,
    conv_x_weight,
    conv_bc_weight,
    conv_x_state,
    conv_bc_state,
    ssm_state,
    out_gain,
):
    req_count = query.shape[0]
    local_cols = query.shape[1]
    heads_here = local_cols // HEAD_DIM
    scale = 1.0 / math.sqrt(HEAD_DIM)
    device = lax.axis_index("req")
    pages_here = page_keys.shape[0]
    long_row = jnp.argmax(cache_lengths)
    owner = long_row // req_count
    long_local = long_row % req_count

    assert heads_here == 2
    tokens_here = pages_here * PAGE_SIZE
    attended = attention(
        n_req,
        cache_lengths,
        block_table,
        query,
        new_key,
        new_value,
        page_keys.reshape(tokens_here, local_cols),
        page_values.reshape(tokens_here, local_cols),
        long_keys,
        long_values,
    )

    projected = jnp.dot(attended, out_weight, preferred_element_type=jnp.float32)
    feature_cols = residual.shape[1]
    feature_start = lax.axis_index("mdl") * feature_cols
    hidden, x_in, z_in, bc_in, dt_in = norm_exchange(
        n_mdl, projected, residual, norm_gain, x_weight.T, z_weight.T, bc_weight, dt_weight.T
    )
    taps = conv_x_state.shape[1]
    x_pre = x_in * conv_x_weight[taps].astype(jnp.float32)
    bc_pre = bc_in * conv_bc_weight[taps].astype(jnp.float32)
    for k in range(taps):
        x_pre = x_pre + conv_x_state[:, k, :].astype(jnp.float32) * conv_x_weight[k].astype(jnp.float32)
        bc_pre = bc_pre + conv_bc_state[:, k, :].astype(jnp.float32) * conv_bc_weight[k].astype(
            jnp.float32
        )
    x_conv = jax.nn.silu(x_pre)
    bc_conv = jax.nn.silu(bc_pre)
    b_part = bc_conv[:, :STATE_DIM]
    c_part = bc_conv[:, STATE_DIM:]
    mamba_heads = dt_bias.shape[0]
    step = jax.nn.softplus(dt_in + dt_bias[None, :])
    decay = jnp.exp(-jnp.exp(a_log)[None, :] * step)
    mixed = mix_exchange(
        n_mdl,
        MHEADS * MHEAD_DIM,
        x_conv,
        z_in,
        bc_conv,
        jnp.tile(c_part, (1, MHEAD_DIM)),
        step,
        decay,
        skip_gain,
        ssm_state,
        out_gain,
    )
    return (hidden, mixed)


def solution(mesh):
    return jax.shard_map(
        functools.partial(shards, mesh.shape["req"], mesh.shape["mdl"]),
        mesh=mesh,
        in_specs=(
            P("req", "mdl"),
            P("req", "mdl"),
            P("req", "mdl"),
            P("req", None, "mdl"),
            P("req", None, "mdl"),
            P("req", "mdl"),
            P("req", "mdl"),
            P(),
            P("req", None),
            P("mdl", None),
            P("req", "mdl"),
            P(),
            P(None, "mdl"),
            P(),
            P(None, "mdl"),
            P(None, "mdl"),
            P("mdl"),
            P("mdl"),
            P("mdl"),
            P(None, "mdl"),
            P(),
            P("req", None, "mdl"),
            P("req", None, None),
            P("req", "mdl", None),
            P("mdl"),
        ),
        out_specs=(P("req", "mdl"), P("req", "mdl")),
        check_vma=False,
    )
```

```python
import functools
import math

import jax
import jax.numpy as jnp
from jax import lax
from jax.experimental import pallas as pl
from jax.experimental.pallas import tpu as pltpu
from jax.sharding import PartitionSpec as P

MODEL_WIDTH = 3584
HEAD_DIM = 224
MHEADS = 56
MHEAD_DIM = 64
STATE_DIM = 64
SHORT_MAX = 32
PAGE_SIZE = 16

MESH_ID = pl.DeviceIdType.MESH


def exchange_kernel(n, axis, count, *refs):
    x_refs = refs[:count]
    out_refs = refs[count : 2 * count]
    lands = refs[2 * count : 3 * count]
    send_sems, recv_sems = refs[3 * count :]
    me = lax.axis_index(axis)
    barrier = pltpu.get_barrier_semaphore()
    for j in range(1, n):
        peer = lax.rem(me + j, n)
        pl.semaphore_signal(barrier, inc=1, device_id={axis: peer}, device_id_type=MESH_ID)
    pl.semaphore_wait(barrier, n - 1)
    copies = []
    for k in range(count):
        rows = len(x_refs[k].shape) == 2 and x_refs[k].shape[0] == 1
        slot = lands[k].at[pl.ds(me, 1)] if rows else lands[k].at[me]
        for j in range(1, n):
            peer = lax.rem(me + j, n)
            copy = pltpu.make_async_remote_copy(
                src_ref=x_refs[k],
                dst_ref=slot,
                send_sem=send_sems.at[k, j - 1],
                recv_sem=recv_sems.at[k, j - 1],
                device_id={axis: peer},
                device_id_type=MESH_ID,
            )
            copy.start()
            copies.append(copy)
    for copy in copies:
        copy.wait()
    for k in range(count):
        rows = len(x_refs[k].shape) == 2 and x_refs[k].shape[0] == 1
        if rows:
            lands[k][pl.ds(me, 1), :] = x_refs[k][...]
        else:
            lands[k][me] = x_refs[k][...]
        out_refs[k][...] = lands[k][...]


def exchange(xs, axis, n, cid):
    shapes = []
    for x in xs:
        rows = x.ndim == 2 and x.shape[0] == 1
        shapes.append(jax.ShapeDtypeStruct((n, x.shape[1]) if rows else (n,) + x.shape, x.dtype))
    count = len(xs)
    return pl.pallas_call(
        functools.partial(exchange_kernel, n, axis, count),
        out_shape=tuple(shapes),
        in_specs=[pl.BlockSpec(memory_space=pltpu.VMEM)] * count,
        out_specs=tuple([pl.BlockSpec(memory_space=pltpu.VMEM)] * count),
        scratch_shapes=[pltpu.VMEM(s.shape, s.dtype) for s in shapes]
        + [pltpu.SemaphoreType.DMA((count, n - 1)), pltpu.SemaphoreType.DMA((count, n - 1))],
        compiler_params=pltpu.CompilerParams(collective_id=cid, has_side_effects=True),
    )(*xs)


def by_head(values, head_mask):
    out = jnp.zeros(values.shape[:-1] + (head_mask.shape[1],), values.dtype)
    for h in range(head_mask.shape[0]):
        out = jnp.where(head_mask[h], values[..., h : h + 1], out)
    return out


def pick_head(values, head_mask):
    out = values[..., 0, :]
    for h in range(1, head_mask.shape[0]):
        out = jnp.where(head_mask[h], values[..., h, :], out)
    return out


def attention_kernel(n, scale, cl_ref, lens_ref, bt_ref, q_ref, k_ref, v_ref, pk_hbm, pv_hbm,
                     lk_hbm, lv_hbm, out_ref, pk_ref, pv_ref, lk_ref, lv_ref, qsend, qland, psend,
                     pland, load_sems, send_sems, recv_sems):
    me = lax.axis_index("req")
    rows, cols = q_ref.shape
    tokens = pk_ref.shape[0]
    loads = []
    for i, (src, dst) in enumerate(((pk_hbm, pk_ref), (pv_hbm, pv_ref), (lk_hbm, lk_ref), (lv_hbm, lv_ref))):
        load = pltpu.make_async_copy(src, dst, load_sems.at[i])
        load.start()
        loads.append(load)
    barrier = pltpu.get_barrier_semaphore()
    for j in range(1, n):
        pl.semaphore_signal(barrier, inc=1, device_id={"req": lax.rem(me + j, n)}, device_id_type=MESH_ID)

    cl = cl_ref[...]
    longest = jnp.max(cl, axis=1, keepdims=True)
    where_long = jnp.where(cl == longest, lax.broadcasted_iota(jnp.int32, cl.shape, 1), cl.shape[1])
    long_row = jnp.min(where_long, axis=1, keepdims=True)
    owner = long_row // rows
    long_local = long_row - owner * rows
    lane = lax.broadcasted_iota(jnp.int32, (1, cols), 1)
    hm0 = lane < HEAD_DIM
    row_id = lax.broadcasted_iota(jnp.int32, (rows, 1), 0)
    q = q_ref[...]
    q32 = q.astype(jnp.float32)
    qsend[...] = jnp.sum(jnp.where(row_id == long_local, q32, 0.0), axis=0, keepdims=True)
    pl.semaphore_wait(barrier, n - 1)

    copies = []
    for j in range(1, n):
        copy = pltpu.make_async_remote_copy(
            src_ref=qsend, dst_ref=qland.at[pl.ds(me, 1)], send_sem=send_sems.at[0, j - 1],
            recv_sem=recv_sems.at[0, j - 1], device_id={"req": lax.rem(me + j, n)}, device_id_type=MESH_ID)
        copy.start()
        copies.append(copy)

    zero_q = jnp.zeros_like(q)
    qm = jnp.concatenate([jnp.where(hm0, q, zero_q), jnp.where(hm0, zero_q, q)], axis=0)
    nt = (((1,), (1,)), ((), ()))
    loads[0].wait()
    loads[1].wait()
    s = lax.dot_general(qm, pk_ref[...], nt, preferred_element_type=jnp.float32) * scale
    length = jnp.zeros((rows, 1), jnp.int32)
    page0 = jnp.zeros((rows, 1), jnp.int32)
    page1 = jnp.zeros((rows, 1), jnp.int32)
    for r in range(rows):
        length = jnp.where(row_id == r, lens_ref[me * rows + r], length)
        page0 = jnp.where(row_id == r, bt_ref[0, r] - me * tokens // PAGE_SIZE, page0)
        page1 = jnp.where(row_id == r, bt_ref[1, r] - me * tokens // PAGE_SIZE, page1)
    tok = lax.broadcasted_iota(jnp.int32, (1, tokens), 1)
    tpage = tok // PAGE_SIZE
    tslot = tok % PAGE_SIZE
    usable = ((tpage == page0) & (tslot < length)) | ((tpage == page1) & (tslot + PAGE_SIZE < length))
    usable = usable & (length <= SHORT_MAX)
    usable2 = jnp.concatenate([usable, usable], axis=0)
    s = jnp.where(usable2, s, -jnp.inf)
    prod = q32 * k_ref[...].astype(jnp.float32)
    own0 = jnp.sum(jnp.where(hm0, prod, 0.0), axis=1, keepdims=True)
    own1 = jnp.sum(jnp.where(hm0, 0.0, prod), axis=1, keepdims=True)
    own = jnp.concatenate([own0, own1], axis=0) * scale
    m_s = jnp.maximum(jnp.max(s, axis=1, keepdims=True), own)
    w = jnp.exp(s - m_s)
    ow = jnp.exp(own - m_s)
    tot_s = jnp.sum(w, axis=1, keepdims=True) + ow
    nm = jnp.dot(w.astype(jnp.bfloat16), pv_ref[...], preferred_element_type=jnp.float32)
    owb = ow.astype(jnp.bfloat16).astype(jnp.float32)
    numer = jnp.where(hm0, nm[:rows], nm[rows:]) + jnp.where(
        hm0, owb[:rows], owb[rows:]) * v_ref[...].astype(jnp.float32)

    for copy in copies:
        copy.wait()
    qland[pl.ds(me, 1), :] = qsend[...]
    src_id = lax.broadcasted_iota(jnp.int32, (n, 1), 0)
    lq = jnp.sum(jnp.where(src_id == owner, qland[...], 0.0), axis=0, keepdims=True)
    lq = lq.astype(jnp.bfloat16)
    zero_l = jnp.zeros_like(lq)
    lqm = jnp.concatenate([jnp.where(hm0, lq, zero_l), jnp.where(hm0, zero_l, lq)], axis=0)
    loads[2].wait()
    loads[3].wait()
    ls = jnp.dot(lqm, lk_ref[...], preferred_element_type=jnp.float32) * scale
    m_l = jnp.max(ls, axis=1, keepdims=True)
    lw = jnp.exp(ls - m_l)
    l_l = jnp.sum(lw, axis=1, keepdims=True)
    acc = lax.dot_general(lw.astype(jnp.bfloat16), lv_ref[...], nt, preferred_element_type=jnp.float32)
    acc_row = jnp.where(hm0, acc[0:1], acc[1:2])
    width = psend.shape[1]
    psend[...] = jnp.zeros((1, width), jnp.float32)
    psend[:, 0:cols] = acc_row
    t = lax.broadcasted_iota(jnp.int32, (1, 128), 1)
    tail = jnp.where(t == 0, m_l[0:1], jnp.where(t == 1, m_l[1:2], jnp.where(
        t == 2, l_l[0:1], jnp.where(t == 3, l_l[1:2], 0.0))))
    psend[:, width - 128 : width] = tail

    copies = []
    for j in range(1, n):
        copy = pltpu.make_async_remote_copy(
            src_ref=psend, dst_ref=pland.at[pl.ds(me, 1)], send_sem=send_sems.at[1, j - 1],
            recv_sem=recv_sems.at[1, j - 1], device_id={"req": lax.rem(me + j, n)}, device_id_type=MESH_ID)
        copy.start()
        copies.append(copy)
    for copy in copies:
        copy.wait()
    pland[pl.ds(me, 1), :] = psend[...]

    parts = pland[...]
    base = width - 128
    sums_all = parts[:, 0:cols]
    whole = []
    for h in range(2):
        mh = parts[:, base + h : base + h + 1]
        lh = parts[:, base + 2 + h : base + 3 + h]
        wm = jnp.max(mh, axis=0, keepdims=True)
        keep = jnp.exp(mh - wm)
        wt = jnp.sum(lh * keep, axis=0, keepdims=True)
        ws = jnp.sum(sums_all * keep, axis=0, keepdims=True)
        whole.append((wm, wt, ws))
    whole_sums = jnp.where(hm0, whole[0][2], whole[1][2])
    chosen = (row_id == long_local) & (me == owner)
    kl, kg, tt = [], [], []
    for h in range(2):
        mh = m_s[h * rows : (h + 1) * rows]
        top = jnp.where(chosen, jnp.maximum(mh, whole[h][0]), mh)
        klh = jnp.exp(mh - top)
        kgh = jnp.where(chosen, jnp.exp(whole[h][0] - top), 0.0)
        kl.append(klh)
        kg.append(kgh)
        tt.append(tot_s[h * rows : (h + 1) * rows] * klh + kgh * whole[h][1])
    numer = numer * jnp.where(hm0, kl[0], kl[1]) + jnp.where(hm0, kg[0], kg[1]) * whole_sums
    out_ref[...] = (numer / jnp.where(hm0, tt[0], tt[1])).astype(out_ref.dtype)


def attention(n, cache_lengths, block_table, query, new_key, new_value, page_k, page_v, long_keys,
              long_values):
    scale = 1.0 / math.sqrt(HEAD_DIM)
    cols = query.shape[1]
    width = -(-cols // 128) * 128 + 128
    vmem = pl.BlockSpec(memory_space=pltpu.VMEM)
    smem = pl.BlockSpec(memory_space=pltpu.SMEM)
    anywhere = pl.BlockSpec(memory_space=pl.ANY)
    return pl.pallas_call(
        functools.partial(attention_kernel, n, scale),
        out_shape=jax.ShapeDtypeStruct(query.shape, jnp.bfloat16),
        in_specs=[vmem, smem, smem, vmem, vmem, vmem] + [anywhere] * 4,
        out_specs=vmem,
        scratch_shapes=[
            pltpu.VMEM(page_k.shape, page_k.dtype),
            pltpu.VMEM(page_v.shape, page_v.dtype),
            pltpu.VMEM(long_keys.shape[::-1], long_keys.dtype),
            pltpu.VMEM(long_values.shape[::-1], long_values.dtype),
            pltpu.VMEM((1, cols), jnp.float32),
            pltpu.VMEM((n, cols), jnp.float32),
            pltpu.VMEM((1, width), jnp.float32),
            pltpu.VMEM((n, width), jnp.float32),
            pltpu.SemaphoreType.DMA((4,)),
            pltpu.SemaphoreType.DMA((2, n - 1)),
            pltpu.SemaphoreType.DMA((2, n - 1)),
        ],
        compiler_params=pltpu.CompilerParams(collective_id=0, has_side_effects=True),
    )(
        cache_lengths.reshape(1, -1),
        cache_lengths,
        block_table.T,
        query,
        new_key,
        new_value,
        page_k,
        page_v,
        long_keys.T,
        long_values.T,
    )


def barrier_all(n, axis, me):
    barrier = pltpu.get_barrier_semaphore()
    for j in range(1, n):
        pl.semaphore_signal(barrier, inc=1, device_id={axis: lax.rem(me + j, n)}, device_id_type=MESH_ID)
    pl.semaphore_wait(barrier, n - 1)


def send_all(n, axis, me, pairs, send_sems, recv_sems):
    copies = []
    for k, (src, land) in enumerate(pairs):
        for j in range(1, n):
            copy = pltpu.make_async_remote_copy(
                src_ref=src, dst_ref=land.at[me], send_sem=send_sems.at[k, j - 1],
                recv_sem=recv_sems.at[k, j - 1], device_id={axis: lax.rem(me + j, n)},
                device_id_type=MESH_ID)
            copy.start()
            copies.append(copy)
    for copy in copies:
        copy.wait()
    for src, land in pairs:
        land[me] = src[...]


def norm_kernel(n, a_ref, ow_hbm, r_ref, g_ref, xw_hbm, zw_hbm, bw_hbm, dw_hbm, hidden_ref, x_ref, z_ref,
                bc_ref, dt_ref, blocks, land, hsend, qsend, h_land, q_land, ow, xw, zw, bw, dw,
                load_sems, send_sems, recv_sems):
    me = lax.axis_index("mdl")
    loads = []
    pairs = ((ow_hbm, ow), (xw_hbm, xw), (zw_hbm, zw), (bw_hbm, bw), (dw_hbm, dw))
    for i, (src, dst) in enumerate(pairs):
        load = pltpu.make_async_copy(src, dst, load_sems.at[i])
        load.start()
        loads.append(load)
    cols = r_ref.shape[1]
    barrier = pltpu.get_barrier_semaphore()
    for j in range(1, n):
        pl.semaphore_signal(barrier, inc=1, device_id={"mdl": lax.rem(me + j, n)}, device_id_type=MESH_ID)
    loads[0].wait()
    projected = jnp.dot(a_ref[...], ow[...], preferred_element_type=jnp.float32)
    for j in range(n):
        blocks[j] = projected[:, j * cols : (j + 1) * cols].astype(blocks.dtype)
    pl.semaphore_wait(barrier, n - 1)
    copies = []
    for j in range(1, n):
        peer = lax.rem(me + j, n)
        copy = pltpu.make_async_remote_copy(
            src_ref=blocks.at[peer], dst_ref=land.at[me], send_sem=send_sems.at[0, j - 1],
            recv_sem=recv_sems.at[0, j - 1], device_id={"mdl": peer}, device_id_type=MESH_ID)
        copy.start()
        copies.append(copy)
    for copy in copies:
        copy.wait()
    land[me] = blocks[me]
    summed = r_ref[...].astype(jnp.float32)
    for j in range(n):
        summed = summed + land[j].astype(jnp.float32)
    hidden = summed.astype(jnp.bfloat16)
    hidden_ref[...] = hidden
    hsend[...] = hidden
    hidden_f = hidden.astype(jnp.float32)
    qsend[...] = jnp.broadcast_to(jnp.sum(hidden_f * hidden_f, axis=1, keepdims=True), qsend.shape)
    send_all(n, "mdl", me, ((hsend, h_land), (qsend, q_land)), send_sems.at[1:3], recv_sems.at[1:3])
    hidden_all = jnp.concatenate([h_land[j] for j in range(n)], axis=1).astype(jnp.float32)
    squares = q_land[0]
    for j in range(1, n):
        squares = squares + q_land[j]
    inverse = lax.rsqrt(squares[:, 0:1] / MODEL_WIDTH + 1e-05)
    gain = g_ref[...].astype(jnp.float32).reshape(1, -1)
    normed = (hidden_all * inverse * gain).astype(jnp.bfloat16)
    nt = (((1,), (1,)), ((), ()))
    for load in loads[1:]:
        load.wait()
    x_ref[...] = lax.dot_general(normed, xw[...], nt, preferred_element_type=jnp.float32)
    z_ref[...] = lax.dot_general(normed, zw[...], nt, preferred_element_type=jnp.float32)
    bc_ref[...] = jnp.dot(normed, bw[...], preferred_element_type=jnp.float32)
    dt_ref[...] = lax.dot_general(normed, dw[...], nt, preferred_element_type=jnp.float32)


def norm_exchange(n, attended, out_weight, residual, norm_gain, x_weight_t, z_weight_t, bc_weight, dt_weight_t):
    rows, cols = residual.shape
    vmem = pl.BlockSpec(memory_space=pltpu.VMEM)
    anywhere = pl.BlockSpec(memory_space=pl.ANY)
    weights = (out_weight, x_weight_t, z_weight_t, bc_weight, dt_weight_t)
    return pl.pallas_call(
        functools.partial(norm_kernel, n),
        out_shape=(
            jax.ShapeDtypeStruct(residual.shape, jnp.bfloat16),
            jax.ShapeDtypeStruct((rows, x_weight_t.shape[0]), jnp.float32),
            jax.ShapeDtypeStruct((rows, z_weight_t.shape[0]), jnp.float32),
            jax.ShapeDtypeStruct((rows, bc_weight.shape[1]), jnp.float32),
            jax.ShapeDtypeStruct((rows, dt_weight_t.shape[0]), jnp.float32),
        ),
        in_specs=[vmem, anywhere, vmem, vmem] + [anywhere] * 4,
        out_specs=(vmem,) * 5,
        scratch_shapes=[
            pltpu.VMEM((n, rows, cols), jnp.bfloat16),
            pltpu.VMEM((n, rows, cols), jnp.bfloat16),
            pltpu.VMEM((rows, cols), jnp.bfloat16),
            pltpu.VMEM((rows, 128), jnp.float32),
            pltpu.VMEM((n, rows, cols), jnp.bfloat16),
            pltpu.VMEM((n, rows, 128), jnp.float32),
        ]
        + [pltpu.VMEM(w.shape, w.dtype) for w in weights]
        + [
            pltpu.SemaphoreType.DMA((5,)),
            pltpu.SemaphoreType.DMA((3, n - 1)),
            pltpu.SemaphoreType.DMA((3, n - 1)),
        ],
        compiler_params=pltpu.CompilerParams(collective_id=2, has_side_effects=True),
    )(attended, out_weight, residual, norm_gain, *weights[1:])


def mix_kernel(n, width, x_ref, z_ref, bc_ref, ct_ref, step_ref, decay_ref, skip_ref, s_hbm,
               gain_ref, mixed_ref, s_ref, msg, land, load_sem, send_sems, recv_sems):
    me = lax.axis_index("mdl")
    load = pltpu.make_async_copy(s_hbm, s_ref, load_sem.at[0])
    load.start()
    rows, heads = step_ref.shape
    head_dim = x_ref.shape[1] // heads
    state_dim = ct_ref.shape[1] // head_dim
    group = (
        lax.broadcasted_iota(jnp.int32, (ct_ref.shape[1], head_dim), 0) // state_dim
        == lax.broadcasted_iota(jnp.int32, (ct_ref.shape[1], head_dim), 1)
    ).astype(jnp.bfloat16)
    bc = bc_ref[...]
    b_dot_c = jnp.sum(bc[:, :state_dim] * bc[:, state_dim:], axis=1, keepdims=True)
    ct = ct_ref[...]
    x = x_ref[...]
    step = step_ref[...]
    decay = decay_ref[...]
    skip = skip_ref[...]
    load.wait()
    highs, lows = [], []
    for h in range(heads):
        prod = s_ref[h] * ct
        high = prod.astype(jnp.bfloat16)
        highs.append(high)
        lows.append((prod - high.astype(jnp.float32)).astype(jnp.bfloat16))
    stacked = jnp.concatenate(highs + lows, axis=0)
    sums = jnp.dot(stacked, group, preferred_element_type=jnp.float32)
    pieces = []
    for h in range(heads):
        state_c = sums[h * rows : (h + 1) * rows] + sums[(heads + h) * rows : (heads + h + 1) * rows]
        x_h = x[:, h * head_dim : (h + 1) * head_dim]
        pieces.append(
            decay[:, h : h + 1] * state_c
            + (step[:, h : h + 1] * b_dot_c) * x_h
            + skip[:, h : h + 1] * x_h
        )
    y = jnp.concatenate(pieces, axis=1)
    z = z_ref[...]
    gated = y * (z * jax.nn.sigmoid(z))
    msg[...] = jnp.broadcast_to(jnp.sum(gated * gated, axis=1, keepdims=True), msg.shape)
    barrier_all(n, "mdl", me)
    send_all(n, "mdl", me, ((msg, land),), send_sems, recv_sems)
    total = land[0]
    for j in range(1, n):
        total = total + land[j]
    inverse = lax.rsqrt(total[:, 0:1] / width + 1e-05)
    gain = gain_ref[...].astype(jnp.float32).reshape(1, -1)
    mixed_ref[...] = (gated * inverse * gain).astype(mixed_ref.dtype)


def mix_exchange(n, width, x_conv, z_in, bc_conv, c_tiled, step, decay, skip_gain, ssm_state,
                 out_gain):
    rows = x_conv.shape[0]
    vmem = pl.BlockSpec(memory_space=pltpu.VMEM)
    return pl.pallas_call(
        functools.partial(mix_kernel, n, width),
        out_shape=jax.ShapeDtypeStruct(x_conv.shape, jnp.bfloat16),
        in_specs=[vmem] * 7 + [pl.BlockSpec(memory_space=pl.ANY), vmem],
        out_specs=vmem,
        scratch_shapes=[
            pltpu.VMEM(ssm_state.shape[1::-1] + ssm_state.shape[2:], ssm_state.dtype),
            pltpu.VMEM((rows, 128), jnp.float32),
            pltpu.VMEM((n, rows, 128), jnp.float32),
            pltpu.SemaphoreType.DMA((1,)),
            pltpu.SemaphoreType.DMA((1, n - 1)),
            pltpu.SemaphoreType.DMA((1, n - 1)),
        ],
        compiler_params=pltpu.CompilerParams(collective_id=3, has_side_effects=True),
    )(
        x_conv,
        z_in,
        bc_conv,
        c_tiled,
        step,
        decay,
        skip_gain.reshape(1, -1),
        jnp.transpose(ssm_state, (1, 0, 2)),
        out_gain,
    )


def shards(
    n_req,
    n_mdl,
    query,
    new_key,
    new_value,
    page_keys,
    page_values,
    long_keys,
    long_values,
    cache_lengths,
    block_table,
    out_weight,
    residual,
    norm_gain,
    x_weight,
    bc_weight,
    dt_weight,
    z_weight,
    dt_bias,
    a_log,
    skip_gain,
    conv_x_weight,
    conv_bc_weight,
    conv_x_state,
    conv_bc_state,
    ssm_state,
    out_gain,
):
    req_count = query.shape[0]
    local_cols = query.shape[1]
    heads_here = local_cols // HEAD_DIM
    scale = 1.0 / math.sqrt(HEAD_DIM)
    device = lax.axis_index("req")
    pages_here = page_keys.shape[0]
    long_row = jnp.argmax(cache_lengths)
    owner = long_row // req_count
    long_local = long_row % req_count

    assert heads_here == 2
    tokens_here = pages_here * PAGE_SIZE
    attended = attention(
        n_req,
        cache_lengths,
        block_table,
        query,
        new_key,
        new_value,
        page_keys.reshape(tokens_here, local_cols),
        page_values.reshape(tokens_here, local_cols),
        long_keys,
        long_values,
    )

    feature_cols = residual.shape[1]
    feature_start = lax.axis_index("mdl") * feature_cols
    hidden, x_in, z_in, bc_in, dt_in = norm_exchange(
        n_mdl, attended, out_weight, residual, norm_gain, x_weight.T, z_weight.T, bc_weight, dt_weight.T
    )
    taps = conv_x_state.shape[1]
    x_pre = x_in * conv_x_weight[taps].astype(jnp.float32)
    bc_pre = bc_in * conv_bc_weight[taps].astype(jnp.float32)
    for k in range(taps):
        x_pre = x_pre + conv_x_state[:, k, :].astype(jnp.float32) * conv_x_weight[k].astype(jnp.float32)
        bc_pre = bc_pre + conv_bc_state[:, k, :].astype(jnp.float32) * conv_bc_weight[k].astype(
            jnp.float32
        )
    x_conv = jax.nn.silu(x_pre)
    bc_conv = jax.nn.silu(bc_pre)
    b_part = bc_conv[:, :STATE_DIM]
    c_part = bc_conv[:, STATE_DIM:]
    mamba_heads = dt_bias.shape[0]
    step = jax.nn.softplus(dt_in + dt_bias[None, :])
    decay = jnp.exp(-jnp.exp(a_log)[None, :] * step)
    mixed = mix_exchange(
        n_mdl,
        MHEADS * MHEAD_DIM,
        x_conv,
        z_in,
        bc_conv,
        jnp.tile(c_part, (1, MHEAD_DIM)),
        step,
        decay,
        skip_gain,
        ssm_state,
        out_gain,
    )
    return (hidden, mixed)


def solution(mesh):
    return jax.shard_map(
        functools.partial(shards, mesh.shape["req"], mesh.shape["mdl"]),
        mesh=mesh,
        in_specs=(
            P("req", "mdl"),
            P("req", "mdl"),
            P("req", "mdl"),
            P("req", None, "mdl"),
            P("req", None, "mdl"),
            P("req", "mdl"),
            P("req", "mdl"),
            P(),
            P("req", None),
            P("mdl", None),
            P("req", "mdl"),
            P(),
            P(None, "mdl"),
            P(),
            P(None, "mdl"),
            P(None, "mdl"),
            P("mdl"),
            P("mdl"),
            P("mdl"),
            P(None, "mdl"),
            P(),
            P("req", None, "mdl"),
            P("req", None, None),
            P("req", "mdl", None),
            P("mdl"),
        ),
        out_specs=(P("req", "mdl"), P("req", "mdl")),
        check_vma=False,
    )
```

```python
import functools
import math

import jax
import jax.numpy as jnp
from jax import lax
from jax.experimental import pallas as pl
from jax.experimental.pallas import tpu as pltpu
from jax.sharding import PartitionSpec as P

MODEL_WIDTH = 3584
HEAD_DIM = 224
MHEADS = 56
MHEAD_DIM = 64
STATE_DIM = 64
SHORT_MAX = 32
PAGE_SIZE = 16

MESH_ID = pl.DeviceIdType.MESH


def exchange_kernel(n, axis, count, *refs):
    x_refs = refs[:count]
    out_refs = refs[count : 2 * count]
    lands = refs[2 * count : 3 * count]
    send_sems, recv_sems = refs[3 * count :]
    me = lax.axis_index(axis)
    barrier = pltpu.get_barrier_semaphore()
    for j in range(1, n):
        peer = lax.rem(me + j, n)
        pl.semaphore_signal(barrier, inc=1, device_id={axis: peer}, device_id_type=MESH_ID)
    pl.semaphore_wait(barrier, n - 1)
    copies = []
    for k in range(count):
        rows = len(x_refs[k].shape) == 2 and x_refs[k].shape[0] == 1
        slot = lands[k].at[pl.ds(me, 1)] if rows else lands[k].at[me]
        for j in range(1, n):
            peer = lax.rem(me + j, n)
            copy = pltpu.make_async_remote_copy(
                src_ref=x_refs[k],
                dst_ref=slot,
                send_sem=send_sems.at[k, j - 1],
                recv_sem=recv_sems.at[k, j - 1],
                device_id={axis: peer},
                device_id_type=MESH_ID,
            )
            copy.start()
            copies.append(copy)
    for copy in copies:
        copy.wait()
    for k in range(count):
        rows = len(x_refs[k].shape) == 2 and x_refs[k].shape[0] == 1
        if rows:
            lands[k][pl.ds(me, 1), :] = x_refs[k][...]
        else:
            lands[k][me] = x_refs[k][...]
        out_refs[k][...] = lands[k][...]


def exchange(xs, axis, n, cid):
    shapes = []
    for x in xs:
        rows = x.ndim == 2 and x.shape[0] == 1
        shapes.append(jax.ShapeDtypeStruct((n, x.shape[1]) if rows else (n,) + x.shape, x.dtype))
    count = len(xs)
    return pl.pallas_call(
        functools.partial(exchange_kernel, n, axis, count),
        out_shape=tuple(shapes),
        in_specs=[pl.BlockSpec(memory_space=pltpu.VMEM)] * count,
        out_specs=tuple([pl.BlockSpec(memory_space=pltpu.VMEM)] * count),
        scratch_shapes=[pltpu.VMEM(s.shape, s.dtype) for s in shapes]
        + [pltpu.SemaphoreType.DMA((count, n - 1)), pltpu.SemaphoreType.DMA((count, n - 1))],
        compiler_params=pltpu.CompilerParams(collective_id=cid, has_side_effects=True),
    )(*xs)


def by_head(values, head_mask):
    out = jnp.zeros(values.shape[:-1] + (head_mask.shape[1],), values.dtype)
    for h in range(head_mask.shape[0]):
        out = jnp.where(head_mask[h], values[..., h : h + 1], out)
    return out


def pick_head(values, head_mask):
    out = values[..., 0, :]
    for h in range(1, head_mask.shape[0]):
        out = jnp.where(head_mask[h], values[..., h, :], out)
    return out


def attention_kernel(n, scale, cl_ref, lens_ref, bt_ref, q_ref, k_ref, v_ref, pk_hbm, pv_hbm,
                     lk_hbm, lv_hbm, out_ref, pk_ref, pv_ref, lk_ref, lv_ref, qsend, qland, psend,
                     pland, load_sems, send_sems, recv_sems):
    me = lax.axis_index("req")
    rows, cols = q_ref.shape
    tokens = pk_ref.shape[0]
    loads = []
    for i, (src, dst) in enumerate(((pk_hbm, pk_ref), (pv_hbm, pv_ref), (lk_hbm, lk_ref), (lv_hbm, lv_ref))):
        load = pltpu.make_async_copy(src, dst, load_sems.at[i])
        load.start()
        loads.append(load)
    barrier = pltpu.get_barrier_semaphore()
    for j in range(1, n):
        pl.semaphore_signal(barrier, inc=1, device_id={"req": lax.rem(me + j, n)}, device_id_type=MESH_ID)

    cl = cl_ref[...]
    longest = jnp.max(cl, axis=1, keepdims=True)
    where_long = jnp.where(cl == longest, lax.broadcasted_iota(jnp.int32, cl.shape, 1), cl.shape[1])
    long_row = jnp.min(where_long, axis=1, keepdims=True)
    owner = long_row // rows
    long_local = long_row - owner * rows
    lane = lax.broadcasted_iota(jnp.int32, (1, cols), 1)
    hm0 = lane < HEAD_DIM
    row_id = lax.broadcasted_iota(jnp.int32, (rows, 1), 0)
    q = q_ref[...]
    q32 = q.astype(jnp.float32)
    qsend[...] = jnp.sum(jnp.where(row_id == long_local, q32, 0.0), axis=0, keepdims=True)
    pl.semaphore_wait(barrier, n - 1)

    copies = []
    for j in range(1, n):
        copy = pltpu.make_async_remote_copy(
            src_ref=qsend, dst_ref=qland.at[pl.ds(me, 1)], send_sem=send_sems.at[0, j - 1],
            recv_sem=recv_sems.at[0, j - 1], device_id={"req": lax.rem(me + j, n)}, device_id_type=MESH_ID)
        copy.start()
        copies.append(copy)

    zero_q = jnp.zeros_like(q)
    qm = jnp.concatenate([jnp.where(hm0, q, zero_q), jnp.where(hm0, zero_q, q)], axis=0)
    nt = (((1,), (1,)), ((), ()))
    loads[0].wait()
    loads[1].wait()
    s = lax.dot_general(qm, pk_ref[...], nt, preferred_element_type=jnp.float32) * scale
    length = jnp.zeros((rows, 1), jnp.int32)
    page0 = jnp.zeros((rows, 1), jnp.int32)
    page1 = jnp.zeros((rows, 1), jnp.int32)
    for r in range(rows):
        length = jnp.where(row_id == r, lens_ref[me * rows + r], length)
        page0 = jnp.where(row_id == r, bt_ref[0, r] - me * tokens // PAGE_SIZE, page0)
        page1 = jnp.where(row_id == r, bt_ref[1, r] - me * tokens // PAGE_SIZE, page1)
    tok = lax.broadcasted_iota(jnp.int32, (1, tokens), 1)
    tpage = tok // PAGE_SIZE
    tslot = tok % PAGE_SIZE
    usable = ((tpage == page0) & (tslot < length)) | ((tpage == page1) & (tslot + PAGE_SIZE < length))
    usable = usable & (length <= SHORT_MAX)
    usable2 = jnp.concatenate([usable, usable], axis=0)
    s = jnp.where(usable2, s, -jnp.inf)
    prod = q32 * k_ref[...].astype(jnp.float32)
    own0 = jnp.sum(jnp.where(hm0, prod, 0.0), axis=1, keepdims=True)
    own1 = jnp.sum(jnp.where(hm0, 0.0, prod), axis=1, keepdims=True)
    own = jnp.concatenate([own0, own1], axis=0) * scale
    m_s = jnp.maximum(jnp.max(s, axis=1, keepdims=True), own)
    w = jnp.exp(s - m_s)
    ow = jnp.exp(own - m_s)
    tot_s = jnp.sum(w, axis=1, keepdims=True) + ow
    nm = jnp.dot(w.astype(jnp.bfloat16), pv_ref[...], preferred_element_type=jnp.float32)
    owb = ow.astype(jnp.bfloat16).astype(jnp.float32)
    numer = jnp.where(hm0, nm[:rows], nm[rows:]) + jnp.where(
        hm0, owb[:rows], owb[rows:]) * v_ref[...].astype(jnp.float32)

    for copy in copies:
        copy.wait()
    qland[pl.ds(me, 1), :] = qsend[...]
    src_id = lax.broadcasted_iota(jnp.int32, (n, 1), 0)
    lq = jnp.sum(jnp.where(src_id == owner, qland[...], 0.0), axis=0, keepdims=True)
    lq = lq.astype(jnp.bfloat16)
    zero_l = jnp.zeros_like(lq)
    lqm = jnp.concatenate([jnp.where(hm0, lq, zero_l), jnp.where(hm0, zero_l, lq)], axis=0)
    loads[2].wait()
    loads[3].wait()
    ls = jnp.dot(lqm, lk_ref[...], preferred_element_type=jnp.float32) * scale
    m_l = jnp.max(ls, axis=1, keepdims=True)
    lw = jnp.exp(ls - m_l)
    l_l = jnp.sum(lw, axis=1, keepdims=True)
    acc = lax.dot_general(lw.astype(jnp.bfloat16), lv_ref[...], nt, preferred_element_type=jnp.float32)
    acc_row = jnp.where(hm0, acc[0:1], acc[1:2])
    width = psend.shape[1]
    psend[...] = jnp.zeros((1, width), jnp.float32)
    psend[:, 0:cols] = acc_row
    t = lax.broadcasted_iota(jnp.int32, (1, 128), 1)
    tail = jnp.where(t == 0, m_l[0:1], jnp.where(t == 1, m_l[1:2], jnp.where(
        t == 2, l_l[0:1], jnp.where(t == 3, l_l[1:2], 0.0))))
    psend[:, width - 128 : width] = tail

    copies = []
    for j in range(1, n):
        copy = pltpu.make_async_remote_copy(
            src_ref=psend, dst_ref=pland.at[pl.ds(me, 1)], send_sem=send_sems.at[1, j - 1],
            recv_sem=recv_sems.at[1, j - 1], device_id={"req": lax.rem(me + j, n)}, device_id_type=MESH_ID)
        copy.start()
        copies.append(copy)
    for copy in copies:
        copy.wait()
    pland[pl.ds(me, 1), :] = psend[...]

    parts = pland[...]
    base = width - 128
    sums_all = parts[:, 0:cols]
    whole = []
    for h in range(2):
        mh = parts[:, base + h : base + h + 1]
        lh = parts[:, base + 2 + h : base + 3 + h]
        wm = jnp.max(mh, axis=0, keepdims=True)
        keep = jnp.exp(mh - wm)
        wt = jnp.sum(lh * keep, axis=0, keepdims=True)
        ws = jnp.sum(sums_all * keep, axis=0, keepdims=True)
        whole.append((wm, wt, ws))
    whole_sums = jnp.where(hm0, whole[0][2], whole[1][2])
    chosen = (row_id == long_local) & (me == owner)
    kl, kg, tt = [], [], []
    for h in range(2):
        mh = m_s[h * rows : (h + 1) * rows]
        top = jnp.where(chosen, jnp.maximum(mh, whole[h][0]), mh)
        klh = jnp.exp(mh - top)
        kgh = jnp.where(chosen, jnp.exp(whole[h][0] - top), 0.0)
        kl.append(klh)
        kg.append(kgh)
        tt.append(tot_s[h * rows : (h + 1) * rows] * klh + kgh * whole[h][1])
    numer = numer * jnp.where(hm0, kl[0], kl[1]) + jnp.where(hm0, kg[0], kg[1]) * whole_sums
    out_ref[...] = (numer / jnp.where(hm0, tt[0], tt[1])).astype(out_ref.dtype)


def attention(n, cache_lengths, block_table, query, new_key, new_value, page_k, page_v, long_keys,
              long_values):
    scale = 1.0 / math.sqrt(HEAD_DIM)
    cols = query.shape[1]
    width = -(-cols // 128) * 128 + 128
    vmem = pl.BlockSpec(memory_space=pltpu.VMEM)
    smem = pl.BlockSpec(memory_space=pltpu.SMEM)
    anywhere = pl.BlockSpec(memory_space=pl.ANY)
    return pl.pallas_call(
        functools.partial(attention_kernel, n, scale),
        out_shape=jax.ShapeDtypeStruct(query.shape, jnp.bfloat16),
        in_specs=[vmem, smem, smem, vmem, vmem, vmem] + [anywhere] * 4,
        out_specs=vmem,
        scratch_shapes=[
            pltpu.VMEM(page_k.shape, page_k.dtype),
            pltpu.VMEM(page_v.shape, page_v.dtype),
            pltpu.VMEM(long_keys.shape[::-1], long_keys.dtype),
            pltpu.VMEM(long_values.shape[::-1], long_values.dtype),
            pltpu.VMEM((1, cols), jnp.float32),
            pltpu.VMEM((n, cols), jnp.float32),
            pltpu.VMEM((1, width), jnp.float32),
            pltpu.VMEM((n, width), jnp.float32),
            pltpu.SemaphoreType.DMA((4,)),
            pltpu.SemaphoreType.DMA((2, n - 1)),
            pltpu.SemaphoreType.DMA((2, n - 1)),
        ],
        compiler_params=pltpu.CompilerParams(collective_id=0, has_side_effects=True),
    )(
        cache_lengths.reshape(1, -1),
        cache_lengths,
        block_table.T,
        query,
        new_key,
        new_value,
        page_k,
        page_v,
        long_keys.T,
        long_values.T,
    )


def barrier_all(n, axis, me):
    barrier = pltpu.get_barrier_semaphore()
    for j in range(1, n):
        pl.semaphore_signal(barrier, inc=1, device_id={axis: lax.rem(me + j, n)}, device_id_type=MESH_ID)
    pl.semaphore_wait(barrier, n - 1)


def send_all(n, axis, me, pairs, send_sems, recv_sems):
    copies = []
    for k, (src, land) in enumerate(pairs):
        for j in range(1, n):
            copy = pltpu.make_async_remote_copy(
                src_ref=src, dst_ref=land.at[me], send_sem=send_sems.at[k, j - 1],
                recv_sem=recv_sems.at[k, j - 1], device_id={axis: lax.rem(me + j, n)},
                device_id_type=MESH_ID)
            copy.start()
            copies.append(copy)
    for copy in copies:
        copy.wait()
    for src, land in pairs:
        land[me] = src[...]


def norm_kernel(n, a_ref, ow_hbm, r_ref, g_ref, xw_hbm, zw_hbm, bw_hbm, dw_hbm, cxs_ref, cbs_ref,
                cxw_ref, cbw_ref, hidden_ref, x_ref, z_ref,
                bc_ref, dt_ref, blocks, land, hsend, qsend, h_land, q_land, ow, xw, zw, bw, dw,
                load_sems, send_sems, recv_sems):
    me = lax.axis_index("mdl")
    loads = []
    pairs = ((ow_hbm, ow), (xw_hbm, xw), (zw_hbm, zw), (bw_hbm, bw), (dw_hbm, dw))
    for i, (src, dst) in enumerate(pairs):
        load = pltpu.make_async_copy(src, dst, load_sems.at[i])
        load.start()
        loads.append(load)
    cols = r_ref.shape[1]
    barrier = pltpu.get_barrier_semaphore()
    for j in range(1, n):
        pl.semaphore_signal(barrier, inc=1, device_id={"mdl": lax.rem(me + j, n)}, device_id_type=MESH_ID)
    loads[0].wait()
    projected = jnp.dot(a_ref[...], ow[...], preferred_element_type=jnp.float32)
    for j in range(n):
        blocks[j] = projected[:, j * cols : (j + 1) * cols].astype(blocks.dtype)
    pl.semaphore_wait(barrier, n - 1)
    copies = []
    for j in range(1, n):
        peer = lax.rem(me + j, n)
        copy = pltpu.make_async_remote_copy(
            src_ref=blocks.at[peer], dst_ref=land.at[me], send_sem=send_sems.at[0, j - 1],
            recv_sem=recv_sems.at[0, j - 1], device_id={"mdl": peer}, device_id_type=MESH_ID)
        copy.start()
        copies.append(copy)
    for copy in copies:
        copy.wait()
    land[me] = blocks[me]
    summed = r_ref[...].astype(jnp.float32)
    for j in range(n):
        summed = summed + land[j].astype(jnp.float32)
    hidden = summed.astype(jnp.bfloat16)
    hidden_ref[...] = hidden
    hsend[...] = hidden
    hidden_f = hidden.astype(jnp.float32)
    qsend[...] = jnp.broadcast_to(jnp.sum(hidden_f * hidden_f, axis=1, keepdims=True), qsend.shape)
    send_all(n, "mdl", me, ((hsend, h_land), (qsend, q_land)), send_sems.at[1:3], recv_sems.at[1:3])
    hidden_all = jnp.concatenate([h_land[j] for j in range(n)], axis=1).astype(jnp.float32)
    squares = q_land[0]
    for j in range(1, n):
        squares = squares + q_land[j]
    inverse = lax.rsqrt(squares[:, 0:1] / MODEL_WIDTH + 1e-05)
    gain = g_ref[...].astype(jnp.float32).reshape(1, -1)
    normed = (hidden_all * inverse * gain).astype(jnp.bfloat16)
    nt = (((1,), (1,)), ((), ()))
    for load in loads[1:]:
        load.wait()
    x_in = lax.dot_general(normed, xw[...], nt, preferred_element_type=jnp.float32)
    bc_in = jnp.dot(normed, bw[...], preferred_element_type=jnp.float32)
    taps = cxs_ref.shape[0]
    x_pre = x_in * cxw_ref[taps : taps + 1, :].astype(jnp.float32)
    bc_pre = bc_in * cbw_ref[taps : taps + 1, :].astype(jnp.float32)
    for k in range(taps):
        x_pre = x_pre + cxs_ref[k].astype(jnp.float32) * cxw_ref[k : k + 1, :].astype(jnp.float32)
        bc_pre = bc_pre + cbs_ref[k].astype(jnp.float32) * cbw_ref[k : k + 1, :].astype(jnp.float32)
    x_ref[...] = x_pre * jax.nn.sigmoid(x_pre)
    z_ref[...] = lax.dot_general(normed, zw[...], nt, preferred_element_type=jnp.float32)
    bc_ref[...] = bc_pre * jax.nn.sigmoid(bc_pre)
    dt_ref[...] = lax.dot_general(normed, dw[...], nt, preferred_element_type=jnp.float32)


def norm_exchange(n, attended, out_weight, residual, norm_gain, x_weight_t, z_weight_t, bc_weight, dt_weight_t,
                  conv_states, conv_weights):
    rows, cols = residual.shape
    vmem = pl.BlockSpec(memory_space=pltpu.VMEM)
    anywhere = pl.BlockSpec(memory_space=pl.ANY)
    weights = (out_weight, x_weight_t, z_weight_t, bc_weight, dt_weight_t)
    return pl.pallas_call(
        functools.partial(norm_kernel, n),
        out_shape=(
            jax.ShapeDtypeStruct(residual.shape, jnp.bfloat16),
            jax.ShapeDtypeStruct((rows, x_weight_t.shape[0]), jnp.float32),
            jax.ShapeDtypeStruct((rows, z_weight_t.shape[0]), jnp.float32),
            jax.ShapeDtypeStruct((rows, bc_weight.shape[1]), jnp.float32),
            jax.ShapeDtypeStruct((rows, dt_weight_t.shape[0]), jnp.float32),
        ),
        in_specs=[vmem, anywhere, vmem, vmem] + [anywhere] * 4 + [vmem] * 4,
        out_specs=(vmem,) * 5,
        scratch_shapes=[
            pltpu.VMEM((n, rows, cols), jnp.bfloat16),
            pltpu.VMEM((n, rows, cols), jnp.bfloat16),
            pltpu.VMEM((rows, cols), jnp.bfloat16),
            pltpu.VMEM((rows, 128), jnp.float32),
            pltpu.VMEM((n, rows, cols), jnp.bfloat16),
            pltpu.VMEM((n, rows, 128), jnp.float32),
        ]
        + [pltpu.VMEM(w.shape, w.dtype) for w in weights]
        + [
            pltpu.SemaphoreType.DMA((5,)),
            pltpu.SemaphoreType.DMA((3, n - 1)),
            pltpu.SemaphoreType.DMA((3, n - 1)),
        ],
        compiler_params=pltpu.CompilerParams(collective_id=2, has_side_effects=True),
    )(attended, out_weight, residual, norm_gain, *weights[1:], *conv_states, *conv_weights)


def mix_kernel(n, width, x_ref, z_ref, bc_ref, ct_ref, step_ref, decay_ref, skip_ref, s_hbm,
               gain_ref, mixed_ref, s_ref, msg, land, load_sem, send_sems, recv_sems):
    me = lax.axis_index("mdl")
    load = pltpu.make_async_copy(s_hbm, s_ref, load_sem.at[0])
    load.start()
    rows, heads = step_ref.shape
    head_dim = x_ref.shape[1] // heads
    state_dim = ct_ref.shape[1] // head_dim
    group = (
        lax.broadcasted_iota(jnp.int32, (ct_ref.shape[1], head_dim), 0) // state_dim
        == lax.broadcasted_iota(jnp.int32, (ct_ref.shape[1], head_dim), 1)
    ).astype(jnp.bfloat16)
    bc = bc_ref[...]
    b_dot_c = jnp.sum(bc[:, :state_dim] * bc[:, state_dim:], axis=1, keepdims=True)
    ct = ct_ref[...]
    x = x_ref[...]
    step = step_ref[...]
    decay = decay_ref[...]
    skip = skip_ref[...]
    load.wait()
    highs, lows = [], []
    for h in range(heads):
        prod = s_ref[h] * ct
        high = prod.astype(jnp.bfloat16)
        highs.append(high)
        lows.append((prod - high.astype(jnp.float32)).astype(jnp.bfloat16))
    stacked = jnp.concatenate(highs + lows, axis=0)
    sums = jnp.dot(stacked, group, preferred_element_type=jnp.float32)
    pieces = []
    for h in range(heads):
        state_c = sums[h * rows : (h + 1) * rows] + sums[(heads + h) * rows : (heads + h + 1) * rows]
        x_h = x[:, h * head_dim : (h + 1) * head_dim]
        pieces.append(
            decay[:, h : h + 1] * state_c
            + (step[:, h : h + 1] * b_dot_c) * x_h
            + skip[:, h : h + 1] * x_h
        )
    y = jnp.concatenate(pieces, axis=1)
    z = z_ref[...]
    gated = y * (z * jax.nn.sigmoid(z))
    msg[...] = jnp.broadcast_to(jnp.sum(gated * gated, axis=1, keepdims=True), msg.shape)
    barrier_all(n, "mdl", me)
    send_all(n, "mdl", me, ((msg, land),), send_sems, recv_sems)
    total = land[0]
    for j in range(1, n):
        total = total + land[j]
    inverse = lax.rsqrt(total[:, 0:1] / width + 1e-05)
    gain = gain_ref[...].astype(jnp.float32).reshape(1, -1)
    mixed_ref[...] = (gated * inverse * gain).astype(mixed_ref.dtype)


def mix_exchange(n, width, x_conv, z_in, bc_conv, c_tiled, step, decay, skip_gain, ssm_state,
                 out_gain):
    rows = x_conv.shape[0]
    vmem = pl.BlockSpec(memory_space=pltpu.VMEM)
    return pl.pallas_call(
        functools.partial(mix_kernel, n, width),
        out_shape=jax.ShapeDtypeStruct(x_conv.shape, jnp.bfloat16),
        in_specs=[vmem] * 7 + [pl.BlockSpec(memory_space=pl.ANY), vmem],
        out_specs=vmem,
        scratch_shapes=[
            pltpu.VMEM(ssm_state.shape[1::-1] + ssm_state.shape[2:], ssm_state.dtype),
            pltpu.VMEM((rows, 128), jnp.float32),
            pltpu.VMEM((n, rows, 128), jnp.float32),
            pltpu.SemaphoreType.DMA((1,)),
            pltpu.SemaphoreType.DMA((1, n - 1)),
            pltpu.SemaphoreType.DMA((1, n - 1)),
        ],
        compiler_params=pltpu.CompilerParams(collective_id=3, has_side_effects=True),
    )(
        x_conv,
        z_in,
        bc_conv,
        c_tiled,
        step,
        decay,
        skip_gain.reshape(1, -1),
        jnp.transpose(ssm_state, (1, 0, 2)),
        out_gain,
    )


def shards(
    n_req,
    n_mdl,
    query,
    new_key,
    new_value,
    page_keys,
    page_values,
    long_keys,
    long_values,
    cache_lengths,
    block_table,
    out_weight,
    residual,
    norm_gain,
    x_weight,
    bc_weight,
    dt_weight,
    z_weight,
    dt_bias,
    a_log,
    skip_gain,
    conv_x_weight,
    conv_bc_weight,
    conv_x_state,
    conv_bc_state,
    ssm_state,
    out_gain,
):
    req_count = query.shape[0]
    local_cols = query.shape[1]
    heads_here = local_cols // HEAD_DIM
    scale = 1.0 / math.sqrt(HEAD_DIM)
    device = lax.axis_index("req")
    pages_here = page_keys.shape[0]
    long_row = jnp.argmax(cache_lengths)
    owner = long_row // req_count
    long_local = long_row % req_count

    assert heads_here == 2
    tokens_here = pages_here * PAGE_SIZE
    attended = attention(
        n_req,
        cache_lengths,
        block_table,
        query,
        new_key,
        new_value,
        page_keys.reshape(tokens_here, local_cols),
        page_values.reshape(tokens_here, local_cols),
        long_keys,
        long_values,
    )

    feature_cols = residual.shape[1]
    feature_start = lax.axis_index("mdl") * feature_cols
    hidden, x_in, z_in, bc_in, dt_in = norm_exchange(
        n_mdl,
        attended,
        out_weight,
        residual,
        norm_gain,
        x_weight.T,
        z_weight.T,
        bc_weight,
        dt_weight.T,
        (jnp.transpose(conv_x_state, (1, 0, 2)), jnp.transpose(conv_bc_state, (1, 0, 2))),
        (conv_x_weight, conv_bc_weight),
    )
    x_conv, bc_conv = x_in, bc_in
    b_part = bc_conv[:, :STATE_DIM]
    c_part = bc_conv[:, STATE_DIM:]
    mamba_heads = dt_bias.shape[0]
    step = jax.nn.softplus(dt_in + dt_bias[None, :])
    decay = jnp.exp(-jnp.exp(a_log)[None, :] * step)
    mixed = mix_exchange(
        n_mdl,
        MHEADS * MHEAD_DIM,
        x_conv,
        z_in,
        bc_conv,
        jnp.tile(c_part, (1, MHEAD_DIM)),
        step,
        decay,
        skip_gain,
        ssm_state,
        out_gain,
    )
    return (hidden, mixed)


def solution(mesh):
    return jax.shard_map(
        functools.partial(shards, mesh.shape["req"], mesh.shape["mdl"]),
        mesh=mesh,
        in_specs=(
            P("req", "mdl"),
            P("req", "mdl"),
            P("req", "mdl"),
            P("req", None, "mdl"),
            P("req", None, "mdl"),
            P("req", "mdl"),
            P("req", "mdl"),
            P(),
            P("req", None),
            P("mdl", None),
            P("req", "mdl"),
            P(),
            P(None, "mdl"),
            P(),
            P(None, "mdl"),
            P(None, "mdl"),
            P("mdl"),
            P("mdl"),
            P("mdl"),
            P(None, "mdl"),
            P(),
            P("req", None, "mdl"),
            P("req", None, None),
            P("req", "mdl", None),
            P("mdl"),
        ),
        out_specs=(P("req", "mdl"), P("req", "mdl")),
        check_vma=False,
    )
```

```python
import functools
import math

import jax
import jax.numpy as jnp
from jax import lax
from jax.experimental import pallas as pl
from jax.experimental.pallas import tpu as pltpu
from jax.sharding import PartitionSpec as P

MODEL_WIDTH = 3584
HEAD_DIM = 224
MHEADS = 56
MHEAD_DIM = 64
STATE_DIM = 64
SHORT_MAX = 32
PAGE_SIZE = 16

MESH_ID = pl.DeviceIdType.MESH


def exchange_kernel(n, axis, count, *refs):
    x_refs = refs[:count]
    out_refs = refs[count : 2 * count]
    lands = refs[2 * count : 3 * count]
    send_sems, recv_sems = refs[3 * count :]
    me = lax.axis_index(axis)
    barrier = pltpu.get_barrier_semaphore()
    for j in range(1, n):
        peer = lax.rem(me + j, n)
        pl.semaphore_signal(barrier, inc=1, device_id={axis: peer}, device_id_type=MESH_ID)
    pl.semaphore_wait(barrier, n - 1)
    copies = []
    for k in range(count):
        rows = len(x_refs[k].shape) == 2 and x_refs[k].shape[0] == 1
        slot = lands[k].at[pl.ds(me, 1)] if rows else lands[k].at[me]
        for j in range(1, n):
            peer = lax.rem(me + j, n)
            copy = pltpu.make_async_remote_copy(
                src_ref=x_refs[k],
                dst_ref=slot,
                send_sem=send_sems.at[k, j - 1],
                recv_sem=recv_sems.at[k, j - 1],
                device_id={axis: peer},
                device_id_type=MESH_ID,
            )
            copy.start()
            copies.append(copy)
    for copy in copies:
        copy.wait()
    for k in range(count):
        rows = len(x_refs[k].shape) == 2 and x_refs[k].shape[0] == 1
        if rows:
            lands[k][pl.ds(me, 1), :] = x_refs[k][...]
        else:
            lands[k][me] = x_refs[k][...]
        out_refs[k][...] = lands[k][...]


def exchange(xs, axis, n, cid):
    shapes = []
    for x in xs:
        rows = x.ndim == 2 and x.shape[0] == 1
        shapes.append(jax.ShapeDtypeStruct((n, x.shape[1]) if rows else (n,) + x.shape, x.dtype))
    count = len(xs)
    return pl.pallas_call(
        functools.partial(exchange_kernel, n, axis, count),
        out_shape=tuple(shapes),
        in_specs=[pl.BlockSpec(memory_space=pltpu.VMEM)] * count,
        out_specs=tuple([pl.BlockSpec(memory_space=pltpu.VMEM)] * count),
        scratch_shapes=[pltpu.VMEM(s.shape, s.dtype) for s in shapes]
        + [pltpu.SemaphoreType.DMA((count, n - 1)), pltpu.SemaphoreType.DMA((count, n - 1))],
        compiler_params=pltpu.CompilerParams(collective_id=cid, has_side_effects=True),
    )(*xs)


def by_head(values, head_mask):
    out = jnp.zeros(values.shape[:-1] + (head_mask.shape[1],), values.dtype)
    for h in range(head_mask.shape[0]):
        out = jnp.where(head_mask[h], values[..., h : h + 1], out)
    return out


def pick_head(values, head_mask):
    out = values[..., 0, :]
    for h in range(1, head_mask.shape[0]):
        out = jnp.where(head_mask[h], values[..., h, :], out)
    return out


def attention_kernel(n, scale, cl_ref, lens_ref, bt_ref, q_ref, k_ref, v_ref, pk_hbm, pv_hbm,
                     lk_hbm, lv_hbm, out_ref, pk_ref, pv_ref, lk_ref, lv_ref, qsend, qland, psend,
                     pland, load_sems, send_sems, recv_sems):
    me = lax.axis_index("req")
    rows, cols = q_ref.shape
    tokens = pk_ref.shape[0]
    loads = []
    for i, (src, dst) in enumerate(((pk_hbm, pk_ref), (pv_hbm, pv_ref), (lk_hbm, lk_ref), (lv_hbm, lv_ref))):
        load = pltpu.make_async_copy(src, dst, load_sems.at[i])
        load.start()
        loads.append(load)
    barrier = pltpu.get_barrier_semaphore()
    for j in range(1, n):
        pl.semaphore_signal(barrier, inc=1, device_id={"req": lax.rem(me + j, n)}, device_id_type=MESH_ID)

    cl = cl_ref[...]
    longest = jnp.max(cl, axis=1, keepdims=True)
    where_long = jnp.where(cl == longest, lax.broadcasted_iota(jnp.int32, cl.shape, 1), cl.shape[1])
    long_row = jnp.min(where_long, axis=1, keepdims=True)
    owner = long_row // rows
    long_local = long_row - owner * rows
    lane = lax.broadcasted_iota(jnp.int32, (1, cols), 1)
    hm0 = lane < HEAD_DIM
    row_id = lax.broadcasted_iota(jnp.int32, (rows, 1), 0)
    q = q_ref[...]
    q32 = q.astype(jnp.float32)
    qsend[...] = jnp.sum(jnp.where(row_id == long_local, q32, 0.0), axis=0, keepdims=True)
    pl.semaphore_wait(barrier, n - 1)

    copies = []
    for j in range(1, n):
        copy = pltpu.make_async_remote_copy(
            src_ref=qsend, dst_ref=qland.at[pl.ds(me, 1)], send_sem=send_sems.at[0, j - 1],
            recv_sem=recv_sems.at[0, j - 1], device_id={"req": lax.rem(me + j, n)}, device_id_type=MESH_ID)
        copy.start()
        copies.append(copy)

    zero_q = jnp.zeros_like(q)
    qm = jnp.concatenate([jnp.where(hm0, q, zero_q), jnp.where(hm0, zero_q, q)], axis=0)
    nt = (((1,), (1,)), ((), ()))
    loads[0].wait()
    loads[1].wait()
    s = lax.dot_general(qm, pk_ref[...], nt, preferred_element_type=jnp.float32) * scale
    length = jnp.zeros((rows, 1), jnp.int32)
    page0 = jnp.zeros((rows, 1), jnp.int32)
    page1 = jnp.zeros((rows, 1), jnp.int32)
    for r in range(rows):
        length = jnp.where(row_id == r, lens_ref[me * rows + r], length)
        page0 = jnp.where(row_id == r, bt_ref[0, r] - me * tokens // PAGE_SIZE, page0)
        page1 = jnp.where(row_id == r, bt_ref[1, r] - me * tokens // PAGE_SIZE, page1)
    tok = lax.broadcasted_iota(jnp.int32, (1, tokens), 1)
    tpage = tok // PAGE_SIZE
    tslot = tok % PAGE_SIZE
    usable = ((tpage == page0) & (tslot < length)) | ((tpage == page1) & (tslot + PAGE_SIZE < length))
    usable = usable & (length <= SHORT_MAX)
    usable2 = jnp.concatenate([usable, usable], axis=0)
    s = jnp.where(usable2, s, -jnp.inf)
    prod = q32 * k_ref[...].astype(jnp.float32)
    own0 = jnp.sum(jnp.where(hm0, prod, 0.0), axis=1, keepdims=True)
    own1 = jnp.sum(jnp.where(hm0, 0.0, prod), axis=1, keepdims=True)
    own = jnp.concatenate([own0, own1], axis=0) * scale
    m_s = jnp.maximum(jnp.max(s, axis=1, keepdims=True), own)
    w = jnp.exp(s - m_s)
    ow = jnp.exp(own - m_s)
    tot_s = jnp.sum(w, axis=1, keepdims=True) + ow
    nm = jnp.dot(w.astype(jnp.bfloat16), pv_ref[...], preferred_element_type=jnp.float32)
    owb = ow.astype(jnp.bfloat16).astype(jnp.float32)
    numer = jnp.where(hm0, nm[:rows], nm[rows:]) + jnp.where(
        hm0, owb[:rows], owb[rows:]) * v_ref[...].astype(jnp.float32)

    for copy in copies:
        copy.wait()
    qland[pl.ds(me, 1), :] = qsend[...]
    src_id = lax.broadcasted_iota(jnp.int32, (n, 1), 0)
    lq = jnp.sum(jnp.where(src_id == owner, qland[...], 0.0), axis=0, keepdims=True)
    lq = lq.astype(jnp.bfloat16)
    zero_l = jnp.zeros_like(lq)
    lqm = jnp.concatenate([jnp.where(hm0, lq, zero_l), jnp.where(hm0, zero_l, lq)], axis=0)
    loads[2].wait()
    loads[3].wait()
    ls = jnp.dot(lqm, lk_ref[...], preferred_element_type=jnp.float32) * scale
    m_l = jnp.max(ls, axis=1, keepdims=True)
    lw = jnp.exp(ls - m_l)
    l_l = jnp.sum(lw, axis=1, keepdims=True)
    acc = lax.dot_general(lw.astype(jnp.bfloat16), lv_ref[...], nt, preferred_element_type=jnp.float32)
    acc_row = jnp.where(hm0, acc[0:1], acc[1:2])
    width = psend.shape[1]
    psend[...] = jnp.zeros((1, width), jnp.float32)
    psend[:, 0:cols] = acc_row
    t = lax.broadcasted_iota(jnp.int32, (1, 128), 1)
    tail = jnp.where(t == 0, m_l[0:1], jnp.where(t == 1, m_l[1:2], jnp.where(
        t == 2, l_l[0:1], jnp.where(t == 3, l_l[1:2], 0.0))))
    psend[:, width - 128 : width] = tail

    copies = []
    for j in range(1, n):
        copy = pltpu.make_async_remote_copy(
            src_ref=psend, dst_ref=pland.at[pl.ds(me, 1)], send_sem=send_sems.at[1, j - 1],
            recv_sem=recv_sems.at[1, j - 1], device_id={"req": lax.rem(me + j, n)}, device_id_type=MESH_ID)
        copy.start()
        copies.append(copy)
    for copy in copies:
        copy.wait()
    pland[pl.ds(me, 1), :] = psend[...]

    parts = pland[...]
    base = width - 128
    sums_all = parts[:, 0:cols]
    whole = []
    for h in range(2):
        mh = parts[:, base + h : base + h + 1]
        lh = parts[:, base + 2 + h : base + 3 + h]
        wm = jnp.max(mh, axis=0, keepdims=True)
        keep = jnp.exp(mh - wm)
        wt = jnp.sum(lh * keep, axis=0, keepdims=True)
        ws = jnp.sum(sums_all * keep, axis=0, keepdims=True)
        whole.append((wm, wt, ws))
    whole_sums = jnp.where(hm0, whole[0][2], whole[1][2])
    chosen = (row_id == long_local) & (me == owner)
    kl, kg, tt = [], [], []
    for h in range(2):
        mh = m_s[h * rows : (h + 1) * rows]
        top = jnp.where(chosen, jnp.maximum(mh, whole[h][0]), mh)
        klh = jnp.exp(mh - top)
        kgh = jnp.where(chosen, jnp.exp(whole[h][0] - top), 0.0)
        kl.append(klh)
        kg.append(kgh)
        tt.append(tot_s[h * rows : (h + 1) * rows] * klh + kgh * whole[h][1])
    numer = numer * jnp.where(hm0, kl[0], kl[1]) + jnp.where(hm0, kg[0], kg[1]) * whole_sums
    out_ref[...] = (numer / jnp.where(hm0, tt[0], tt[1])).astype(out_ref.dtype)


def attention(n, cache_lengths, block_table, query, new_key, new_value, page_k, page_v, long_keys,
              long_values):
    scale = 1.0 / math.sqrt(HEAD_DIM)
    cols = query.shape[1]
    width = -(-cols // 128) * 128 + 128
    vmem = pl.BlockSpec(memory_space=pltpu.VMEM)
    smem = pl.BlockSpec(memory_space=pltpu.SMEM)
    anywhere = pl.BlockSpec(memory_space=pl.ANY)
    return pl.pallas_call(
        functools.partial(attention_kernel, n, scale),
        out_shape=jax.ShapeDtypeStruct(query.shape, jnp.bfloat16),
        in_specs=[vmem, smem, smem, vmem, vmem, vmem] + [anywhere] * 4,
        out_specs=vmem,
        scratch_shapes=[
            pltpu.VMEM(page_k.shape, page_k.dtype),
            pltpu.VMEM(page_v.shape, page_v.dtype),
            pltpu.VMEM(long_keys.shape[::-1], long_keys.dtype),
            pltpu.VMEM(long_values.shape[::-1], long_values.dtype),
            pltpu.VMEM((1, cols), jnp.float32),
            pltpu.VMEM((n, cols), jnp.float32),
            pltpu.VMEM((1, width), jnp.float32),
            pltpu.VMEM((n, width), jnp.float32),
            pltpu.SemaphoreType.DMA((4,)),
            pltpu.SemaphoreType.DMA((2, n - 1)),
            pltpu.SemaphoreType.DMA((2, n - 1)),
        ],
        compiler_params=pltpu.CompilerParams(collective_id=0, has_side_effects=True),
    )(
        cache_lengths.reshape(1, -1),
        cache_lengths,
        block_table.T,
        query,
        new_key,
        new_value,
        page_k,
        page_v,
        long_keys.T,
        long_values.T,
    )


def barrier_all(n, axis, me):
    barrier = pltpu.get_barrier_semaphore()
    for j in range(1, n):
        pl.semaphore_signal(barrier, inc=1, device_id={axis: lax.rem(me + j, n)}, device_id_type=MESH_ID)
    pl.semaphore_wait(barrier, n - 1)


def send_all(n, axis, me, pairs, send_sems, recv_sems):
    copies = []
    for k, (src, land) in enumerate(pairs):
        for j in range(1, n):
            copy = pltpu.make_async_remote_copy(
                src_ref=src, dst_ref=land.at[me], send_sem=send_sems.at[k, j - 1],
                recv_sem=recv_sems.at[k, j - 1], device_id={axis: lax.rem(me + j, n)},
                device_id_type=MESH_ID)
            copy.start()
            copies.append(copy)
    for copy in copies:
        copy.wait()
    for src, land in pairs:
        land[me] = src[...]


def norm_kernel(n, a_ref, ow_hbm, r_ref, g_ref, xw_hbm, zw_hbm, bw_hbm, dw_hbm, cxs_ref, cbs_ref,
                cxw_ref, cbw_ref, dtb_ref, al_ref, hidden_ref, x_ref, z_ref,
                bc_ref, dt_ref, decay_ref, blocks, land, hsend, qsend, h_land, q_land, ow, xw, zw, bw, dw,
                load_sems, send_sems, recv_sems):
    me = lax.axis_index("mdl")
    loads = []
    pairs = ((ow_hbm, ow), (xw_hbm, xw), (zw_hbm, zw), (bw_hbm, bw), (dw_hbm, dw))
    for i, (src, dst) in enumerate(pairs):
        load = pltpu.make_async_copy(src, dst, load_sems.at[i])
        load.start()
        loads.append(load)
    cols = r_ref.shape[1]
    barrier = pltpu.get_barrier_semaphore()
    for j in range(1, n):
        pl.semaphore_signal(barrier, inc=1, device_id={"mdl": lax.rem(me + j, n)}, device_id_type=MESH_ID)
    loads[0].wait()
    projected = jnp.dot(a_ref[...], ow[...], preferred_element_type=jnp.float32)
    for j in range(n):
        blocks[j] = projected[:, j * cols : (j + 1) * cols].astype(blocks.dtype)
    pl.semaphore_wait(barrier, n - 1)
    copies = []
    for j in range(1, n):
        peer = lax.rem(me + j, n)
        copy = pltpu.make_async_remote_copy(
            src_ref=blocks.at[peer], dst_ref=land.at[me], send_sem=send_sems.at[0, j - 1],
            recv_sem=recv_sems.at[0, j - 1], device_id={"mdl": peer}, device_id_type=MESH_ID)
        copy.start()
        copies.append(copy)
    for copy in copies:
        copy.wait()
    land[me] = blocks[me]
    summed = r_ref[...].astype(jnp.float32)
    for j in range(n):
        summed = summed + land[j].astype(jnp.float32)
    hidden = summed.astype(jnp.bfloat16)
    hidden_ref[...] = hidden
    hsend[...] = hidden
    hidden_f = hidden.astype(jnp.float32)
    qsend[...] = jnp.broadcast_to(jnp.sum(hidden_f * hidden_f, axis=1, keepdims=True), qsend.shape)
    send_all(n, "mdl", me, ((hsend, h_land), (qsend, q_land)), send_sems.at[1:3], recv_sems.at[1:3])
    hidden_all = jnp.concatenate([h_land[j] for j in range(n)], axis=1).astype(jnp.float32)
    squares = q_land[0]
    for j in range(1, n):
        squares = squares + q_land[j]
    inverse = lax.rsqrt(squares[:, 0:1] / MODEL_WIDTH + 1e-05)
    gain = g_ref[...].astype(jnp.float32).reshape(1, -1)
    normed = (hidden_all * inverse * gain).astype(jnp.bfloat16)
    nt = (((1,), (1,)), ((), ()))
    for load in loads[1:]:
        load.wait()
    x_in = lax.dot_general(normed, xw[...], nt, preferred_element_type=jnp.float32)
    bc_in = jnp.dot(normed, bw[...], preferred_element_type=jnp.float32)
    taps = cxs_ref.shape[0]
    x_pre = x_in * cxw_ref[taps : taps + 1, :].astype(jnp.float32)
    bc_pre = bc_in * cbw_ref[taps : taps + 1, :].astype(jnp.float32)
    for k in range(taps):
        x_pre = x_pre + cxs_ref[k].astype(jnp.float32) * cxw_ref[k : k + 1, :].astype(jnp.float32)
        bc_pre = bc_pre + cbs_ref[k].astype(jnp.float32) * cbw_ref[k : k + 1, :].astype(jnp.float32)
    x_ref[...] = x_pre * jax.nn.sigmoid(x_pre)
    z_ref[...] = lax.dot_general(normed, zw[...], nt, preferred_element_type=jnp.float32)
    bc_ref[...] = bc_pre * jax.nn.sigmoid(bc_pre)
    dt_pre = lax.dot_general(normed, dw[...], nt, preferred_element_type=jnp.float32)
    dt_pre = dt_pre + dtb_ref[...].reshape(1, -1)
    step = jnp.maximum(dt_pre, 0.0) + jnp.log1p(jnp.exp(-jnp.abs(dt_pre)))
    dt_ref[...] = step
    decay_ref[...] = jnp.exp(-jnp.exp(al_ref[...].reshape(1, -1)) * step)


def norm_exchange(n, attended, out_weight, residual, norm_gain, x_weight_t, z_weight_t, bc_weight, dt_weight_t,
                  conv_states, conv_weights, dt_bias, a_log):
    rows, cols = residual.shape
    vmem = pl.BlockSpec(memory_space=pltpu.VMEM)
    anywhere = pl.BlockSpec(memory_space=pl.ANY)
    weights = (out_weight, x_weight_t, z_weight_t, bc_weight, dt_weight_t)
    return pl.pallas_call(
        functools.partial(norm_kernel, n),
        out_shape=(
            jax.ShapeDtypeStruct(residual.shape, jnp.bfloat16),
            jax.ShapeDtypeStruct((rows, x_weight_t.shape[0]), jnp.float32),
            jax.ShapeDtypeStruct((rows, z_weight_t.shape[0]), jnp.float32),
            jax.ShapeDtypeStruct((rows, bc_weight.shape[1]), jnp.float32),
            jax.ShapeDtypeStruct((rows, dt_weight_t.shape[0]), jnp.float32),
            jax.ShapeDtypeStruct((rows, dt_weight_t.shape[0]), jnp.float32),
        ),
        in_specs=[vmem, anywhere, vmem, vmem] + [anywhere] * 4 + [vmem] * 6,
        out_specs=(vmem,) * 6,
        scratch_shapes=[
            pltpu.VMEM((n, rows, cols), jnp.bfloat16),
            pltpu.VMEM((n, rows, cols), jnp.bfloat16),
            pltpu.VMEM((rows, cols), jnp.bfloat16),
            pltpu.VMEM((rows, 128), jnp.float32),
            pltpu.VMEM((n, rows, cols), jnp.bfloat16),
            pltpu.VMEM((n, rows, 128), jnp.float32),
        ]
        + [pltpu.VMEM(w.shape, w.dtype) for w in weights]
        + [
            pltpu.SemaphoreType.DMA((5,)),
            pltpu.SemaphoreType.DMA((3, n - 1)),
            pltpu.SemaphoreType.DMA((3, n - 1)),
        ],
        compiler_params=pltpu.CompilerParams(collective_id=2, has_side_effects=True),
    )(attended, out_weight, residual, norm_gain, *weights[1:], *conv_states, *conv_weights, dt_bias, a_log)


def mix_kernel(n, width, x_ref, z_ref, bc_ref, ct_ref, step_ref, decay_ref, skip_ref, s_hbm,
               gain_ref, mixed_ref, s_ref, msg, land, load_sem, send_sems, recv_sems):
    me = lax.axis_index("mdl")
    load = pltpu.make_async_copy(s_hbm, s_ref, load_sem.at[0])
    load.start()
    rows, heads = step_ref.shape
    head_dim = x_ref.shape[1] // heads
    state_dim = ct_ref.shape[1] // head_dim
    group = (
        lax.broadcasted_iota(jnp.int32, (ct_ref.shape[1], head_dim), 0) // state_dim
        == lax.broadcasted_iota(jnp.int32, (ct_ref.shape[1], head_dim), 1)
    ).astype(jnp.bfloat16)
    bc = bc_ref[...]
    b_dot_c = jnp.sum(bc[:, :state_dim] * bc[:, state_dim:], axis=1, keepdims=True)
    ct = ct_ref[...]
    x = x_ref[...]
    step = step_ref[...]
    decay = decay_ref[...]
    skip = skip_ref[...]
    load.wait()
    highs, lows = [], []
    for h in range(heads):
        prod = s_ref[h] * ct
        high = prod.astype(jnp.bfloat16)
        highs.append(high)
        lows.append((prod - high.astype(jnp.float32)).astype(jnp.bfloat16))
    stacked = jnp.concatenate(highs + lows, axis=0)
    sums = jnp.dot(stacked, group, preferred_element_type=jnp.float32)
    pieces = []
    for h in range(heads):
        state_c = sums[h * rows : (h + 1) * rows] + sums[(heads + h) * rows : (heads + h + 1) * rows]
        x_h = x[:, h * head_dim : (h + 1) * head_dim]
        pieces.append(
            decay[:, h : h + 1] * state_c
            + (step[:, h : h + 1] * b_dot_c) * x_h
            + skip[:, h : h + 1] * x_h
        )
    y = jnp.concatenate(pieces, axis=1)
    z = z_ref[...]
    gated = y * (z * jax.nn.sigmoid(z))
    msg[...] = jnp.broadcast_to(jnp.sum(gated * gated, axis=1, keepdims=True), msg.shape)
    barrier_all(n, "mdl", me)
    send_all(n, "mdl", me, ((msg, land),), send_sems, recv_sems)
    total = land[0]
    for j in range(1, n):
        total = total + land[j]
    inverse = lax.rsqrt(total[:, 0:1] / width + 1e-05)
    gain = gain_ref[...].astype(jnp.float32).reshape(1, -1)
    mixed_ref[...] = (gated * inverse * gain).astype(mixed_ref.dtype)


def mix_exchange(n, width, x_conv, z_in, bc_conv, c_tiled, step, decay, skip_gain, ssm_state,
                 out_gain):
    rows = x_conv.shape[0]
    vmem = pl.BlockSpec(memory_space=pltpu.VMEM)
    return pl.pallas_call(
        functools.partial(mix_kernel, n, width),
        out_shape=jax.ShapeDtypeStruct(x_conv.shape, jnp.bfloat16),
        in_specs=[vmem] * 7 + [pl.BlockSpec(memory_space=pl.ANY), vmem],
        out_specs=vmem,
        scratch_shapes=[
            pltpu.VMEM(ssm_state.shape[1::-1] + ssm_state.shape[2:], ssm_state.dtype),
            pltpu.VMEM((rows, 128), jnp.float32),
            pltpu.VMEM((n, rows, 128), jnp.float32),
            pltpu.SemaphoreType.DMA((1,)),
            pltpu.SemaphoreType.DMA((1, n - 1)),
            pltpu.SemaphoreType.DMA((1, n - 1)),
        ],
        compiler_params=pltpu.CompilerParams(collective_id=3, has_side_effects=True),
    )(
        x_conv,
        z_in,
        bc_conv,
        c_tiled,
        step,
        decay,
        skip_gain.reshape(1, -1),
        jnp.transpose(ssm_state, (1, 0, 2)),
        out_gain,
    )


def shards(
    n_req,
    n_mdl,
    query,
    new_key,
    new_value,
    page_keys,
    page_values,
    long_keys,
    long_values,
    cache_lengths,
    block_table,
    out_weight,
    residual,
    norm_gain,
    x_weight,
    bc_weight,
    dt_weight,
    z_weight,
    dt_bias,
    a_log,
    skip_gain,
    conv_x_weight,
    conv_bc_weight,
    conv_x_state,
    conv_bc_state,
    ssm_state,
    out_gain,
):
    req_count = query.shape[0]
    local_cols = query.shape[1]
    heads_here = local_cols // HEAD_DIM
    scale = 1.0 / math.sqrt(HEAD_DIM)
    device = lax.axis_index("req")
    pages_here = page_keys.shape[0]
    long_row = jnp.argmax(cache_lengths)
    owner = long_row // req_count
    long_local = long_row % req_count

    assert heads_here == 2
    tokens_here = pages_here * PAGE_SIZE
    attended = attention(
        n_req,
        cache_lengths,
        block_table,
        query,
        new_key,
        new_value,
        page_keys.reshape(tokens_here, local_cols),
        page_values.reshape(tokens_here, local_cols),
        long_keys,
        long_values,
    )

    feature_cols = residual.shape[1]
    feature_start = lax.axis_index("mdl") * feature_cols
    hidden, x_in, z_in, bc_in, step, decay = norm_exchange(
        n_mdl,
        attended,
        out_weight,
        residual,
        norm_gain,
        x_weight.T,
        z_weight.T,
        bc_weight,
        dt_weight.T,
        (jnp.transpose(conv_x_state, (1, 0, 2)), jnp.transpose(conv_bc_state, (1, 0, 2))),
        (conv_x_weight, conv_bc_weight),
        dt_bias,
        a_log,
    )
    x_conv, bc_conv = x_in, bc_in
    b_part = bc_conv[:, :STATE_DIM]
    c_part = bc_conv[:, STATE_DIM:]
    mamba_heads = dt_bias.shape[0]
    mixed = mix_exchange(
        n_mdl,
        MHEADS * MHEAD_DIM,
        x_conv,
        z_in,
        bc_conv,
        jnp.tile(c_part, (1, MHEAD_DIM)),
        step,
        decay,
        skip_gain,
        ssm_state,
        out_gain,
    )
    return (hidden, mixed)


def solution(mesh):
    return jax.shard_map(
        functools.partial(shards, mesh.shape["req"], mesh.shape["mdl"]),
        mesh=mesh,
        in_specs=(
            P("req", "mdl"),
            P("req", "mdl"),
            P("req", "mdl"),
            P("req", None, "mdl"),
            P("req", None, "mdl"),
            P("req", "mdl"),
            P("req", "mdl"),
            P(),
            P("req", None),
            P("mdl", None),
            P("req", "mdl"),
            P(),
            P(None, "mdl"),
            P(),
            P(None, "mdl"),
            P(None, "mdl"),
            P("mdl"),
            P("mdl"),
            P("mdl"),
            P(None, "mdl"),
            P(),
            P("req", None, "mdl"),
            P("req", None, None),
            P("req", "mdl", None),
            P("mdl"),
        ),
        out_specs=(P("req", "mdl"), P("req", "mdl")),
        check_vma=False,
    )
```

```python
import functools
import math

import jax
import jax.numpy as jnp
from jax import lax
from jax.experimental import pallas as pl
from jax.experimental.pallas import tpu as pltpu
from jax.sharding import PartitionSpec as P

MODEL_WIDTH = 3584
HEAD_DIM = 224
MHEADS = 56
MHEAD_DIM = 64
STATE_DIM = 64
SHORT_MAX = 32
PAGE_SIZE = 16

MESH_ID = pl.DeviceIdType.MESH


def exchange_kernel(n, axis, count, *refs):
    x_refs = refs[:count]
    out_refs = refs[count : 2 * count]
    lands = refs[2 * count : 3 * count]
    send_sems, recv_sems = refs[3 * count :]
    me = lax.axis_index(axis)
    barrier = pltpu.get_barrier_semaphore()
    for j in range(1, n):
        peer = lax.rem(me + j, n)
        pl.semaphore_signal(barrier, inc=1, device_id={axis: peer}, device_id_type=MESH_ID)
    pl.semaphore_wait(barrier, n - 1)
    copies = []
    for k in range(count):
        rows = len(x_refs[k].shape) == 2 and x_refs[k].shape[0] == 1
        slot = lands[k].at[pl.ds(me, 1)] if rows else lands[k].at[me]
        for j in range(1, n):
            peer = lax.rem(me + j, n)
            copy = pltpu.make_async_remote_copy(
                src_ref=x_refs[k],
                dst_ref=slot,
                send_sem=send_sems.at[k, j - 1],
                recv_sem=recv_sems.at[k, j - 1],
                device_id={axis: peer},
                device_id_type=MESH_ID,
            )
            copy.start()
            copies.append(copy)
    for copy in copies:
        copy.wait()
    for k in range(count):
        rows = len(x_refs[k].shape) == 2 and x_refs[k].shape[0] == 1
        if rows:
            lands[k][pl.ds(me, 1), :] = x_refs[k][...]
        else:
            lands[k][me] = x_refs[k][...]
        out_refs[k][...] = lands[k][...]


def exchange(xs, axis, n, cid):
    shapes = []
    for x in xs:
        rows = x.ndim == 2 and x.shape[0] == 1
        shapes.append(jax.ShapeDtypeStruct((n, x.shape[1]) if rows else (n,) + x.shape, x.dtype))
    count = len(xs)
    return pl.pallas_call(
        functools.partial(exchange_kernel, n, axis, count),
        out_shape=tuple(shapes),
        in_specs=[pl.BlockSpec(memory_space=pltpu.VMEM)] * count,
        out_specs=tuple([pl.BlockSpec(memory_space=pltpu.VMEM)] * count),
        scratch_shapes=[pltpu.VMEM(s.shape, s.dtype) for s in shapes]
        + [pltpu.SemaphoreType.DMA((count, n - 1)), pltpu.SemaphoreType.DMA((count, n - 1))],
        compiler_params=pltpu.CompilerParams(collective_id=cid, has_side_effects=True),
    )(*xs)


def by_head(values, head_mask):
    out = jnp.zeros(values.shape[:-1] + (head_mask.shape[1],), values.dtype)
    for h in range(head_mask.shape[0]):
        out = jnp.where(head_mask[h], values[..., h : h + 1], out)
    return out


def pick_head(values, head_mask):
    out = values[..., 0, :]
    for h in range(1, head_mask.shape[0]):
        out = jnp.where(head_mask[h], values[..., h, :], out)
    return out


def attention_kernel(n, scale, cl_ref, lens_ref, bt_ref, q_ref, k_ref, v_ref, pk_hbm, pv_hbm,
                     lk_hbm, lv_hbm, out_ref, pk_ref, pv_ref, lk_ref, lv_ref, qsend, qland, psend,
                     pland, load_sems, send_sems, recv_sems):
    me = lax.axis_index("req")
    rows, cols = q_ref.shape
    tokens = pk_ref.shape[0]
    loads = []
    for i, (src, dst) in enumerate(((pk_hbm, pk_ref), (pv_hbm, pv_ref), (lk_hbm, lk_ref), (lv_hbm, lv_ref))):
        load = pltpu.make_async_copy(src, dst, load_sems.at[i])
        load.start()
        loads.append(load)
    barrier = pltpu.get_barrier_semaphore()
    for j in range(1, n):
        pl.semaphore_signal(barrier, inc=1, device_id={"req": lax.rem(me + j, n)}, device_id_type=MESH_ID)

    cl = cl_ref[...]
    longest = jnp.max(cl, axis=1, keepdims=True)
    where_long = jnp.where(cl == longest, lax.broadcasted_iota(jnp.int32, cl.shape, 1), cl.shape[1])
    long_row = jnp.min(where_long, axis=1, keepdims=True)
    owner = long_row // rows
    long_local = long_row - owner * rows
    lane = lax.broadcasted_iota(jnp.int32, (1, cols), 1)
    hm0 = lane < HEAD_DIM
    row_id = lax.broadcasted_iota(jnp.int32, (rows, 1), 0)
    q = q_ref[...]
    q32 = q.astype(jnp.float32)
    qsend[...] = jnp.sum(jnp.where(row_id == long_local, q32, 0.0), axis=0, keepdims=True)
    pl.semaphore_wait(barrier, n - 1)

    copies = []
    for j in range(1, n):
        copy = pltpu.make_async_remote_copy(
            src_ref=qsend, dst_ref=qland.at[pl.ds(me, 1)], send_sem=send_sems.at[0, j - 1],
            recv_sem=recv_sems.at[0, j - 1], device_id={"req": lax.rem(me + j, n)}, device_id_type=MESH_ID)
        copy.start()
        copies.append(copy)

    zero_q = jnp.zeros_like(q)
    qm = jnp.concatenate([jnp.where(hm0, q, zero_q), jnp.where(hm0, zero_q, q)], axis=0)
    nt = (((1,), (1,)), ((), ()))
    loads[0].wait()
    loads[1].wait()
    s = lax.dot_general(qm, pk_ref[...], nt, preferred_element_type=jnp.float32) * scale
    length = jnp.zeros((rows, 1), jnp.int32)
    page0 = jnp.zeros((rows, 1), jnp.int32)
    page1 = jnp.zeros((rows, 1), jnp.int32)
    for r in range(rows):
        length = jnp.where(row_id == r, lens_ref[me * rows + r], length)
        page0 = jnp.where(row_id == r, bt_ref[0, r] - me * tokens // PAGE_SIZE, page0)
        page1 = jnp.where(row_id == r, bt_ref[1, r] - me * tokens // PAGE_SIZE, page1)
    tok = lax.broadcasted_iota(jnp.int32, (1, tokens), 1)
    tpage = tok // PAGE_SIZE
    tslot = tok % PAGE_SIZE
    usable = ((tpage == page0) & (tslot < length)) | ((tpage == page1) & (tslot + PAGE_SIZE < length))
    usable = usable & (length <= SHORT_MAX)
    usable2 = jnp.concatenate([usable, usable], axis=0)
    s = jnp.where(usable2, s, -jnp.inf)
    prod = q32 * k_ref[...].astype(jnp.float32)
    own0 = jnp.sum(jnp.where(hm0, prod, 0.0), axis=1, keepdims=True)
    own1 = jnp.sum(jnp.where(hm0, 0.0, prod), axis=1, keepdims=True)
    own = jnp.concatenate([own0, own1], axis=0) * scale
    m_s = jnp.maximum(jnp.max(s, axis=1, keepdims=True), own)
    w = jnp.exp(s - m_s)
    ow = jnp.exp(own - m_s)
    tot_s = jnp.sum(w, axis=1, keepdims=True) + ow
    nm = jnp.dot(w.astype(jnp.bfloat16), pv_ref[...], preferred_element_type=jnp.float32)
    owb = ow.astype(jnp.bfloat16).astype(jnp.float32)
    numer = jnp.where(hm0, nm[:rows], nm[rows:]) + jnp.where(
        hm0, owb[:rows], owb[rows:]) * v_ref[...].astype(jnp.float32)

    for copy in copies:
        copy.wait()
    qland[pl.ds(me, 1), :] = qsend[...]
    src_id = lax.broadcasted_iota(jnp.int32, (n, 1), 0)
    lq = jnp.sum(jnp.where(src_id == owner, qland[...], 0.0), axis=0, keepdims=True)
    lq = lq.astype(jnp.bfloat16)
    zero_l = jnp.zeros_like(lq)
    lqm = jnp.concatenate([jnp.where(hm0, lq, zero_l), jnp.where(hm0, zero_l, lq)], axis=0)
    loads[2].wait()
    loads[3].wait()
    ls = jnp.dot(lqm, lk_ref[...], preferred_element_type=jnp.float32) * scale
    m_l = jnp.max(ls, axis=1, keepdims=True)
    lw = jnp.exp(ls - m_l)
    l_l = jnp.sum(lw, axis=1, keepdims=True)
    acc = lax.dot_general(lw.astype(jnp.bfloat16), lv_ref[...], nt, preferred_element_type=jnp.float32)
    acc_row = jnp.where(hm0, acc[0:1], acc[1:2])
    width = psend.shape[1]
    psend[...] = jnp.zeros((1, width), jnp.float32)
    psend[:, 0:cols] = acc_row
    t = lax.broadcasted_iota(jnp.int32, (1, 128), 1)
    tail = jnp.where(t == 0, m_l[0:1], jnp.where(t == 1, m_l[1:2], jnp.where(
        t == 2, l_l[0:1], jnp.where(t == 3, l_l[1:2], 0.0))))
    psend[:, width - 128 : width] = tail

    copies = []
    for j in range(1, n):
        copy = pltpu.make_async_remote_copy(
            src_ref=psend, dst_ref=pland.at[pl.ds(me, 1)], send_sem=send_sems.at[1, j - 1],
            recv_sem=recv_sems.at[1, j - 1], device_id={"req": lax.rem(me + j, n)}, device_id_type=MESH_ID)
        copy.start()
        copies.append(copy)
    for copy in copies:
        copy.wait()
    pland[pl.ds(me, 1), :] = psend[...]

    parts = pland[...]
    base = width - 128
    sums_all = parts[:, 0:cols]
    whole = []
    for h in range(2):
        mh = parts[:, base + h : base + h + 1]
        lh = parts[:, base + 2 + h : base + 3 + h]
        wm = jnp.max(mh, axis=0, keepdims=True)
        keep = jnp.exp(mh - wm)
        wt = jnp.sum(lh * keep, axis=0, keepdims=True)
        ws = jnp.sum(sums_all * keep, axis=0, keepdims=True)
        whole.append((wm, wt, ws))
    whole_sums = jnp.where(hm0, whole[0][2], whole[1][2])
    chosen = (row_id == long_local) & (me == owner)
    kl, kg, tt = [], [], []
    for h in range(2):
        mh = m_s[h * rows : (h + 1) * rows]
        top = jnp.where(chosen, jnp.maximum(mh, whole[h][0]), mh)
        klh = jnp.exp(mh - top)
        kgh = jnp.where(chosen, jnp.exp(whole[h][0] - top), 0.0)
        kl.append(klh)
        kg.append(kgh)
        tt.append(tot_s[h * rows : (h + 1) * rows] * klh + kgh * whole[h][1])
    numer = numer * jnp.where(hm0, kl[0], kl[1]) + jnp.where(hm0, kg[0], kg[1]) * whole_sums
    out_ref[...] = (numer / jnp.where(hm0, tt[0], tt[1])).astype(out_ref.dtype)


def attention(n, cache_lengths, block_table, query, new_key, new_value, page_k, page_v, long_keys,
              long_values):
    scale = 1.0 / math.sqrt(HEAD_DIM)
    cols = query.shape[1]
    width = -(-cols // 128) * 128 + 128
    vmem = pl.BlockSpec(memory_space=pltpu.VMEM)
    smem = pl.BlockSpec(memory_space=pltpu.SMEM)
    anywhere = pl.BlockSpec(memory_space=pl.ANY)
    return pl.pallas_call(
        functools.partial(attention_kernel, n, scale),
        out_shape=jax.ShapeDtypeStruct(query.shape, jnp.bfloat16),
        in_specs=[vmem, smem, smem, vmem, vmem, vmem] + [anywhere] * 4,
        out_specs=vmem,
        scratch_shapes=[
            pltpu.VMEM(page_k.shape, page_k.dtype),
            pltpu.VMEM(page_v.shape, page_v.dtype),
            pltpu.VMEM(long_keys.shape[::-1], long_keys.dtype),
            pltpu.VMEM(long_values.shape[::-1], long_values.dtype),
            pltpu.VMEM((1, cols), jnp.float32),
            pltpu.VMEM((n, cols), jnp.float32),
            pltpu.VMEM((1, width), jnp.float32),
            pltpu.VMEM((n, width), jnp.float32),
            pltpu.SemaphoreType.DMA((4,)),
            pltpu.SemaphoreType.DMA((2, n - 1)),
            pltpu.SemaphoreType.DMA((2, n - 1)),
        ],
        compiler_params=pltpu.CompilerParams(collective_id=0, has_side_effects=True),
    )(
        cache_lengths.reshape(1, -1),
        cache_lengths,
        block_table.T,
        query,
        new_key,
        new_value,
        page_k,
        page_v,
        long_keys.T,
        long_values.T,
    )


def barrier_all(n, axis, me):
    barrier = pltpu.get_barrier_semaphore()
    for j in range(1, n):
        pl.semaphore_signal(barrier, inc=1, device_id={axis: lax.rem(me + j, n)}, device_id_type=MESH_ID)
    pl.semaphore_wait(barrier, n - 1)


def send_all(n, axis, me, pairs, send_sems, recv_sems):
    copies = []
    for k, (src, land) in enumerate(pairs):
        for j in range(1, n):
            copy = pltpu.make_async_remote_copy(
                src_ref=src, dst_ref=land.at[me], send_sem=send_sems.at[k, j - 1],
                recv_sem=recv_sems.at[k, j - 1], device_id={axis: lax.rem(me + j, n)},
                device_id_type=MESH_ID)
            copy.start()
            copies.append(copy)
    for copy in copies:
        copy.wait()
    for src, land in pairs:
        land[me] = src[...]


def norm_kernel(n, a_ref, ow_hbm, r_ref, g_ref, xw_hbm, zw_hbm, bw_hbm, dw_hbm, cxs_ref, cbs_ref,
                cxw_ref, cbw_ref, dtb_ref, al_ref, hidden_ref, x_ref, z_ref,
                bc_ref, dt_ref, decay_ref, blocks, land, hsend, qsend, h_land, q_land, ow, xw, zw, bw, dw,
                load_sems, send_sems, recv_sems):
    me = lax.axis_index("mdl")
    loads = []
    pairs = ((ow_hbm, ow), (xw_hbm, xw), (zw_hbm, zw), (bw_hbm, bw), (dw_hbm, dw))
    for i, (src, dst) in enumerate(pairs):
        load = pltpu.make_async_copy(src, dst, load_sems.at[i])
        load.start()
        loads.append(load)
    cols = r_ref.shape[1]
    barrier = pltpu.get_barrier_semaphore()
    for j in range(1, n):
        pl.semaphore_signal(barrier, inc=1, device_id={"mdl": lax.rem(me + j, n)}, device_id_type=MESH_ID)
    loads[0].wait()
    projected = jnp.dot(a_ref[...], ow[...], preferred_element_type=jnp.float32)
    for j in range(n):
        blocks[j] = projected[:, j * cols : (j + 1) * cols].astype(blocks.dtype)
    pl.semaphore_wait(barrier, n - 1)
    copies = []
    for j in range(1, n):
        peer = lax.rem(me + j, n)
        copy = pltpu.make_async_remote_copy(
            src_ref=blocks.at[peer], dst_ref=land.at[me], send_sem=send_sems.at[0, j - 1],
            recv_sem=recv_sems.at[0, j - 1], device_id={"mdl": peer}, device_id_type=MESH_ID)
        copy.start()
        copies.append(copy)
    for copy in copies:
        copy.wait()
    land[me] = blocks[me]
    summed = r_ref[...].astype(jnp.float32)
    for j in range(n):
        summed = summed + land[j].astype(jnp.float32)
    hidden = summed.astype(jnp.bfloat16)
    hidden_ref[...] = hidden
    hsend[...] = hidden
    hidden_f = hidden.astype(jnp.float32)
    qsend[...] = jnp.broadcast_to(jnp.sum(hidden_f * hidden_f, axis=1, keepdims=True), qsend.shape)
    send_all(n, "mdl", me, ((hsend, h_land), (qsend, q_land)), send_sems.at[1:3], recv_sems.at[1:3])
    hidden_all = jnp.concatenate([h_land[j] for j in range(n)], axis=1).astype(jnp.float32)
    squares = q_land[0]
    for j in range(1, n):
        squares = squares + q_land[j]
    inverse = lax.rsqrt(squares[:, 0:1] / MODEL_WIDTH + 1e-05)
    gain = g_ref[...].astype(jnp.float32).reshape(1, -1)
    normed = (hidden_all * inverse * gain).astype(jnp.bfloat16)
    nt = (((1,), (1,)), ((), ()))
    for load in loads[1:]:
        load.wait()
    x_in = lax.dot_general(normed, xw[...], nt, preferred_element_type=jnp.float32)
    bc_in = jnp.dot(normed, bw[...], preferred_element_type=jnp.float32)
    taps = cxs_ref.shape[0]
    x_pre = x_in * cxw_ref[taps : taps + 1, :].astype(jnp.float32)
    bc_pre = bc_in * cbw_ref[taps : taps + 1, :].astype(jnp.float32)
    for k in range(taps):
        x_pre = x_pre + cxs_ref[k].astype(jnp.float32) * cxw_ref[k : k + 1, :].astype(jnp.float32)
        bc_pre = bc_pre + cbs_ref[k].astype(jnp.float32) * cbw_ref[k : k + 1, :].astype(jnp.float32)
    x_ref[...] = x_pre * jax.nn.sigmoid(x_pre)
    z_ref[...] = lax.dot_general(normed, zw[...], nt, preferred_element_type=jnp.float32)
    bc_ref[...] = bc_pre * jax.nn.sigmoid(bc_pre)
    dt_pre = lax.dot_general(normed, dw[...], nt, preferred_element_type=jnp.float32)
    dt_pre = dt_pre + dtb_ref[...].reshape(1, -1)
    step = jnp.maximum(dt_pre, 0.0) + jnp.log1p(jnp.exp(-jnp.abs(dt_pre)))
    dt_ref[...] = step
    decay_ref[...] = jnp.exp(-jnp.exp(al_ref[...].reshape(1, -1)) * step)


def norm_exchange(n, attended, out_weight, residual, norm_gain, x_weight_t, z_weight_t, bc_weight, dt_weight_t,
                  conv_states, conv_weights, dt_bias, a_log):
    rows, cols = residual.shape
    vmem = pl.BlockSpec(memory_space=pltpu.VMEM)
    anywhere = pl.BlockSpec(memory_space=pl.ANY)
    weights = (out_weight, x_weight_t, z_weight_t, bc_weight, dt_weight_t)
    return pl.pallas_call(
        functools.partial(norm_kernel, n),
        out_shape=(
            jax.ShapeDtypeStruct(residual.shape, jnp.bfloat16),
            jax.ShapeDtypeStruct((rows, x_weight_t.shape[0]), jnp.float32),
            jax.ShapeDtypeStruct((rows, z_weight_t.shape[0]), jnp.float32),
            jax.ShapeDtypeStruct((rows, bc_weight.shape[1]), jnp.float32),
            jax.ShapeDtypeStruct((rows, dt_weight_t.shape[0]), jnp.float32),
            jax.ShapeDtypeStruct((rows, dt_weight_t.shape[0]), jnp.float32),
        ),
        in_specs=[vmem, anywhere, vmem, vmem] + [anywhere] * 4 + [vmem] * 6,
        out_specs=(vmem,) * 6,
        scratch_shapes=[
            pltpu.VMEM((n, rows, cols), jnp.bfloat16),
            pltpu.VMEM((n, rows, cols), jnp.bfloat16),
            pltpu.VMEM((rows, cols), jnp.bfloat16),
            pltpu.VMEM((rows, 128), jnp.float32),
            pltpu.VMEM((n, rows, cols), jnp.bfloat16),
            pltpu.VMEM((n, rows, 128), jnp.float32),
        ]
        + [pltpu.VMEM(w.shape, w.dtype) for w in weights]
        + [
            pltpu.SemaphoreType.DMA((5,)),
            pltpu.SemaphoreType.DMA((3, n - 1)),
            pltpu.SemaphoreType.DMA((3, n - 1)),
        ],
        compiler_params=pltpu.CompilerParams(collective_id=2, has_side_effects=True),
    )(attended, out_weight, residual, norm_gain, *weights[1:], *conv_states, *conv_weights, dt_bias, a_log)


def mix_kernel(n, width, x_ref, z_ref, bc_ref, step_ref, decay_ref, skip_ref, s_hbm,
               gain_ref, mixed_ref, s_ref, msg, land, load_sem, send_sems, recv_sems):
    me = lax.axis_index("mdl")
    load = pltpu.make_async_copy(s_hbm, s_ref, load_sem.at[0])
    load.start()
    rows, heads = step_ref.shape
    head_dim = x_ref.shape[1] // heads
    state_dim = bc_ref.shape[1] // 2
    span = head_dim * state_dim
    group = (
        lax.broadcasted_iota(jnp.int32, (span, head_dim), 0) // state_dim
        == lax.broadcasted_iota(jnp.int32, (span, head_dim), 1)
    ).astype(jnp.bfloat16)
    bc = bc_ref[...]
    b_dot_c = jnp.sum(bc[:, :state_dim] * bc[:, state_dim:], axis=1, keepdims=True)
    pair = jnp.concatenate([bc[:, state_dim:], bc[:, state_dim:]], axis=1)
    ct = jnp.concatenate([pair] * (span // pair.shape[1]), axis=1)
    x = x_ref[...]
    step = step_ref[...]
    decay = decay_ref[...]
    skip = skip_ref[...]
    load.wait()
    highs, lows = [], []
    for h in range(heads):
        prod = s_ref[h] * ct
        high = prod.astype(jnp.bfloat16)
        highs.append(high)
        lows.append((prod - high.astype(jnp.float32)).astype(jnp.bfloat16))
    stacked = jnp.concatenate(highs + lows, axis=0)
    sums = jnp.dot(stacked, group, preferred_element_type=jnp.float32)
    pieces = []
    for h in range(heads):
        state_c = sums[h * rows : (h + 1) * rows] + sums[(heads + h) * rows : (heads + h + 1) * rows]
        x_h = x[:, h * head_dim : (h + 1) * head_dim]
        pieces.append(
            decay[:, h : h + 1] * state_c
            + (step[:, h : h + 1] * b_dot_c) * x_h
            + skip[:, h : h + 1] * x_h
        )
    y = jnp.concatenate(pieces, axis=1)
    z = z_ref[...]
    gated = y * (z * jax.nn.sigmoid(z))
    msg[...] = jnp.broadcast_to(jnp.sum(gated * gated, axis=1, keepdims=True), msg.shape)
    barrier_all(n, "mdl", me)
    send_all(n, "mdl", me, ((msg, land),), send_sems, recv_sems)
    total = land[0]
    for j in range(1, n):
        total = total + land[j]
    inverse = lax.rsqrt(total[:, 0:1] / width + 1e-05)
    gain = gain_ref[...].astype(jnp.float32).reshape(1, -1)
    mixed_ref[...] = (gated * inverse * gain).astype(mixed_ref.dtype)


def mix_exchange(n, width, x_conv, z_in, bc_conv, step, decay, skip_gain, ssm_state,
                 out_gain):
    rows = x_conv.shape[0]
    vmem = pl.BlockSpec(memory_space=pltpu.VMEM)
    return pl.pallas_call(
        functools.partial(mix_kernel, n, width),
        out_shape=jax.ShapeDtypeStruct(x_conv.shape, jnp.bfloat16),
        in_specs=[vmem] * 6 + [pl.BlockSpec(memory_space=pl.ANY), vmem],
        out_specs=vmem,
        scratch_shapes=[
            pltpu.VMEM(ssm_state.shape[1::-1] + ssm_state.shape[2:], ssm_state.dtype),
            pltpu.VMEM((rows, 128), jnp.float32),
            pltpu.VMEM((n, rows, 128), jnp.float32),
            pltpu.SemaphoreType.DMA((1,)),
            pltpu.SemaphoreType.DMA((1, n - 1)),
            pltpu.SemaphoreType.DMA((1, n - 1)),
        ],
        compiler_params=pltpu.CompilerParams(collective_id=3, has_side_effects=True),
    )(
        x_conv,
        z_in,
        bc_conv,
        step,
        decay,
        skip_gain.reshape(1, -1),
        jnp.transpose(ssm_state, (1, 0, 2)),
        out_gain,
    )


def shards(
    n_req,
    n_mdl,
    query,
    new_key,
    new_value,
    page_keys,
    page_values,
    long_keys,
    long_values,
    cache_lengths,
    block_table,
    out_weight,
    residual,
    norm_gain,
    x_weight,
    bc_weight,
    dt_weight,
    z_weight,
    dt_bias,
    a_log,
    skip_gain,
    conv_x_weight,
    conv_bc_weight,
    conv_x_state,
    conv_bc_state,
    ssm_state,
    out_gain,
):
    req_count = query.shape[0]
    local_cols = query.shape[1]
    heads_here = local_cols // HEAD_DIM
    scale = 1.0 / math.sqrt(HEAD_DIM)
    device = lax.axis_index("req")
    pages_here = page_keys.shape[0]
    long_row = jnp.argmax(cache_lengths)
    owner = long_row // req_count
    long_local = long_row % req_count

    assert heads_here == 2
    tokens_here = pages_here * PAGE_SIZE
    attended = attention(
        n_req,
        cache_lengths,
        block_table,
        query,
        new_key,
        new_value,
        page_keys.reshape(tokens_here, local_cols),
        page_values.reshape(tokens_here, local_cols),
        long_keys,
        long_values,
    )

    feature_cols = residual.shape[1]
    feature_start = lax.axis_index("mdl") * feature_cols
    hidden, x_in, z_in, bc_in, step, decay = norm_exchange(
        n_mdl,
        attended,
        out_weight,
        residual,
        norm_gain,
        x_weight.T,
        z_weight.T,
        bc_weight,
        dt_weight.T,
        (jnp.transpose(conv_x_state, (1, 0, 2)), jnp.transpose(conv_bc_state, (1, 0, 2))),
        (conv_x_weight, conv_bc_weight),
        dt_bias,
        a_log,
    )
    x_conv, bc_conv = x_in, bc_in
    b_part = bc_conv[:, :STATE_DIM]
    c_part = bc_conv[:, STATE_DIM:]
    mamba_heads = dt_bias.shape[0]
    mixed = mix_exchange(
        n_mdl,
        MHEADS * MHEAD_DIM,
        x_conv,
        z_in,
        bc_conv,
        step,
        decay,
        skip_gain,
        ssm_state,
        out_gain,
    )
    return (hidden, mixed)


def solution(mesh):
    return jax.shard_map(
        functools.partial(shards, mesh.shape["req"], mesh.shape["mdl"]),
        mesh=mesh,
        in_specs=(
            P("req", "mdl"),
            P("req", "mdl"),
            P("req", "mdl"),
            P("req", None, "mdl"),
            P("req", None, "mdl"),
            P("req", "mdl"),
            P("req", "mdl"),
            P(),
            P("req", None),
            P("mdl", None),
            P("req", "mdl"),
            P(),
            P(None, "mdl"),
            P(),
            P(None, "mdl"),
            P(None, "mdl"),
            P("mdl"),
            P("mdl"),
            P("mdl"),
            P(None, "mdl"),
            P(),
            P("req", None, "mdl"),
            P("req", None, None),
            P("req", "mdl", None),
            P("mdl"),
        ),
        out_specs=(P("req", "mdl"), P("req", "mdl")),
        check_vma=False,
    )
```
